128 devices in a mesh: wide: 16 (over x, y), narrow: 8 (over z, core).
Axes of the slice: x: 4, y: 4, z: 4, core: 2. Of those that a mesh axis runs over, the one named last changes fastest.
Arguments:
- tokens: bfloat16 [16384, 4608], P('wide', 'narrow'), may hold values from -6 to 6
- segment_ids: int32 [16384], P('wide'), may hold values from 0 to 7, never falling along the last dimension, each value on 1 to 8192 neighbouring positions
- page_table: int32 [128], P('wide'), may hold values from 0 to 127, as said below
- pre_gain: bfloat16 [4608], P('narrow'), may hold values from 0.099609375 to 1.8984375
- post_gain: bfloat16 [4608], P('narrow'), may hold values from 0.25 to 1.75
- w_query: bfloat16 [4608, 4096], P('wide', 'narrow'), may hold values from -0.25 to 0.25
- w_key: bfloat16 [4608, 2048], P('wide', 'narrow'), may hold values from -0.09375 to 0.09375
- w_value: bfloat16 [4608, 2048], P('wide', 'narrow'), may hold values from -0.09375 to 0.09375
- w_out: bfloat16 [4096, 4608], P('narrow', 'wide'), may hold values from -0.09375 to 0.09375
Outputs:
- mixed: bfloat16 [16384, 4608], P('wide', 'narrow')
- kv_pages: bfloat16 [128, 16, 128, 256], P('wide', 'narrow')
The draws below stay inside these ranges and needn't reach their ends.
Inputs may be any that keep to these rules, and one draw needn't show every extreme that they name: page_table is a permutation; kv_pages places pages i * 8 to (i + 1) * 8 - 1 on wide index i; the 8 blocks of tokens held by one wide index go to pages placed on 8 different wide indices. `segment_ids`: segment ids never fall along the tokens; every prompt has at least one token and the longest has exactly 8192.
All inputs are finite; a program needn't handle non-finite values.
Results may differ from the reference program's by a relative error of at most 0.014.
Values may be sent and summed in bfloat16 or wider, within the bound.
A program may use at most 192 MiB of HBM per device.

```python
import math
import jax
import jax.numpy as jnp
import numpy as np
from jax import lax

D = 4608
HQ = 32
KVH = 16
HD = 128
WINDOW = 4096
TOK_W = 1024
SEGS = 8
BLK_DEV = 8
PAGE = 128
SHARDS = 16
TOKENS = 16384
NPAGES = 128
N_WIDE = 16
N_NARROW = 8


def draw_page_table(key, part):
    base_key = jax.random.fold_in(key, 11)
    key_offsets, key_sources, key_owners, key_slots = jax.random.split(base_key, 4)
    offsets = jax.random.permutation(key_offsets, SHARDS)[:BLK_DEV]
    relabel_source = jax.random.permutation(key_sources, SHARDS)
    relabel_owner = jax.random.permutation(key_owners, SHARDS)
    source_ids = jnp.arange(SHARDS, dtype=jnp.int32)[:, None]
    owners = relabel_owner[(relabel_source[source_ids] + offsets[None, :]) % SHARDS]
    slot_keys = jax.random.split(key_slots, SHARDS)
    slot_orders = jax.vmap(lambda slot_key: jax.random.permutation(slot_key, BLK_DEV))(slot_keys)
    columns = jnp.broadcast_to(jnp.arange(BLK_DEV, dtype=jnp.int32)[None, :], owners.shape)
    slots = slot_orders[owners, columns]
    return (owners * BLK_DEV + slots).reshape(-1).astype(jnp.int32)


def block_levels(stream_key, extent, cuts, low, top_value):
    gain = 1.0
    for position, blocks in cuts:
        draws = jax.random.uniform(jax.random.fold_in(jax.random.fold_in(stream_key, 6), position), (blocks,), jnp.float32, low / len(cuts), top_value / len(cuts))
        gain = gain * jnp.repeat(jnp.exp(draws), extent[position] // blocks).reshape((-1,) + (1,) * (len(extent) - 1 - position))
    return gain


def length_profile(number_of, total, limit, skew):
    loads = [(1 << 20) // math.isqrt(grade ** skew) + 1 for grade in range(2, number_of + 1)]
    surplus, holding = total - limit - (number_of - 1), [1] * (number_of - 1)
    while surplus > 0:
        candidates = [i for i in range(number_of - 1) if holding[i] < limit]
        mass, remaining = sum([loads[i] for i in candidates]), surplus
        for i in candidates:
            more = min(limit - holding[i], max(1, remaining * loads[i] // mass), surplus)
            holding[i] = holding[i] + more
            surplus = surplus - more
    return np.array([limit] + holding)


def uneven(own_key, amount, total, bound, lean):
    if amount == 2:
        one = jax.random.randint(own_key, (), max(1, total - bound), min(bound, total - 1) + 1)
        return jnp.stack([one, total - one])
    tallies = jnp.asarray(length_profile(amount, total, bound, lean), jnp.int32)
    twos = (amount - 1) // 2
    donor, receiver = tallies[1:1 + 2 * twos:2], tallies[2:2 + 2 * twos:2]
    slack = jnp.minimum(donor - 1, bound - receiver)
    passed = jax.random.randint(jax.random.fold_in(own_key, 1), (twos,), 0, 1 << 20) % (slack + 1)
    tallies = tallies.at[1:1 + 2 * twos:2].set(donor - passed).at[2:2 + 2 * twos:2].set(receiver + passed)
    return tallies[jax.random.permutation(jax.random.fold_in(own_key, 2), amount)]


def normal_values(key, dims, spread, most, cuts=(), kind=jnp.bfloat16):
    gain = block_levels(key, dims, cuts, -0.22, 0.18) if cuts else 1.0
    entries = jax.random.normal(key, dims, jnp.float32) * spread * gain
    return jnp.minimum(jnp.maximum(entries, -most), most).astype(kind)


def setup_inputs(seed: int = 0) -> dict:
    arg_keys = jax.random.split(jax.random.key(seed), 10)
    return {
        "tokens": normal_values(arg_keys[0], (TOKENS, D), 1.0, 6.0, ((0, 16), (1, 8))),
        "segment_ids": jnp.searchsorted(jnp.cumsum(uneven(arg_keys[1], SEGS, TOKENS, TOKENS // 2, 2)), jnp.arange(TOKENS), side="right").astype(jnp.int32),
        "page_table": draw_page_table(jax.random.fold_in(arg_keys[9], 71), 0),
        "pre_gain": jnp.clip(1.0 + 0.18 * jax.random.normal(arg_keys[3], (D,), jnp.float32), 0.099609375, 1.8984375).astype(jnp.bfloat16),
        "post_gain": jnp.clip(1.0 + 0.15 * jax.random.normal(arg_keys[4], (D,), jnp.float32), 0.25, 1.75).astype(jnp.bfloat16),
        "w_query": normal_values(arg_keys[5], (D, HQ * HD), (D // 8) ** -0.5, 0.25, ((0, 16), (1, 8))),
        "w_key": normal_values(arg_keys[6], (D, KVH * HD), D ** -0.5, 0.09375, ((0, 16), (1, 8))),
        "w_value": normal_values(arg_keys[7], (D, KVH * HD), D ** -0.5, 0.09375, ((0, 16), (1, 8))),
        "w_out": normal_values(arg_keys[8], (HQ * HD, D), (HQ * HD) ** -0.5, 0.09375, ((0, 8), (1, 16))),
    }


SOFT_CAP = 50.0
QUERY_SCALE = 1.0 / 12.0
NORM_EPSILON = 1e-06

def rms_scale(values):
    return lax.rsqrt(lax.optimization_barrier(jnp.mean(values * values, axis=-1, keepdims=True)) + NORM_EPSILON)

def rotate_half(values, positions):
    half_width = values.shape[-1] // 2
    inverse_freq = jnp.exp(-math.log(10000.0) * 2.0 * jnp.arange(half_width, dtype=jnp.float32) / values.shape[-1])
    angle_table = positions.astype(jnp.float32)[:, None] * inverse_freq[None, :]
    cosine = jnp.cos(angle_table)[:, None, :]
    sine = jnp.sin(angle_table)[:, None, :]
    first_half = values[..., :half_width]
    second_half = values[..., half_width:]
    return jnp.concatenate([first_half * cosine - second_half * sine, second_half * cosine + first_half * sine], axis=-1)

def reference(tokens, segment_ids, page_table, pre_gain, post_gain, w_query, w_key, w_value, w_out):
    residual = tokens.astype(jnp.float32)
    normed = (residual * rms_scale(residual) * pre_gain.astype(jnp.float32)).astype(jnp.bfloat16)
    query_raw = jnp.dot(normed, w_query, preferred_element_type=jnp.float32).reshape(TOKENS, HQ, HD)
    key_raw = jnp.dot(normed, w_key, preferred_element_type=jnp.float32).reshape(TOKENS, KVH, HD)
    values_new = jnp.dot(normed, w_value, preferred_element_type=jnp.float32).reshape(TOKENS, KVH, HD).astype(jnp.bfloat16)
    token_index = jnp.arange(TOKENS, dtype=jnp.int32)
    labels = jnp.arange(SEGS, dtype=jnp.int32)
    member = segment_ids[:, None] == labels[None, :]
    seg_counts = lax.optimization_barrier(jnp.sum(member.astype(jnp.int32), axis=0))
    seg_firsts = jnp.cumsum(seg_counts) - seg_counts
    seg_start = lax.optimization_barrier(jnp.sum(jnp.where(member, seg_firsts[None, :], 0), axis=1)).astype(jnp.int32)
    positions = token_index - seg_start
    query_new = rotate_half(query_raw, positions).astype(jnp.bfloat16)
    keys_new = rotate_half(key_raw, positions).astype(jnp.bfloat16)
    paired = jnp.concatenate([keys_new, values_new], axis=2)
    token_blocks = paired.reshape(NPAGES, PAGE, KVH, 2 * HD).transpose(0, 2, 1, 3)
    kv_pages = jnp.zeros_like(token_blocks).at[page_table].set(token_blocks)
    padded = jnp.concatenate([jnp.zeros((WINDOW, KVH, 2 * HD), jnp.bfloat16), paired], axis=0)
    key_floor = jnp.maximum(seg_start, token_index - WINDOW + 1)
    group_size = HQ // KVH
    grouped = query_new.reshape(TOKENS, KVH, group_size, HD)

    def one_block(item_index):
        block_index = item_index // KVH
        head_index = item_index % KVH
        first_token = (block_index * TOK_W).astype(jnp.int32)
        rows_all = lax.dynamic_slice_in_dim(grouped, first_token, TOK_W, 0)
        query_rows = lax.dynamic_index_in_dim(rows_all, head_index, 1, keepdims=False)
        keys_all = lax.dynamic_slice_in_dim(padded, first_token, WINDOW + TOK_W, 0)
        key_rows = lax.dynamic_index_in_dim(keys_all, head_index, 1, keepdims=False)
        query_index = first_token + jnp.arange(TOK_W, dtype=jnp.int32)
        key_index = first_token - WINDOW + jnp.arange(WINDOW + TOK_W, dtype=jnp.int32)
        floor_rows = lax.dynamic_slice_in_dim(key_floor, first_token, TOK_W, 0)
        allowed = (key_index[None, :] >= floor_rows[:, None]) & (key_index[None, :] <= query_index[:, None])
        scores = jnp.einsum('qrh,kh->rqk', query_rows.astype(jnp.float32), key_rows[:, :HD].astype(jnp.float32)) * QUERY_SCALE
        capped = SOFT_CAP * jnp.tanh(scores / SOFT_CAP)
        weights = jnp.where(allowed[None], jnp.exp(capped), 0.0)
        totals = lax.optimization_barrier(jnp.sum(weights, axis=2))
        probs = weights.astype(jnp.bfloat16)
        numerator = jnp.einsum('rqk,kh->qrh', probs.astype(jnp.float32), key_rows[:, HD:].astype(jnp.float32))
        return (numerator / jnp.transpose(totals)[:, :, None]).astype(jnp.bfloat16)
    items = jnp.arange(N_WIDE * KVH, dtype=jnp.int32)
    head_outputs = lax.map(one_block, items)
    attn = head_outputs.reshape(N_WIDE, KVH, TOK_W, group_size, HD).transpose(0, 2, 1, 3, 4).reshape(TOKENS, HQ * HD)
    group_width = HQ * HD // N_NARROW

    def add_group(running, group_index):
        start_column = (group_index * group_width).astype(jnp.int32)
        head_columns = lax.dynamic_slice_in_dim(attn, start_column, group_width, 1)
        weight_rows = lax.dynamic_slice_in_dim(w_out, start_column, group_width, 0)
        group_term = jnp.dot(head_columns, weight_rows, preferred_element_type=jnp.float32).astype(jnp.bfloat16)
        group_term = lax.optimization_barrier(group_term)
        return (running + group_term.astype(jnp.float32), None)
    projected, _ = lax.scan(add_group, jnp.zeros((TOKENS, D), jnp.float32), jnp.arange(N_NARROW, dtype=jnp.int32))
    mixed = (residual + projected * rms_scale(projected) * post_gain.astype(jnp.float32)).astype(jnp.bfloat16)
    return (mixed, kv_pages)
```

```python
import functools
import math

import jax
import jax.numpy as jnp
from jax import lax
from jax.experimental import pallas as pl
from jax.experimental.pallas import tpu as pltpu
from jax.sharding import PartitionSpec as P

D = 4608
HD = 128
WINDOW = 4096
SEGS = 8

SOFT_CAP = 50.0
QUERY_SCALE = 1.0 / 12.0
NORM_EPSILON = 1e-06
NX, NY, NZ = 4, 4, 4
MESH = pl.DeviceIdType.MESH
PRE = QUERY_SCALE / SOFT_CAP
POST = SOFT_CAP * math.log2(math.e)


def shifted(value, axis, steps):
    count = lax.axis_size(axis)
    leading, last = (max(0, -steps), min(count, count - steps))
    return lax.ppermute(value, axis, [(source, source + steps) for source in range(leading, last)])


def rms_scale(values):
    return lax.rsqrt(jnp.mean(values * values, axis=-1, keepdims=True) + NORM_EPSILON)


def rotate_half(values, cosine, sine):
    half_width = values.shape[-1] // 2
    first_half = values[..., :half_width]
    second_half = values[..., half_width:]
    return jnp.concatenate(
        [first_half * cosine - second_half * sine, second_half * cosine + first_half * sine],
        axis=-1,
    )


def gather_kernel(
    tok_ref, w_ref, meta_ref, gain_ref,
    tok_all, w_all, meta_all, gain_all,
    w_send, w_recv, z_send, z_recv, c_send, c_recv, m_send, m_recv, g_send, g_recv, own_sem,
):
    wide = lax.axis_index("wide")
    narrow = lax.axis_index("narrow")
    x, y = lax.div(wide, NY), lax.rem(wide, NY)
    z, core = lax.div(narrow, 2), lax.rem(narrow, 2)
    shard = w_ref.shape[0]
    half = shard // 2
    cols = w_ref.shape[1] // 2
    rows = tok_ref.shape[0]

    def ring(position, count, step):
        return lax.rem(position + step + count, count)

    def at_wide(x_new, y_new):
        return {"wide": x_new * NY + y_new}

    def remote(src, dst, send, recv, where):
        return pltpu.make_async_remote_copy(
            src_ref=src, dst_ref=dst, send_sem=send, recv_sem=recv,
            device_id=where, device_id_type=MESH,
        )

    def peer(part, stage, step):
        if (part == 0) == (stage == 0):
            return at_wide(ring(x, NX, step), y)
        return at_wide(x, ring(y, NY, step))

    def block(part, along, across):
        if part == 0:
            return ring(x, NX, along) * NY + ring(y, NY, across)
        return ring(x, NX, across) * NY + ring(y, NY, along)

    def rows_of(part, along, across):
        return pl.ds(block(part, along, across) * shard + part * half, half)

    def send(part, group, kind, along, across, own=False):
        stage = 0 if group == 0 else 1
        where = peer(part, stage, 1 if kind % 2 == 0 else -1)
        there = rows_of(part, along, across)
        if kind < 2:
            span = slice(None)
        else:
            span = pl.ds((kind - 2) * cols, cols)
        if own:
            src = w_ref.at[pl.ds(part * half, half), span]
        else:
            src = w_all.at[there, span]
        return remote(
            src, w_all.at[there, span],
            w_send.at[part, group, kind], w_recv.at[part, group, kind], where,
        )

    started = []

    def start(copy):
        copy.start()
        started.append(copy)
        return copy

    sent = {}

    def go(part, group, kind, along, across, own=False):
        sent[part, group, kind] = start(send(part, group, kind, along, across, own))

    toks = {}

    def zgo(kind, index, src, span):
        where = {"narrow": ring(z, NZ, 1 if kind % 2 == 0 else -1) * 2 + core}
        toks[kind] = start(remote(src, tok_all.at[index, span], z_send.at[kind], z_recv.at[kind], where))

    pair = {}

    def cgo(kind, index, src, span):
        where = {"narrow": z * 2 + (1 - core)}
        pair[kind] = start(remote(src, tok_all.at[index, span], c_send.at[kind], c_recv.at[kind], where))

    every = pl.ds(0, rows)
    low, high = pl.ds(0, rows // 2), pl.ds(rows // 2, rows // 2)

    def zblock(step):
        return ring(z, NZ, step) * 2 + core

    small = []
    for other in range(1, NX * NY):
        target = lax.rem(wide + other, NX * NY)
        small.append(start(remote(
            meta_ref, meta_all.at[wide], m_send.at[other], m_recv.at[other], {"wide": target})))
    for other in range(1, NZ * 2):
        target = lax.rem(narrow + other, NZ * 2)
        small.append(start(remote(
            gain_ref, gain_all.at[narrow], g_send.at[other], g_recv.at[other], {"narrow": target})))

    for part in (0, 1):
        go(part, 0, 0, 0, 0, True)
        go(part, 0, 1, 0, 0, True)
    zgo(0, narrow, tok_ref, every)
    zgo(1, narrow, tok_ref, every)
    cgo(0, narrow, tok_ref, every)
    for part in (0, 1):
        go(part, 1, 0, 0, 0, True)
        go(part, 1, 1, 0, 0, True)
    local = [
        pltpu.make_async_copy(w_ref, w_all.at[pl.ds(wide * shard, shard)], own_sem.at[0]),
        pltpu.make_async_copy(tok_ref, tok_all.at[narrow], own_sem.at[1]),
        pltpu.make_async_copy(meta_ref, meta_all.at[wide], own_sem.at[2]),
        pltpu.make_async_copy(gain_ref, gain_all.at[narrow], own_sem.at[3]),
    ]
    for copy in local:
        copy.start()

    for part in (0, 1):
        sent[part, 0, 0].wait_recv()
        go(part, 0, 2, -1, 0)
        go(part, 2, 0, -1, 0)
        go(part, 2, 1, -1, 0)
    for part in (0, 1):
        sent[part, 0, 1].wait_recv()
        go(part, 0, 3, 1, 0)
        go(part, 3, 0, 1, 0)
        go(part, 3, 1, 1, 0)

    toks[0].wait_recv()
    zgo(2, zblock(-1), tok_all.at[zblock(-1), low], low)
    cgo(1, zblock(-1), tok_all.at[zblock(-1)], every)
    toks[1].wait_recv()
    zgo(3, zblock(1), tok_all.at[zblock(1), high], high)
    cgo(2, zblock(1), tok_all.at[zblock(1)], every)

    for part in (0, 1):
        sent[part, 1, 0].wait_recv()
        go(part, 1, 2, 0, -1)
        sent[part, 1, 1].wait_recv()
        go(part, 1, 3, 0, 1)
    for part in (0, 1):
        sent[part, 0, 2].wait_recv()
        sent[part, 0, 3].wait_recv()
        go(part, 4, 0, 2, 0)
        go(part, 4, 1, 2, 0)
    for group, along in ((2, -1), (3, 1)):
        for part in (0, 1):
            sent[part, group, 0].wait_recv()
            go(part, group, 2, along, -1)
            sent[part, group, 1].wait_recv()
            go(part, group, 3, along, 1)
    toks[2].wait_recv()
    cgo(3, zblock(2), tok_all.at[zblock(2), low], low)
    toks[3].wait_recv()
    cgo(4, zblock(2), tok_all.at[zblock(2), high], high)
    for part in (0, 1):
        sent[part, 4, 0].wait_recv()
        go(part, 4, 2, 2, -1)
        sent[part, 4, 1].wait_recv()
        go(part, 4, 3, 2, 1)

    for part in (0, 1):
        for group in range(1, 5):
            sent[part, group, 2].wait_recv()
            sent[part, group, 3].wait_recv()
    for kind in range(5):
        pair[kind].wait_recv()
    for copy in small:
        copy.wait_recv()
    for copy in local:
        copy.wait()
    for copy in started:
        copy.wait_send()


def gather_all(tokens, weights, meta, gain):
    rows, width = tokens.shape
    shard, columns = weights.shape
    any_spec = pl.BlockSpec(memory_space=pl.ANY)
    vmem_spec = pl.BlockSpec(memory_space=pltpu.VMEM)
    dma = pltpu.SemaphoreType.DMA
    return pl.pallas_call(
        gather_kernel,
        out_shape=(
            jax.ShapeDtypeStruct((8, rows, width), tokens.dtype),
            jax.ShapeDtypeStruct((16 * shard, columns), weights.dtype),
            jax.ShapeDtypeStruct((16,) + meta.shape, meta.dtype),
            jax.ShapeDtypeStruct((8,) + gain.shape, gain.dtype),
        ),
        in_specs=[vmem_spec] * 4,
        out_specs=(any_spec,) * 4,
        scratch_shapes=[
            dma((2, 5, 4)), dma((2, 5, 4)), dma((4,)), dma((4,)), dma((5,)), dma((5,)),
            dma((16,)), dma((16,)), dma((8,)), dma((8,)), dma((4,)),
        ],
        compiler_params=pltpu.CompilerParams(has_side_effects=True),
        name="gather_all",
    )(tokens, weights, meta, gain)


QB = 256


def attention_kernel(q_ref, floor_ref, k0, k1, k2, k3, k4, out_ref, held, total, sems):
    sources = (k0, k1, k2, k3, k4)
    tokens = q_ref.shape[0]
    blocks = tokens // QB
    copies = [
        pltpu.make_async_copy(source, held.at[d], sems.at[d]) for d, source in enumerate(sources)
    ]
    for copy in copies:
        copy.start()

    def lanes(start, size):
        return pl.ds(pl.multiple_of(start, 128), size)

    def chunk(d, g, qb, first, size, diagonal=False, fresh=False):
        qrows = pl.ds(pl.multiple_of(qb * QB, QB), QB)
        krows = pl.ds(pl.multiple_of(first, 256), size)
        query = jnp.concatenate(
            [q_ref[qrows, lanes(g * 256, 128)], q_ref[qrows, lanes(g * 256 + 128, 128)]], axis=0
        )
        keys = held[d, krows, lanes(g * 256, 128)]
        values = held[d, krows, lanes(g * 256 + 128, 128)]
        scores = lax.dot_general(
            query, keys, (((1,), (1,)), ((), ())), preferred_element_type=jnp.float32
        )
        floor = floor_ref[qrows, :] - ((4 - d) * tokens + first)
        floor = jnp.concatenate([floor] * (size // 128), axis=1)
        column = lax.broadcasted_iota(jnp.int32, (QB, size), 1)
        allowed = column >= floor
        if diagonal:
            allowed = allowed & (column <= lax.broadcasted_iota(jnp.int32, (QB, size), 0))
        weights = jnp.exp2(jnp.tanh(scores * PRE) * POST)
        weights = jnp.concatenate(
            [
                jnp.where(allowed, weights[:QB], 0.0).astype(jnp.bfloat16),
                jnp.where(allowed, weights[QB:], 0.0).astype(jnp.bfloat16),
            ],
            axis=0,
        )
        wide_values = jnp.concatenate([values, jnp.ones_like(values)], axis=1)
        product = jnp.dot(weights, wide_values, preferred_element_type=jnp.float32)
        slot = g * blocks + qb
        if fresh:
            total[slot] = product
        else:
            total[slot] += product

    for d in range(5):
        copies[d].wait()

        def pair(t, carry):
            g, qb = lax.div(t, blocks), lax.rem(t, blocks)
            if d == 0:
                chunk(0, g, qb, qb * QB, QB, diagonal=True, fresh=True)
                lax.fori_loop(0, qb, lambda k, c: (chunk(0, g, qb, k * QB, QB), c)[1], 0)
            elif d < 4:
                chunk(d, g, qb, 0, tokens // 2)
                chunk(d, g, qb, tokens // 2, tokens // 2)
            else:
                lax.fori_loop(qb, blocks, lambda k, c: (chunk(4, g, qb, k * QB, QB), c)[1], 0)
                slot = g * blocks + qb
                result = (total[slot, :, :HD] / total[slot, :, HD:]).astype(out_ref.dtype)
                qrows = pl.ds(pl.multiple_of(qb * QB, QB), QB)
                out_ref[qrows, lanes(g * 256, 128)] = result[:QB]
                out_ref[qrows, lanes(g * 256 + 128, 128)] = result[QB:]
            return carry

        lax.fori_loop(0, 2 * blocks, pair, 0)


def attention(query, floor, sources):
    tokens = query.shape[0]
    vmem_spec = pl.BlockSpec(memory_space=pltpu.VMEM)
    any_spec = pl.BlockSpec(memory_space=pl.ANY)
    return pl.pallas_call(
        attention_kernel,
        out_shape=jax.ShapeDtypeStruct(query.shape, jnp.bfloat16),
        in_specs=[vmem_spec, vmem_spec] + [any_spec] * 5,
        out_specs=vmem_spec,
        scratch_shapes=[
            pltpu.VMEM((5,) + sources[0].shape, jnp.bfloat16),
            pltpu.VMEM((8, 2 * QB, 256), jnp.float32),
            pltpu.SemaphoreType.DMA((5,)),
        ],
        cost_estimate=pl.CostEstimate(
            flops=4 * tokens * 4352 * 128 * 8, bytes_accessed=8 << 20,
            transcendentals=8 * tokens * 4352,
        ),
        compiler_params=pltpu.CompilerParams(vmem_limit_bytes=40 << 20),
        name="attention",
    )(query, floor, *sources)


def local(tokens, segment_ids, page_table, pre_gain, post_gain, w_query, w_key, w_value, w_out):
    tok_w = tokens.shape[0]
    shard_count = lax.axis_size("wide")
    shard_index = lax.axis_index("wide")
    block_count = page_table.shape[0]
    seg_rows = segment_ids.reshape(8, tok_w // 8)
    table_row = jnp.pad(page_table[None, :], ((0, 7), (0, tok_w // 8 - block_count)))
    meta = jnp.concatenate([seg_rows, table_row], axis=0)
    gain_in = jnp.pad(pre_gain[None, :], ((0, 15), (0, 64)))
    weights = jnp.concatenate([w_query, w_key, w_value], axis=1)
    tok_all, w_all, meta_all, gain_all = gather_all(tokens, weights, meta, gain_in)

    residual = tokens.astype(jnp.float32)
    gathered = jnp.transpose(tok_all, (1, 0, 2)).reshape(tok_w, D)
    features = gathered.astype(jnp.float32)
    gain = gain_all[:, 0, : pre_gain.shape[0]].reshape(D)
    normed = (features * rms_scale(features) * gain.astype(jnp.float32)).astype(jnp.bfloat16)

    labels = jnp.arange(SEGS, dtype=jnp.int32)
    all_ids = meta_all[:, :8, :].reshape(-1)
    table_all = meta_all[:, 8, :block_count].reshape(-1)
    seg_firsts = jnp.sum((all_ids[:, None] < labels[None, :]).astype(jnp.int32), axis=0)
    member = segment_ids[:, None] == labels[None, :]
    seg_start = jnp.sum(jnp.where(member, seg_firsts[None, :], 0), axis=1)
    first_token = shard_index * tok_w
    token_index = first_token + jnp.arange(tok_w, dtype=jnp.int32)
    positions = token_index - seg_start
    half_width = HD // 2
    inverse_freq = jnp.exp(
        -math.log(10000.0) * 2.0 * jnp.arange(half_width, dtype=jnp.float32) / HD
    )
    angle_table = positions.astype(jnp.float32)[:, None] * inverse_freq[None, :]
    cosine = jnp.cos(angle_table)[:, None, :]
    sine = jnp.sin(angle_table)[:, None, :]

    heads_here = w_query.shape[1] // HD
    pairs_here = w_key.shape[1] // HD
    raw = jnp.dot(normed, w_all, preferred_element_type=jnp.float32)
    q_width, k_width = w_query.shape[1], w_key.shape[1]
    query_raw = raw[:, :q_width]
    key_raw = raw[:, q_width : q_width + k_width]
    value_raw = raw[:, q_width + k_width :]
    keys_new = rotate_half(key_raw.reshape(tok_w, pairs_here, HD), cosine, sine).astype(
        jnp.bfloat16
    )
    values_new = value_raw.reshape(tok_w, pairs_here, HD).astype(jnp.bfloat16)
    paired = jnp.concatenate([keys_new, values_new], axis=2)
    flat = paired.reshape(tok_w, pairs_here * 2 * HD)
    reach_depth = min((WINDOW - 1) // tok_w + 1, shard_count - 1)
    sources = [flat] + [shifted(flat, "wide", distance + 1) for distance in range(reach_depth)]
    query_new = rotate_half(query_raw.reshape(tok_w, heads_here, HD), cosine, sine).astype(
        jnp.bfloat16
    ).reshape(tok_w, heads_here * HD)
    key_floor = jnp.maximum(seg_start, token_index - WINDOW + 1) - (first_token - WINDOW)
    floor = jnp.broadcast_to(key_floor[:, None], (tok_w, 128))
    w_out_late, _ = lax.optimization_barrier((w_out, w_all[:8, :128]))
    w_out_all = lax.all_gather(w_out_late, "wide", axis=1, tiled=True)
    attn_out = attention(query_new, floor, sources)

    head_terms = jnp.dot(attn_out, w_out_all, preferred_element_type=jnp.float32)
    projected = lax.psum_scatter(
        head_terms.astype(jnp.bfloat16), "narrow", scatter_dimension=1, tiled=True
    ).astype(jnp.float32)
    square_sums = lax.psum(jnp.sum(projected * projected, axis=1), "narrow")
    post_scale = lax.rsqrt(square_sums / D + NORM_EPSILON)
    mixed = (residual + projected * post_scale[:, None] * post_gain.astype(jnp.float32)).astype(
        jnp.bfloat16
    )
    page_len = tok_w // block_count
    token_blocks = paired.reshape(block_count, page_len, pairs_here, 2 * HD)
    owners = page_table // block_count
    shard_ids = jnp.arange(shard_count, dtype=jnp.int32)
    send_pick = (owners[None, :] == shard_ids[:, None]).astype(jnp.bfloat16)
    outgoing = jnp.einsum(
        "sj,jpgc->sgpc", send_pick, token_blocks, preferred_element_type=jnp.float32
    ).astype(jnp.bfloat16)
    incoming = lax.all_to_all(outgoing, "wide", split_axis=0, concat_axis=0, tiled=True)
    my_pages = shard_index * block_count + jnp.arange(block_count, dtype=jnp.int32)
    found_page = table_all[None, :] == my_pages[:, None]
    anchor = jnp.sum(
        jnp.where(
            found_page, jnp.arange(table_all.shape[0], dtype=jnp.int32)[None, :] // block_count, 0
        ),
        axis=1,
    )
    take_pick = (anchor[:, None] == shard_ids[None, :]).astype(jnp.bfloat16)
    kv_pages = jnp.einsum(
        "qs,sgpc->qgpc", take_pick, incoming, preferred_element_type=jnp.float32
    ).astype(jnp.bfloat16)
    return (mixed, kv_pages)


def solution(mesh):
    return jax.shard_map(
        local,
        mesh=mesh,
        in_specs=(
            P("wide", "narrow"),
            P("wide"),
            P("wide"),
            P("narrow"),
            P("narrow"),
            P("wide", "narrow"),
            P("wide", "narrow"),
            P("wide", "narrow"),
            P("narrow", "wide"),
        ),
        out_specs=(P("wide", "narrow"), P("wide", "narrow", None, None)),
        check_vma=False,
    )
```

```python
import functools
import math

import jax
import jax.numpy as jnp
from jax import lax
from jax.experimental import pallas as pl
from jax.experimental.pallas import tpu as pltpu
from jax.sharding import PartitionSpec as P

D = 4608
HD = 128
WINDOW = 4096
SEGS = 8

SOFT_CAP = 50.0
QUERY_SCALE = 1.0 / 12.0
NORM_EPSILON = 1e-06
NX, NY, NZ = 4, 4, 4
MESH = pl.DeviceIdType.MESH
PRE = QUERY_SCALE / SOFT_CAP
POST = SOFT_CAP * math.log2(math.e)


def gather_kernel(
    tok_ref, w_ref, meta_ref, gain_ref,
    tok_all, w_all, meta_all, gain_all,
    w_send, w_recv, z_send, z_recv, c_send, c_recv, m_send, m_recv, g_send, g_recv, own_sem,
):
    wide = lax.axis_index("wide")
    narrow = lax.axis_index("narrow")
    x, y = lax.div(wide, NY), lax.rem(wide, NY)
    z, core = lax.div(narrow, 2), lax.rem(narrow, 2)
    shard = w_ref.shape[0]
    half = shard // 2
    cols = w_ref.shape[1] // 2
    rows = tok_ref.shape[0]

    def ring(position, count, step):
        return lax.rem(position + step + count, count)

    def at_wide(x_new, y_new):
        return {"wide": x_new * NY + y_new}

    def remote(src, dst, send, recv, where):
        return pltpu.make_async_remote_copy(
            src_ref=src, dst_ref=dst, send_sem=send, recv_sem=recv,
            device_id=where, device_id_type=MESH,
        )

    def peer(part, stage, step):
        if (part == 0) == (stage == 0):
            return at_wide(ring(x, NX, step), y)
        return at_wide(x, ring(y, NY, step))

    def block(part, along, across):
        if part == 0:
            return ring(x, NX, along) * NY + ring(y, NY, across)
        return ring(x, NX, across) * NY + ring(y, NY, along)

    def rows_of(part, along, across):
        return pl.ds(block(part, along, across) * shard + part * half, half)

    def send(part, group, kind, along, across, own=False):
        stage = 0 if group == 0 else 1
        where = peer(part, stage, 1 if kind % 2 == 0 else -1)
        there = rows_of(part, along, across)
        if kind < 2:
            span = slice(None)
        else:
            span = pl.ds((kind - 2) * cols, cols)
        if own:
            src = w_ref.at[pl.ds(part * half, half), span]
        else:
            src = w_all.at[there, span]
        return remote(
            src, w_all.at[there, span],
            w_send.at[part, group, kind], w_recv.at[part, group, kind], where,
        )

    started = []

    def start(copy):
        copy.start()
        started.append(copy)
        return copy

    sent = {}

    def go(part, group, kind, along, across, own=False):
        sent[part, group, kind] = start(send(part, group, kind, along, across, own))

    toks = {}

    def zgo(kind, index, src, span):
        where = {"narrow": ring(z, NZ, 1 if kind % 2 == 0 else -1) * 2 + core}
        toks[kind] = start(remote(src, tok_all.at[index, span], z_send.at[kind], z_recv.at[kind], where))

    pair = {}

    def cgo(kind, index, src, span):
        where = {"narrow": z * 2 + (1 - core)}
        pair[kind] = start(remote(src, tok_all.at[index, span], c_send.at[kind], c_recv.at[kind], where))

    every = pl.ds(0, rows)
    low, high = pl.ds(0, rows // 2), pl.ds(rows // 2, rows // 2)

    def zblock(step):
        return ring(z, NZ, step) * 2 + core

    small = []
    for other in range(1, NX * NY):
        target = lax.rem(wide + other, NX * NY)
        small.append(start(remote(
            meta_ref, meta_all.at[wide], m_send.at[other], m_recv.at[other], {"wide": target})))
    for other in range(1, NZ * 2):
        target = lax.rem(narrow + other, NZ * 2)
        small.append(start(remote(
            gain_ref, gain_all.at[narrow], g_send.at[other], g_recv.at[other], {"narrow": target})))

    for part in (0, 1):
        go(part, 0, 0, 0, 0, True)
        go(part, 0, 1, 0, 0, True)
    zgo(0, narrow, tok_ref, every)
    zgo(1, narrow, tok_ref, every)
    cgo(0, narrow, tok_ref, every)
    for part in (0, 1):
        go(part, 1, 0, 0, 0, True)
        go(part, 1, 1, 0, 0, True)
    local = [
        pltpu.make_async_copy(w_ref, w_all.at[pl.ds(wide * shard, shard)], own_sem.at[0]),
        pltpu.make_async_copy(tok_ref, tok_all.at[narrow], own_sem.at[1]),
        pltpu.make_async_copy(meta_ref, meta_all.at[wide], own_sem.at[2]),
        pltpu.make_async_copy(gain_ref, gain_all.at[narrow], own_sem.at[3]),
    ]
    for copy in local:
        copy.start()

    for part in (0, 1):
        sent[part, 0, 0].wait_recv()
        go(part, 0, 2, -1, 0)
        go(part, 2, 0, -1, 0)
        go(part, 2, 1, -1, 0)
    for part in (0, 1):
        sent[part, 0, 1].wait_recv()
        go(part, 0, 3, 1, 0)
        go(part, 3, 0, 1, 0)
        go(part, 3, 1, 1, 0)

    toks[0].wait_recv()
    zgo(2, zblock(-1), tok_all.at[zblock(-1), low], low)
    cgo(1, zblock(-1), tok_all.at[zblock(-1)], every)
    toks[1].wait_recv()
    zgo(3, zblock(1), tok_all.at[zblock(1), high], high)
    cgo(2, zblock(1), tok_all.at[zblock(1)], every)

    for part in (0, 1):
        sent[part, 1, 0].wait_recv()
        go(part, 1, 2, 0, -1)
        sent[part, 1, 1].wait_recv()
        go(part, 1, 3, 0, 1)
    for part in (0, 1):
        sent[part, 0, 2].wait_recv()
        sent[part, 0, 3].wait_recv()
        go(part, 4, 0, 2, 0)
        go(part, 4, 1, 2, 0)
    for group, along in ((2, -1), (3, 1)):
        for part in (0, 1):
            sent[part, group, 0].wait_recv()
            go(part, group, 2, along, -1)
            sent[part, group, 1].wait_recv()
            go(part, group, 3, along, 1)
    toks[2].wait_recv()
    cgo(3, zblock(2), tok_all.at[zblock(2), low], low)
    toks[3].wait_recv()
    cgo(4, zblock(2), tok_all.at[zblock(2), high], high)
    for part in (0, 1):
        sent[part, 4, 0].wait_recv()
        go(part, 4, 2, 2, -1)
        sent[part, 4, 1].wait_recv()
        go(part, 4, 3, 2, 1)

    for part in (0, 1):
        for group in range(1, 5):
            sent[part, group, 2].wait_recv()
            sent[part, group, 3].wait_recv()
    for kind in range(5):
        pair[kind].wait_recv()
    for copy in small:
        copy.wait_recv()
    for copy in local:
        copy.wait()
    for copy in started:
        copy.wait_send()


def gather_all(tokens, weights, meta, gain):
    rows, width = tokens.shape
    shard, columns = weights.shape
    any_spec = pl.BlockSpec(memory_space=pl.ANY)
    vmem_spec = pl.BlockSpec(memory_space=pltpu.VMEM)
    dma = pltpu.SemaphoreType.DMA
    return pl.pallas_call(
        gather_kernel,
        out_shape=(
            jax.ShapeDtypeStruct((8, rows, width), tokens.dtype),
            jax.ShapeDtypeStruct((16 * shard, columns), weights.dtype),
            jax.ShapeDtypeStruct((16,) + meta.shape, meta.dtype),
            jax.ShapeDtypeStruct((8,) + gain.shape, gain.dtype),
        ),
        in_specs=[vmem_spec] * 4,
        out_specs=(any_spec,) * 4,
        scratch_shapes=[
            dma((2, 5, 4)), dma((2, 5, 4)), dma((4,)), dma((4,)), dma((5,)), dma((5,)),
            dma((16,)), dma((16,)), dma((8,)), dma((8,)), dma((4,)),
        ],
        compiler_params=pltpu.CompilerParams(has_side_effects=True),
        name="gather_all",
    )(tokens, weights, meta, gain)


QB = 256
REACH = 4


def lanes(start, size):
    return pl.ds(pl.multiple_of(start, 128), size)


def attention_kernel(
    tok_hbm, w_hbm, gain_ref, cos_ref, sin_ref, floor_ref,
    out_ref, kv_hbm,
    tok, w, query_all, held, total, tok_sem, w_sem, kv_sem, send, recv,
):
    parts, tokens, width = tok.shape
    blocks = tokens // QB
    half = w.shape[1] // 2
    wide = lax.axis_index("wide")
    count = NX * NY

    def block_rows(b):
        return pl.ds(pl.multiple_of(b * QB, QB), QB)

    def load_tok(b):
        return pltpu.make_async_copy(
            tok_hbm.at[:, block_rows(b), :], tok.at[:, block_rows(b), :], tok_sem.at[b]
        )

    loads_w = [
        pltpu.make_async_copy(
            w_hbm.at[:, pl.ds(part * half, half)], w.at[:, pl.ds(part * half, half)], w_sem.at[part]
        )
        for part in range(2)
    ]
    load_tok(0).start()
    loads_w[0].start()
    for b in range(1, blocks):
        load_tok(b).start()
    loads_w[1].start()

    def rotated(value, rows):
        return value * cos_ref[rows, :] + pltpu.roll(value, HD // 2, 1) * sin_ref[rows, :]

    loads_w[0].wait()

    def key_block(b, carry):
        load_tok(b).wait()
        rows = block_rows(b)
        squares = jnp.zeros((QB, 1), jnp.float32)
        for n in range(parts):
            piece = tok[n, rows, :].astype(jnp.float32)
            squares += jnp.sum(piece * piece, axis=1, keepdims=True)
        scale = lax.rsqrt(squares / D + NORM_EPSILON)
        product = jnp.zeros((QB, half), jnp.float32)
        for n in range(parts):
            piece = tok[n, rows, :].astype(jnp.float32)
            normed = (piece * scale * gain_ref[n, 0:1, :].astype(jnp.float32)).astype(jnp.bfloat16)
            tok[n, rows, :] = normed
            product += jnp.dot(
                normed, w[pl.ds(n * width, width), 0:half], preferred_element_type=jnp.float32
            )
        for g in range(2):
            key = product[:, g * 256 : g * 256 + HD]
            held[0, rows, g * 256 : g * 256 + HD] = rotated(key, rows).astype(jnp.bfloat16)
            held[0, rows, g * 256 + HD : g * 256 + 256] = product[
                :, g * 256 + HD : g * 256 + 256
            ].astype(jnp.bfloat16)
        return carry

    lax.fori_loop(0, blocks, key_block, 0)
    save = pltpu.make_async_copy(held.at[0], kv_hbm, kv_sem)
    save.start()
    moves = {}
    for d in (1, 4, 2, 3):
        moves[d] = pltpu.make_async_remote_copy(
            src_ref=held.at[0], dst_ref=held.at[d], send_sem=send.at[d], recv_sem=recv.at[d],
            device_id={"wide": lax.rem(wide + d, count)}, device_id_type=MESH,
        )
        moves[d].start()
    loads_w[1].wait()

    def query_block(b, carry):
        rows = block_rows(b)
        product = jnp.zeros((QB, half), jnp.float32)
        for n in range(parts):
            product += jnp.dot(
                tok[n, rows, :], w[pl.ds(n * width, width), half : 2 * half],
                preferred_element_type=jnp.float32,
            )
        for h in range(half // HD):
            value = product[:, h * HD : (h + 1) * HD]
            query_all[rows, h * HD : (h + 1) * HD] = rotated(value, rows).astype(jnp.bfloat16)
        return carry

    lax.fori_loop(0, blocks, query_block, 0)

    def chunk(d, g, qb, first, size, diagonal=False, fresh=False):
        qrows = block_rows(qb)
        krows = pl.ds(pl.multiple_of(first, 256), size)
        query = jnp.concatenate(
            [query_all[qrows, lanes(g * 256, 128)], query_all[qrows, lanes(g * 256 + 128, 128)]],
            axis=0,
        )
        keys = held[d, krows, lanes(g * 256, 128)]
        values = held[d, krows, lanes(g * 256 + 128, 128)]
        scores = lax.dot_general(
            query, keys, (((1,), (1,)), ((), ())), preferred_element_type=jnp.float32
        )
        floor = floor_ref[qrows, :] - ((REACH - d) * tokens + first)
        floor = jnp.concatenate([floor] * (size // 128), axis=1)
        column = lax.broadcasted_iota(jnp.int32, (QB, size), 1)
        allowed = column >= floor
        if diagonal:
            allowed = allowed & (column <= lax.broadcasted_iota(jnp.int32, (QB, size), 0))
        weights = jnp.exp2(jnp.tanh(scores * PRE) * POST)
        weights = jnp.concatenate(
            [
                jnp.where(allowed, weights[:QB], 0.0).astype(jnp.bfloat16),
                jnp.where(allowed, weights[QB:], 0.0).astype(jnp.bfloat16),
            ],
            axis=0,
        )
        wide_values = jnp.concatenate([values, jnp.ones_like(values)], axis=1)
        product = jnp.dot(weights, wide_values, preferred_element_type=jnp.float32)
        slot = g * blocks + qb
        if fresh:
            total[slot] = product
        else:
            total[slot] += product

    for d in (0, 1, 4, 2, 3):
        if d > 0:
            moves[d].wait_recv()

        def pair(t, carry):
            g, qb = lax.div(t, blocks), lax.rem(t, blocks)
            if d == 0:
                chunk(0, g, qb, qb * QB, QB, diagonal=True, fresh=True)
                lax.fori_loop(0, qb, lambda k, c: (chunk(0, g, qb, k * QB, QB), c)[1], 0)
            elif d < REACH:
                chunk(d, g, qb, 0, tokens // 2)
                chunk(d, g, qb, tokens // 2, tokens // 2)
            else:
                lax.fori_loop(qb, blocks, lambda k, c: (chunk(4, g, qb, k * QB, QB), c)[1], 0)
            if d == 3:
                slot = g * blocks + qb
                result = (total[slot, :, :HD] / total[slot, :, HD:]).astype(out_ref.dtype)
                out_ref[block_rows(qb), lanes(g * 256, 128)] = result[:QB]
                out_ref[block_rows(qb), lanes(g * 256 + 128, 128)] = result[QB:]
            return carry

        lax.fori_loop(0, 2 * blocks, pair, 0)
    save.wait()
    for d in range(1, REACH + 1):
        moves[d].wait_send()


def attention(tok_all, w_all, gain, cosine, sine, floor):
    parts, tokens, width = tok_all.shape
    columns = w_all.shape[1]
    half = columns // 2
    vmem_spec = pl.BlockSpec(memory_space=pltpu.VMEM)
    any_spec = pl.BlockSpec(memory_space=pl.ANY)
    dma = pltpu.SemaphoreType.DMA
    return pl.pallas_call(
        attention_kernel,
        out_shape=(
            jax.ShapeDtypeStruct((tokens, half), jnp.bfloat16),
            jax.ShapeDtypeStruct((tokens, half), jnp.bfloat16),
        ),
        in_specs=[any_spec] * 2 + [vmem_spec] * 4,
        out_specs=(vmem_spec, any_spec),
        scratch_shapes=[
            pltpu.VMEM(tok_all.shape, jnp.bfloat16),
            pltpu.VMEM(w_all.shape, jnp.bfloat16),
            pltpu.VMEM((tokens, half), jnp.bfloat16),
            pltpu.VMEM((REACH + 1, tokens, half), jnp.bfloat16),
            pltpu.VMEM((8, 2 * QB, 256), jnp.float32),
            dma((tokens // QB,)), dma((2,)), dma, dma((REACH + 1,)), dma((REACH + 1,)),
        ],
        cost_estimate=pl.CostEstimate(
            flops=4 * tokens * 4352 * 128 * 8, bytes_accessed=32 << 20,
            transcendentals=8 * tokens * 4352,
        ),
        compiler_params=pltpu.CompilerParams(
            vmem_limit_bytes=56 << 20, has_side_effects=True
        ),
        name="attention",
    )(tok_all, w_all, gain, cosine, sine, floor)


def tail_kernel(
    attn_ref, w_ref, tok_ref, gain_ref, pages_hbm,
    mixed_ref, pages_in,
    give, take, stage, far, near, kept, squares,
    p_send, p_recv, own_sem, c_send, c_recv, f_send, f_recv, n_send, n_recv, s_send, s_recv,
):
    wide = lax.axis_index("wide")
    narrow = lax.axis_index("narrow")
    z, core = lax.div(narrow, 2), lax.rem(narrow, 2)
    count = NX * NY
    tokens = attn_ref.shape[0]
    mid = tokens // 2
    low, high = pl.ds(0, mid), pl.ds(mid, mid)
    sibling = {"narrow": z * 2 + (1 - core)}

    def at_z(step):
        return lax.rem(z + step + NZ, NZ)

    def remote(src, dst, send, recv, where):
        copy = pltpu.make_async_remote_copy(
            src_ref=src, dst_ref=dst, send_sem=send, recv_sem=recv,
            device_id=where, device_id_type=MESH,
        )
        copy.start()
        return copy

    pages = [
        remote(
            pages_hbm.at[lax.rem(wide + other, count)], pages_in.at[wide],
            p_send.at[other], p_recv.at[other], {"wide": lax.rem(wide + other, count)},
        )
        for other in range(1, count)
    ]
    own = pltpu.make_async_copy(pages_hbm.at[wide], pages_in.at[wide], own_sem)
    own.start()

    def term(index, rows):
        weights = jnp.concatenate([w_ref[2 * index], w_ref[2 * index + 1]], axis=1)
        return jnp.dot(
            attn_ref[rows, :], weights, preferred_element_type=jnp.float32
        ).astype(jnp.bfloat16)

    def over_rows(body, first=0, size=tokens):
        def step(b, carry):
            body(pl.ds(pl.multiple_of(first + b * QB, QB), QB))
            return carry

        lax.fori_loop(0, size // QB, step, 0)

    steps = (2, 1, -1, 0)
    passes = []
    for i, step in enumerate(steps):
        index = at_z(step) * 2 + (1 - core)

        def fill(rows, i=i, index=index):
            give[i, rows, :] = term(index, rows)

        over_rows(fill)
        passes.append(remote(give.at[i], take.at[i], c_send.at[i], c_recv.at[i], sibling))

    def own_sum(i, rows):
        mine = term(at_z(steps[i]) * 2 + core, rows)
        return mine.astype(jnp.float32) + take[i, rows, :].astype(jnp.float32)

    def put(i):
        def body(rows):
            stage[i, rows, :] = own_sum(i, rows).astype(jnp.bfloat16)

        return body

    ahead, behind = {"narrow": at_z(1) * 2 + core}, {"narrow": at_z(-1) * 2 + core}
    passes[0].wait_recv()
    over_rows(put(0), 0, mid)
    far_up = remote(stage.at[0, low], far.at[0], f_send.at[0], f_recv.at[0], ahead)
    over_rows(put(0), mid, mid)
    far_down = remote(stage.at[0, high], far.at[1], f_send.at[1], f_recv.at[1], behind)
    passes[1].wait_recv()
    over_rows(put(1), mid, mid)
    near_a = remote(stage.at[1, high], near.at[0, high], n_send.at[0], n_recv.at[0], ahead)
    passes[2].wait_recv()
    over_rows(put(2), 0, mid)
    near_b = remote(stage.at[2, low], near.at[1, low], n_send.at[1], n_recv.at[1], behind)

    far_up.wait_recv()

    def with_far_up(rows):
        stage[1, rows, :] = (own_sum(1, rows) + far[0, rows, :].astype(jnp.float32)).astype(
            jnp.bfloat16
        )

    over_rows(with_far_up, 0, mid)
    near_c = remote(stage.at[1, low], near.at[0, low], n_send.at[2], n_recv.at[2], ahead)
    far_down.wait_recv()

    def with_far_down(b, carry):
        rows = pl.ds(pl.multiple_of(mid + b * QB, QB), QB)
        source = pl.ds(pl.multiple_of(b * QB, QB), QB)
        stage[2, rows, :] = (own_sum(2, rows) + far[1, source, :].astype(jnp.float32)).astype(
            jnp.bfloat16
        )
        return carry

    lax.fori_loop(0, mid // QB, with_far_down, 0)
    near_d = remote(stage.at[2, high], near.at[1, high], n_send.at[3], n_recv.at[3], behind)
    passes[3].wait_recv()

    def keep(rows):
        kept[rows, :] = own_sum(3, rows)

    over_rows(keep)
    for copy in (near_a, near_b, near_c, near_d):
        copy.wait_recv()

    ones = jnp.ones((8, tok_ref.shape[1]), jnp.float32)

    def finish(rows):
        value = (
            kept[rows, :]
            + near[0, rows, :].astype(jnp.float32)
            + near[1, rows, :].astype(jnp.float32)
        )
        kept[rows, :] = value
        squares[0, :, rows] = lax.dot_general(
            ones, value * value, (((1,), (1,)), ((), ())),
            precision=lax.Precision.HIGHEST, preferred_element_type=jnp.float32,
        )

    over_rows(finish)
    sums = [
        remote(
            squares.at[0], squares.at[other], s_send.at[other], s_recv.at[other],
            {"narrow": lax.rem(narrow + other, NZ * 2)},
        )
        for other in range(1, NZ * 2)
    ]
    for copy in sums:
        copy.wait_recv()
    pick = jnp.full((8, 128), 0.125, jnp.float32)

    def emit(rows):
        whole = squares[0, :, rows]
        for other in range(1, NZ * 2):
            whole += squares[other, :, rows]
        column = lax.dot_general(
            whole, pick, (((0,), (0,)), ((), ())),
            precision=lax.Precision.HIGHEST, preferred_element_type=jnp.float32,
        )
        scale = lax.rsqrt(column / D + NORM_EPSILON)[:, 0:1]
        mixed_ref[rows, :] = (
            tok_ref[rows, :].astype(jnp.float32)
            + kept[rows, :] * scale * gain_ref[0:1, :].astype(jnp.float32)
        ).astype(jnp.bfloat16)

    over_rows(emit)
    for copy in pages:
        copy.wait_recv()
    own.wait()
    for copy in pages + passes + sums:
        copy.wait_send()
    for copy in (far_up, far_down, near_a, near_b, near_c, near_d):
        copy.wait_send()


def tail(attn, w_out_all, tokens, post_gain, outgoing):
    rows, width = tokens.shape
    vmem_spec = pl.BlockSpec(memory_space=pltpu.VMEM)
    any_spec = pl.BlockSpec(memory_space=pl.ANY)
    dma = pltpu.SemaphoreType.DMA
    bf16 = jnp.bfloat16
    return pl.pallas_call(
        tail_kernel,
        out_shape=(
            jax.ShapeDtypeStruct(tokens.shape, bf16),
            jax.ShapeDtypeStruct(outgoing.shape, bf16),
        ),
        in_specs=[vmem_spec] * 4 + [any_spec],
        out_specs=(vmem_spec, any_spec),
        scratch_shapes=[
            pltpu.VMEM((4, rows, width), bf16),
            pltpu.VMEM((4, rows, width), bf16),
            pltpu.VMEM((3, rows, width), bf16),
            pltpu.VMEM((2, rows // 2, width), bf16),
            pltpu.VMEM((2, rows, width), bf16),
            pltpu.VMEM((rows, width), jnp.float32),
            pltpu.VMEM((8, 8, rows), jnp.float32),
            dma((16,)), dma((16,)), dma, dma((4,)), dma((4,)), dma((2,)), dma((2,)),
            dma((4,)), dma((4,)), dma((8,)), dma((8,)),
        ],
        cost_estimate=pl.CostEstimate(
            flops=2 * rows * 512 * D, bytes_accessed=24 << 20, transcendentals=0
        ),
        compiler_params=pltpu.CompilerParams(
            vmem_limit_bytes=56 << 20, has_side_effects=True
        ),
        name="tail",
    )(attn, w_out_all, tokens, post_gain, outgoing)


def local(tokens, segment_ids, page_table, pre_gain, post_gain, w_query, w_key, w_value, w_out):
    tok_w = tokens.shape[0]
    shard_count = lax.axis_size("wide")
    shard_index = lax.axis_index("wide")
    block_count = page_table.shape[0]
    pairs_here = w_key.shape[1] // HD
    seg_rows = segment_ids.reshape(8, tok_w // 8)
    table_row = jnp.pad(page_table[None, :], ((0, 7), (0, tok_w // 8 - block_count)))
    meta = jnp.concatenate([seg_rows, table_row], axis=0)
    gain_in = jnp.pad(pre_gain[None, :], ((0, 15), (0, 0)))
    columns = []
    for g in range(pairs_here):
        columns += [w_key[:, g * HD : (g + 1) * HD], w_value[:, g * HD : (g + 1) * HD]]
    weights = jnp.concatenate(columns + [w_query], axis=1)
    tok_all, w_all, meta_all, gain_all = gather_all(tokens, weights, meta, gain_in)
    w_out_late, _ = lax.optimization_barrier((w_out, meta_all))
    w_out_all = lax.all_gather(w_out_late, "wide", axis=0, tiled=False)

    labels = jnp.arange(SEGS, dtype=jnp.int32)
    all_ids = meta_all[:, :8, :].reshape(-1)
    table_all = meta_all[:, 8, :block_count].reshape(-1)
    seg_firsts = jnp.sum((all_ids[:, None] < labels[None, :]).astype(jnp.int32), axis=0)
    member = segment_ids[:, None] == labels[None, :]
    seg_start = jnp.sum(jnp.where(member, seg_firsts[None, :], 0), axis=1)
    first_token = shard_index * tok_w
    token_index = first_token + jnp.arange(tok_w, dtype=jnp.int32)
    positions = token_index - seg_start
    half_width = HD // 2
    inverse_freq = jnp.exp(
        -math.log(10000.0) * 2.0 * jnp.arange(half_width, dtype=jnp.float32) / HD
    )
    angle_table = positions.astype(jnp.float32)[:, None] * inverse_freq[None, :]
    cosine = jnp.cos(angle_table)
    sine = jnp.sin(angle_table)
    cosine = jnp.concatenate([cosine, cosine], axis=1)
    sine = jnp.concatenate([-sine, sine], axis=1)
    key_floor = jnp.maximum(seg_start, token_index - WINDOW + 1) - (first_token - WINDOW)
    floor = jnp.broadcast_to(key_floor[:, None], (tok_w, 128))
    attn_out, flat = attention(tok_all, w_all, gain_all, cosine, sine, floor)

    page_len = tok_w // block_count
    token_blocks = flat.reshape(block_count, page_len, pairs_here, 2 * HD)
    owners = page_table // block_count
    shard_ids = jnp.arange(shard_count, dtype=jnp.int32)
    send_pick = (owners[None, :] == shard_ids[:, None]).astype(jnp.bfloat16)
    outgoing = jnp.einsum(
        "sj,jpgc->sgpc", send_pick, token_blocks, preferred_element_type=jnp.float32
    ).astype(jnp.bfloat16)
    mixed, incoming = tail(
        attn_out, w_out_all, tokens, jnp.pad(post_gain[None, :], ((0, 15), (0, 0))), outgoing
    )
    my_pages = shard_index * block_count + jnp.arange(block_count, dtype=jnp.int32)
    found_page = table_all[None, :] == my_pages[:, None]
    anchor = jnp.sum(
        jnp.where(
            found_page, jnp.arange(table_all.shape[0], dtype=jnp.int32)[None, :] // block_count, 0
        ),
        axis=1,
    )
    take_pick = (anchor[:, None] == shard_ids[None, :]).astype(jnp.bfloat16)
    kv_pages = jnp.einsum(
        "qs,sgpc->qgpc", take_pick, incoming, preferred_element_type=jnp.float32
    ).astype(jnp.bfloat16)
    return (mixed, kv_pages)


def solution(mesh):
    return jax.shard_map(
        local,
        mesh=mesh,
        in_specs=(
            P("wide", "narrow"),
            P("wide"),
            P("wide"),
            P("narrow"),
            P("narrow"),
            P("wide", "narrow"),
            P("wide", "narrow"),
            P("wide", "narrow"),
            P("narrow", "wide"),
        ),
        out_specs=(P("wide", "narrow"), P("wide", "narrow", None, None)),
        check_vma=False,
    )
```

```python
import functools
import math

import jax
import jax.numpy as jnp
from jax import lax
from jax.experimental import pallas as pl
from jax.experimental.pallas import tpu as pltpu
from jax.sharding import PartitionSpec as P

D = 4608
HD = 128
WINDOW = 4096
SEGS = 8

SOFT_CAP = 50.0
QUERY_SCALE = 1.0 / 12.0
NORM_EPSILON = 1e-06
NX, NY, NZ = 4, 4, 4
MESH = pl.DeviceIdType.MESH
PRE = QUERY_SCALE / SOFT_CAP
POST = SOFT_CAP * math.log2(math.e)


def gather_kernel(
    tok_ref, w_ref, meta_ref, gain_ref,
    tok_all, w_all, meta_all, gain_all,
    w_send, w_recv, z_send, z_recv, c_send, c_recv, m_send, m_recv, g_send, g_recv, own_sem,
):
    wide = lax.axis_index("wide")
    narrow = lax.axis_index("narrow")
    x, y = lax.div(wide, NY), lax.rem(wide, NY)
    z, core = lax.div(narrow, 2), lax.rem(narrow, 2)
    shard = w_ref.shape[0]
    half = shard // 2
    cols = w_ref.shape[1] // 2
    rows = tok_ref.shape[0]

    def ring(position, count, step):
        return lax.rem(position + step + count, count)

    def at_wide(x_new, y_new):
        return {"wide": x_new * NY + y_new}

    def remote(src, dst, send, recv, where):
        return pltpu.make_async_remote_copy(
            src_ref=src, dst_ref=dst, send_sem=send, recv_sem=recv,
            device_id=where, device_id_type=MESH,
        )

    def peer(part, stage, step):
        if (part == 0) == (stage == 0):
            return at_wide(ring(x, NX, step), y)
        return at_wide(x, ring(y, NY, step))

    def block(part, along, across):
        if part == 0:
            return ring(x, NX, along) * NY + ring(y, NY, across)
        return ring(x, NX, across) * NY + ring(y, NY, along)

    def rows_of(part, along, across):
        return pl.ds(block(part, along, across) * shard + part * half, half)

    def send(part, group, kind, along, across, own=False):
        stage = 0 if group == 0 else 1
        where = peer(part, stage, 1 if kind % 2 == 0 else -1)
        there = rows_of(part, along, across)
        if kind < 2:
            span = slice(None)
        else:
            span = pl.ds((kind - 2) * cols, cols)
        if own:
            src = w_ref.at[pl.ds(part * half, half), span]
        else:
            src = w_all.at[there, span]
        return remote(
            src, w_all.at[there, span],
            w_send.at[part, group, kind], w_recv.at[part, group, kind], where,
        )

    started = []

    def start(copy):
        copy.start()
        started.append(copy)
        return copy

    sent = {}

    def go(part, group, kind, along, across, own=False):
        sent[part, group, kind] = start(send(part, group, kind, along, across, own))

    toks = {}

    def zgo(kind, index, src, span):
        where = {"narrow": ring(z, NZ, 1 if kind % 2 == 0 else -1) * 2 + core}
        toks[kind] = start(remote(src, tok_all.at[index, span], z_send.at[kind], z_recv.at[kind], where))

    pair = {}

    def cgo(kind, index, src, span):
        where = {"narrow": z * 2 + (1 - core)}
        pair[kind] = start(remote(src, tok_all.at[index, span], c_send.at[kind], c_recv.at[kind], where))

    every = pl.ds(0, rows)
    low, high = pl.ds(0, rows // 2), pl.ds(rows // 2, rows // 2)

    def zblock(step):
        return ring(z, NZ, step) * 2 + core

    small = []
    for other in range(1, NX * NY):
        target = lax.rem(wide + other, NX * NY)
        small.append(start(remote(
            meta_ref, meta_all.at[wide], m_send.at[other], m_recv.at[other], {"wide": target})))
    for other in range(1, NZ * 2):
        target = lax.rem(narrow + other, NZ * 2)
        small.append(start(remote(
            gain_ref, gain_all.at[narrow], g_send.at[other], g_recv.at[other], {"narrow": target})))

    for part in (0, 1):
        go(part, 0, 0, 0, 0, True)
        go(part, 0, 1, 0, 0, True)
    zgo(0, narrow, tok_ref, every)
    zgo(1, narrow, tok_ref, every)
    cgo(0, narrow, tok_ref, every)
    for part in (0, 1):
        go(part, 1, 0, 0, 0, True)
        go(part, 1, 1, 0, 0, True)
    local = [
        pltpu.make_async_copy(w_ref, w_all.at[pl.ds(wide * shard, shard)], own_sem.at[0]),
        pltpu.make_async_copy(tok_ref, tok_all.at[narrow], own_sem.at[1]),
        pltpu.make_async_copy(meta_ref, meta_all.at[wide], own_sem.at[2]),
        pltpu.make_async_copy(gain_ref, gain_all.at[narrow], own_sem.at[3]),
    ]
    for copy in local:
        copy.start()

    for part in (0, 1):
        sent[part, 0, 0].wait_recv()
        go(part, 0, 2, -1, 0)
        go(part, 2, 0, -1, 0)
        go(part, 2, 1, -1, 0)
    for part in (0, 1):
        sent[part, 0, 1].wait_recv()
        go(part, 0, 3, 1, 0)
        go(part, 3, 0, 1, 0)
        go(part, 3, 1, 1, 0)

    toks[0].wait_recv()
    zgo(2, zblock(-1), tok_all.at[zblock(-1), low], low)
    cgo(1, zblock(-1), tok_all.at[zblock(-1)], every)
    toks[1].wait_recv()
    zgo(3, zblock(1), tok_all.at[zblock(1), high], high)
    cgo(2, zblock(1), tok_all.at[zblock(1)], every)

    for part in (0, 1):
        sent[part, 1, 0].wait_recv()
        go(part, 1, 2, 0, -1)
        sent[part, 1, 1].wait_recv()
        go(part, 1, 3, 0, 1)
    for part in (0, 1):
        sent[part, 0, 2].wait_recv()
        sent[part, 0, 3].wait_recv()
        go(part, 4, 0, 2, 0)
        go(part, 4, 1, 2, 0)
    for group, along in ((2, -1), (3, 1)):
        for part in (0, 1):
            sent[part, group, 0].wait_recv()
            go(part, group, 2, along, -1)
            sent[part, group, 1].wait_recv()
            go(part, group, 3, along, 1)
    toks[2].wait_recv()
    cgo(3, zblock(2), tok_all.at[zblock(2), low], low)
    toks[3].wait_recv()
    cgo(4, zblock(2), tok_all.at[zblock(2), high], high)
    for part in (0, 1):
        sent[part, 4, 0].wait_recv()
        go(part, 4, 2, 2, -1)
        sent[part, 4, 1].wait_recv()
        go(part, 4, 3, 2, 1)

    for part in (0, 1):
        for group in range(1, 5):
            sent[part, group, 2].wait_recv()
            sent[part, group, 3].wait_recv()
    for kind in range(5):
        pair[kind].wait_recv()
    for copy in small:
        copy.wait_recv()
    for copy in local:
        copy.wait()
    for copy in started:
        copy.wait_send()


def gather_all(tokens, weights, meta, gain):
    rows, width = tokens.shape
    shard, columns = weights.shape
    any_spec = pl.BlockSpec(memory_space=pl.ANY)
    vmem_spec = pl.BlockSpec(memory_space=pltpu.VMEM)
    dma = pltpu.SemaphoreType.DMA
    return pl.pallas_call(
        gather_kernel,
        out_shape=(
            jax.ShapeDtypeStruct((8, rows, width), tokens.dtype),
            jax.ShapeDtypeStruct((16 * shard, columns), weights.dtype),
            jax.ShapeDtypeStruct((16,) + meta.shape, meta.dtype),
            jax.ShapeDtypeStruct((8,) + gain.shape, gain.dtype),
        ),
        in_specs=[vmem_spec] * 4,
        out_specs=(any_spec,) * 4,
        scratch_shapes=[
            dma((2, 5, 4)), dma((2, 5, 4)), dma((4,)), dma((4,)), dma((5,)), dma((5,)),
            dma((16,)), dma((16,)), dma((8,)), dma((8,)), dma((4,)),
        ],
        compiler_params=pltpu.CompilerParams(has_side_effects=True),
        name="gather_all",
    )(tokens, weights, meta, gain)


QB = 256
REACH = 4


def lanes(start, size):
    return pl.ds(pl.multiple_of(start, 128), size)


def attention_kernel(
    tok_hbm, w_hbm, gain_ref, cos_ref, sin_ref, floor_ref,
    out_ref, kv_hbm,
    tok, w, query_all, held, total, tok_sem, w_sem, kv_sem, send, recv,
):
    parts, tokens, width = tok.shape
    blocks = tokens // QB
    half = w.shape[1] // 2
    wide = lax.axis_index("wide")
    count = NX * NY

    def block_rows(b):
        return pl.ds(pl.multiple_of(b * QB, QB), QB)

    def load_tok(b):
        return pltpu.make_async_copy(
            tok_hbm.at[:, block_rows(b), :], tok.at[:, block_rows(b), :], tok_sem.at[b]
        )

    loads_w = [
        pltpu.make_async_copy(
            w_hbm.at[:, pl.ds(part * half, half)], w.at[:, pl.ds(part * half, half)], w_sem.at[part]
        )
        for part in range(2)
    ]
    load_tok(0).start()
    loads_w[0].start()
    for b in range(1, blocks):
        load_tok(b).start()
    loads_w[1].start()

    def rotated(value, rows):
        return value * cos_ref[rows, :] + pltpu.roll(value, HD // 2, 1) * sin_ref[rows, :]

    loads_w[0].wait()

    def key_block(b, carry):
        load_tok(b).wait()
        rows = block_rows(b)
        squares = jnp.zeros((QB, 1), jnp.float32)
        for n in range(parts):
            piece = tok[n, rows, :].astype(jnp.float32)
            squares += jnp.sum(piece * piece, axis=1, keepdims=True)
        scale = lax.rsqrt(squares / D + NORM_EPSILON)
        product = jnp.zeros((QB, half), jnp.float32)
        for n in range(parts):
            piece = tok[n, rows, :].astype(jnp.float32)
            normed = (piece * scale * gain_ref[n, 0:1, :].astype(jnp.float32)).astype(jnp.bfloat16)
            tok[n, rows, :] = normed
            product += jnp.dot(
                normed, w[pl.ds(n * width, width), 0:half], preferred_element_type=jnp.float32
            )
        for g in range(2):
            key = product[:, g * 256 : g * 256 + HD]
            held[0, rows, g * 256 : g * 256 + HD] = rotated(key, rows).astype(jnp.bfloat16)
            held[0, rows, g * 256 + HD : g * 256 + 256] = product[
                :, g * 256 + HD : g * 256 + 256
            ].astype(jnp.bfloat16)
        return carry

    lax.fori_loop(0, blocks, key_block, 0)
    save = pltpu.make_async_copy(held.at[0], kv_hbm, kv_sem)
    save.start()
    x, y = lax.div(wide, NY), lax.rem(wide, NY)
    next_x = lax.rem(x + 1, NX) * NY + y
    next_y = x * NY + lax.rem(y + 1, NY)
    last_y = x * NY + lax.rem(y + NY - 1, NY)
    inner = (y == 1) | (y == 2)

    def move(kind, source, slot, where, c):
        rows = block_rows(c)
        return pltpu.make_async_remote_copy(
            src_ref=held.at[source, rows], dst_ref=held.at[slot, rows],
            send_sem=send.at[kind, c], recv_sem=recv.at[slot, c],
            device_id={"wide": where}, device_id_type=MESH,
        )

    def along_x(c):
        return move(0, 0, 4, next_x, c)

    def up(source, c):
        return move(1, source, 1, next_y, c)

    def down(source, c):
        return move(2, source, 3, last_y, c)

    def pass_up(c):
        return move(3, 1, 2, next_y, c)

    def pass_down(c):
        return move(4, 3, 2, last_y, c)

    def begin(c, carry):
        along_x(c).start()

        @pl.when(y < NY - 1)
        def _():
            up(0, c).start()

        @pl.when(y == 0)
        def _():
            down(0, c).start()

        return carry

    lax.fori_loop(0, blocks, begin, 0)
    loads_w[1].wait()

    def query_block(b, carry):
        rows = block_rows(b)
        product = jnp.zeros((QB, half), jnp.float32)
        for n in range(parts):
            product += jnp.dot(
                tok[n, rows, :], w[pl.ds(n * width, width), half : 2 * half],
                preferred_element_type=jnp.float32,
            )
        for h in range(half // HD):
            value = product[:, h * HD : (h + 1) * HD]
            query_all[rows, h * HD : (h + 1) * HD] = rotated(value, rows).astype(jnp.bfloat16)
        return carry

    lax.fori_loop(0, blocks, query_block, 0)

    def chunk(d, g, qb, first, size, diagonal=False, fresh=False):
        qrows = block_rows(qb)
        krows = pl.ds(pl.multiple_of(first, 256), size)
        query = jnp.concatenate(
            [query_all[qrows, lanes(g * 256, 128)], query_all[qrows, lanes(g * 256 + 128, 128)]],
            axis=0,
        )
        keys = held[d, krows, lanes(g * 256, 128)]
        values = held[d, krows, lanes(g * 256 + 128, 128)]
        scores = lax.dot_general(
            query, keys, (((1,), (1,)), ((), ())), preferred_element_type=jnp.float32
        )
        floor = floor_ref[qrows, :] - ((REACH - d) * tokens + first)
        floor = jnp.concatenate([floor] * (size // 128), axis=1)
        column = lax.broadcasted_iota(jnp.int32, (QB, size), 1)
        allowed = column >= floor
        if diagonal:
            allowed = allowed & (column <= lax.broadcasted_iota(jnp.int32, (QB, size), 0))
        weights = jnp.exp2(jnp.tanh(scores * PRE) * POST)
        weights = jnp.concatenate(
            [
                jnp.where(allowed, weights[:QB], 0.0).astype(jnp.bfloat16),
                jnp.where(allowed, weights[QB:], 0.0).astype(jnp.bfloat16),
            ],
            axis=0,
        )
        wide_values = jnp.concatenate([values, jnp.ones_like(values)], axis=1)
        product = jnp.dot(weights, wide_values, preferred_element_type=jnp.float32)
        slot = g * blocks + qb
        if fresh:
            total[slot] = product
        else:
            total[slot] += product

    def own_pair(t, carry):
        g, qb = lax.div(t, blocks), lax.rem(t, blocks)
        chunk(0, g, qb, qb * QB, QB, diagonal=True, fresh=True)
        lax.fori_loop(0, qb, lambda k, c: (chunk(0, g, qb, k * QB, QB), c)[1], 0)
        return carry

    def segment(d, k, pairs):
        def pair(t, carry):
            chunk(d, lax.rem(t, 2), lax.div(t, 2), k * QB, QB)
            return carry

        lax.fori_loop(0, pairs, pair, 0)

    lax.fori_loop(0, 2 * blocks, own_pair, 0)

    def step(i, carry):
        @pl.when(i < blocks)
        def _():
            along_x(i).wait_recv()

            @pl.when(y == NY - 1)
            def _():
                up(4, i).start()

            @pl.when(y > 0)
            def _():
                down(4, i).start()

            up(0, i).wait_recv()

            @pl.when(inner)
            def _():
                pass_up(i).start()

            segment(4, i, 2 * (i + 1))
            segment(1, i, 2 * blocks)

        @pl.when((i >= 1) & (i < blocks + 1))
        def _():
            down(0, i - 1).wait_recv()

            @pl.when(inner)
            def _():
                pass_down(i - 1).start()

            segment(3, i - 1, 2 * blocks)

        @pl.when(i >= 2)
        def _():
            pass_up(i - 2).wait_recv()
            segment(2, i - 2, 2 * blocks)

        return carry

    lax.fori_loop(0, blocks + 2, step, 0)

    def finish(t, carry):
        g, qb = lax.div(t, blocks), lax.rem(t, blocks)
        slot = g * blocks + qb
        result = (total[slot, :, :HD] / total[slot, :, HD:]).astype(out_ref.dtype)
        out_ref[block_rows(qb), lanes(g * 256, 128)] = result[:QB]
        out_ref[block_rows(qb), lanes(g * 256 + 128, 128)] = result[QB:]
        return carry

    lax.fori_loop(0, 2 * blocks, finish, 0)
    save.wait()

    def drain(c, carry):
        along_x(c).wait_send()
        up(0, c).wait_send()
        down(0, c).wait_send()

        @pl.when(inner)
        def _():
            pass_up(c).wait_send()
            pass_down(c).wait_send()

        return carry

    lax.fori_loop(0, blocks, drain, 0)


def attention(tok_all, w_all, gain, cosine, sine, floor):
    parts, tokens, width = tok_all.shape
    half = w_all.shape[1] // 3
    vmem_spec = pl.BlockSpec(memory_space=pltpu.VMEM)
    any_spec = pl.BlockSpec(memory_space=pl.ANY)
    dma = pltpu.SemaphoreType.DMA
    return pl.pallas_call(
        attention_kernel,
        out_shape=(
            jax.ShapeDtypeStruct((tokens, half), jnp.bfloat16),
            jax.ShapeDtypeStruct((tokens, half), jnp.bfloat16),
        ),
        in_specs=[any_spec] * 2 + [vmem_spec] * 4,
        out_specs=(vmem_spec, any_spec),
        scratch_shapes=[
            pltpu.VMEM(tok_all.shape, jnp.bfloat16),
            pltpu.VMEM((w_all.shape[0], 2 * half), jnp.bfloat16),
            pltpu.VMEM((tokens, half), jnp.bfloat16),
            pltpu.VMEM((REACH + 1, tokens, half), jnp.bfloat16),
            pltpu.VMEM((8, 2 * QB, 256), jnp.float32),
            dma((tokens // QB,)), dma((2,)), dma, dma((5, tokens // QB)),
            dma((REACH + 1, tokens // QB)),
        ],
        cost_estimate=pl.CostEstimate(
            flops=4 * tokens * 4352 * 128 * 8, bytes_accessed=32 << 20,
            transcendentals=8 * tokens * 4352,
        ),
        compiler_params=pltpu.CompilerParams(
            vmem_limit_bytes=56 << 20, has_side_effects=True
        ),
        name="attention",
    )(tok_all, w_all, gain, cosine, sine, floor)


def tail_kernel(
    attn_ref, tok_ref, gain_ref, w_hbm, pages_hbm,
    mixed_ref, pages_in,
    w, w_sem, give, take, stage, far, near, kept, squares,
    p_send, p_recv, own_sem, c_send, c_recv, f_send, f_recv, n_send, n_recv, s_send, s_recv,
):
    wide = lax.axis_index("wide")
    narrow = lax.axis_index("narrow")
    z, core = lax.div(narrow, 2), lax.rem(narrow, 2)
    count = NX * NY
    tokens = attn_ref.shape[0]
    mid = tokens // 2
    low, high = pl.ds(0, mid), pl.ds(mid, mid)
    sibling = {"narrow": z * 2 + (1 - core)}

    def at_z(step):
        return lax.rem(z + step + NZ, NZ)

    def remote(src, dst, send, recv, where):
        copy = pltpu.make_async_remote_copy(
            src_ref=src, dst_ref=dst, send_sem=send, recv_sem=recv,
            device_id=where, device_id_type=MESH,
        )
        copy.start()
        return copy

    pages = [
        remote(
            pages_hbm.at[lax.rem(wide + other, count)], pages_in.at[wide],
            p_send.at[other], p_recv.at[other], {"wide": lax.rem(wide + other, count)},
        )
        for other in range(1, count)
    ]
    own = pltpu.make_async_copy(pages_hbm.at[wide], pages_in.at[wide], own_sem)
    own.start()

    steps = (2, 1, -1, 0)
    depth, width = attn_ref.shape[1], tok_ref.shape[1]
    loads = []
    for slot in range(8):
        index = at_z(steps[slot % 4]) * 2 + ((1 - core) if slot < 4 else core)
        source = pl.ds(pl.multiple_of(index * width, width), width)
        loads.append(
            pltpu.make_async_copy(
                w_hbm.at[source, pl.ds(w_hbm.shape[1] - depth, depth)], w.at[slot], w_sem.at[slot]
            )
        )
        loads[-1].start()

    def term(slot, rows):
        return lax.dot_general(
            attn_ref[rows, :], w[slot], (((1,), (1,)), ((), ())),
            preferred_element_type=jnp.float32,
        ).astype(jnp.bfloat16)

    def over_rows(body, first=0, size=tokens):
        def step(b, carry):
            body(pl.ds(pl.multiple_of(first + b * QB, QB), QB))
            return carry

        lax.fori_loop(0, size // QB, step, 0)

    passes = []
    for i in range(4):
        loads[i].wait()

        def fill(rows, i=i):
            give[i, rows, :] = term(i, rows)

        over_rows(fill)
        passes.append(remote(give.at[i], take.at[i], c_send.at[i], c_recv.at[i], sibling))

    def own_sum(i, rows):
        mine = term(4 + i, rows)
        return mine.astype(jnp.float32) + take[i, rows, :].astype(jnp.float32)

    def put(i):
        def body(rows):
            stage[i, rows, :] = own_sum(i, rows).astype(jnp.bfloat16)

        return body

    ahead, behind = {"narrow": at_z(1) * 2 + core}, {"narrow": at_z(-1) * 2 + core}
    for i in range(4, 8):
        loads[i].wait()
    passes[0].wait_recv()
    over_rows(put(0), 0, mid)
    far_up = remote(stage.at[0, low], far.at[0], f_send.at[0], f_recv.at[0], ahead)
    over_rows(put(0), mid, mid)
    far_down = remote(stage.at[0, high], far.at[1], f_send.at[1], f_recv.at[1], behind)
    passes[1].wait_recv()
    over_rows(put(1), mid, mid)
    near_a = remote(stage.at[1, high], near.at[0, high], n_send.at[0], n_recv.at[0], ahead)
    passes[2].wait_recv()
    over_rows(put(2), 0, mid)
    near_b = remote(stage.at[2, low], near.at[1, low], n_send.at[1], n_recv.at[1], behind)

    far_up.wait_recv()

    def with_far_up(rows):
        stage[1, rows, :] = (own_sum(1, rows) + far[0, rows, :].astype(jnp.float32)).astype(
            jnp.bfloat16
        )

    over_rows(with_far_up, 0, mid)
    near_c = remote(stage.at[1, low], near.at[0, low], n_send.at[2], n_recv.at[2], ahead)
    far_down.wait_recv()

    def with_far_down(b, carry):
        rows = pl.ds(pl.multiple_of(mid + b * QB, QB), QB)
        source = pl.ds(pl.multiple_of(b * QB, QB), QB)
        stage[2, rows, :] = (own_sum(2, rows) + far[1, source, :].astype(jnp.float32)).astype(
            jnp.bfloat16
        )
        return carry

    lax.fori_loop(0, mid // QB, with_far_down, 0)
    near_d = remote(stage.at[2, high], near.at[1, high], n_send.at[3], n_recv.at[3], behind)
    passes[3].wait_recv()

    def keep(rows):
        kept[rows, :] = own_sum(3, rows)

    over_rows(keep)
    for copy in (near_a, near_b, near_c, near_d):
        copy.wait_recv()

    ones = jnp.ones((8, tok_ref.shape[1]), jnp.float32)

    def finish(rows):
        value = (
            kept[rows, :]
            + near[0, rows, :].astype(jnp.float32)
            + near[1, rows, :].astype(jnp.float32)
        )
        kept[rows, :] = value
        squares[0, :, rows] = lax.dot_general(
            ones, value * value, (((1,), (1,)), ((), ())),
            precision=lax.Precision.HIGHEST, preferred_element_type=jnp.float32,
        )

    over_rows(finish)
    sums = [
        remote(
            squares.at[0], squares.at[other], s_send.at[other], s_recv.at[other],
            {"narrow": lax.rem(narrow + other, NZ * 2)},
        )
        for other in range(1, NZ * 2)
    ]
    for copy in sums:
        copy.wait_recv()
    pick = jnp.full((8, 128), 0.125, jnp.float32)

    def emit(rows):
        whole = squares[0, :, rows]
        for other in range(1, NZ * 2):
            whole += squares[other, :, rows]
        column = lax.dot_general(
            whole, pick, (((0,), (0,)), ((), ())),
            precision=lax.Precision.HIGHEST, preferred_element_type=jnp.float32,
        )
        scale = lax.rsqrt(column / D + NORM_EPSILON)[:, 0:1]
        mixed_ref[rows, :] = (
            tok_ref[rows, :].astype(jnp.float32)
            + kept[rows, :] * scale * gain_ref[0:1, :].astype(jnp.float32)
        ).astype(jnp.bfloat16)

    over_rows(emit)
    for copy in pages:
        copy.wait_recv()
    own.wait()
    for copy in pages + passes + sums:
        copy.wait_send()
    for copy in (far_up, far_down, near_a, near_b, near_c, near_d):
        copy.wait_send()


def tail(attn, w_all, tokens, post_gain, outgoing):
    rows, width = tokens.shape
    vmem_spec = pl.BlockSpec(memory_space=pltpu.VMEM)
    any_spec = pl.BlockSpec(memory_space=pl.ANY)
    dma = pltpu.SemaphoreType.DMA
    bf16 = jnp.bfloat16
    return pl.pallas_call(
        tail_kernel,
        out_shape=(
            jax.ShapeDtypeStruct(tokens.shape, bf16),
            jax.ShapeDtypeStruct(outgoing.shape, bf16),
        ),
        in_specs=[vmem_spec] * 3 + [any_spec] * 2,
        out_specs=(vmem_spec, any_spec),
        scratch_shapes=[
            pltpu.VMEM((8, width, attn.shape[1]), bf16),
            dma((8,)),
            pltpu.VMEM((4, rows, width), bf16),
            pltpu.VMEM((4, rows, width), bf16),
            pltpu.VMEM((3, rows, width), bf16),
            pltpu.VMEM((2, rows // 2, width), bf16),
            pltpu.VMEM((2, rows, width), bf16),
            pltpu.VMEM((rows, width), jnp.float32),
            pltpu.VMEM((8, 8, rows), jnp.float32),
            dma((16,)), dma((16,)), dma, dma((4,)), dma((4,)), dma((2,)), dma((2,)),
            dma((4,)), dma((4,)), dma((8,)), dma((8,)),
        ],
        cost_estimate=pl.CostEstimate(
            flops=2 * rows * 512 * D, bytes_accessed=24 << 20, transcendentals=0
        ),
        compiler_params=pltpu.CompilerParams(
            vmem_limit_bytes=56 << 20, has_side_effects=True
        ),
        name="tail",
    )(attn, tokens, post_gain, w_all, outgoing)


def local(tokens, segment_ids, page_table, pre_gain, post_gain, w_query, w_key, w_value, w_out):
    tok_w = tokens.shape[0]
    shard_count = lax.axis_size("wide")
    shard_index = lax.axis_index("wide")
    block_count = page_table.shape[0]
    pairs_here = w_key.shape[1] // HD
    seg_rows = segment_ids.reshape(8, tok_w // 8)
    table_row = jnp.pad(page_table[None, :], ((0, 7), (0, tok_w // 8 - block_count)))
    meta = jnp.concatenate([seg_rows, table_row], axis=0)
    gain_in = jnp.pad(pre_gain[None, :], ((0, 15), (0, 0)))
    columns = []
    for g in range(pairs_here):
        columns += [w_key[:, g * HD : (g + 1) * HD], w_value[:, g * HD : (g + 1) * HD]]
    weights = jnp.concatenate(columns + [w_query, jnp.transpose(w_out)], axis=1)
    tok_all, w_all, meta_all, gain_all = gather_all(tokens, weights, meta, gain_in)
    labels = jnp.arange(SEGS, dtype=jnp.int32)
    all_ids = meta_all[:, :8, :].reshape(-1)
    table_all = meta_all[:, 8, :block_count].reshape(-1)
    seg_firsts = jnp.sum((all_ids[:, None] < labels[None, :]).astype(jnp.int32), axis=0)
    member = segment_ids[:, None] == labels[None, :]
    seg_start = jnp.sum(jnp.where(member, seg_firsts[None, :], 0), axis=1)
    first_token = shard_index * tok_w
    token_index = first_token + jnp.arange(tok_w, dtype=jnp.int32)
    positions = token_index - seg_start
    half_width = HD // 2
    inverse_freq = jnp.exp(
        -math.log(10000.0) * 2.0 * jnp.arange(half_width, dtype=jnp.float32) / HD
    )
    angle_table = positions.astype(jnp.float32)[:, None] * inverse_freq[None, :]
    cosine = jnp.cos(angle_table)
    sine = jnp.sin(angle_table)
    cosine = jnp.concatenate([cosine, cosine], axis=1)
    sine = jnp.concatenate([-sine, sine], axis=1)
    key_floor = jnp.maximum(seg_start, token_index - WINDOW + 1) - (first_token - WINDOW)
    floor = jnp.broadcast_to(key_floor[:, None], (tok_w, 128))
    attn_out, flat = attention(tok_all, w_all, gain_all, cosine, sine, floor)

    page_len = tok_w // block_count
    token_blocks = flat.reshape(block_count, page_len, pairs_here, 2 * HD)
    owners = page_table // block_count
    shard_ids = jnp.arange(shard_count, dtype=jnp.int32)
    send_pick = (owners[None, :] == shard_ids[:, None]).astype(jnp.bfloat16)
    outgoing = jnp.einsum(
        "sj,jpgc->sgpc", send_pick, token_blocks, preferred_element_type=jnp.float32
    ).astype(jnp.bfloat16)
    mixed, incoming = tail(
        attn_out, w_all, tokens, jnp.pad(post_gain[None, :], ((0, 15), (0, 0))), outgoing
    )
    my_pages = shard_index * block_count + jnp.arange(block_count, dtype=jnp.int32)
    found_page = table_all[None, :] == my_pages[:, None]
    anchor = jnp.sum(
        jnp.where(
            found_page, jnp.arange(table_all.shape[0], dtype=jnp.int32)[None, :] // block_count, 0
        ),
        axis=1,
    )
    take_pick = (anchor[:, None] == shard_ids[None, :]).astype(jnp.bfloat16)
    kv_pages = jnp.einsum(
        "qs,sgpc->qgpc", take_pick, incoming, preferred_element_type=jnp.float32
    ).astype(jnp.bfloat16)
    return (mixed, kv_pages)


def solution(mesh):
    return jax.shard_map(
        local,
        mesh=mesh,
        in_specs=(
            P("wide", "narrow"),
            P("wide"),
            P("wide"),
            P("narrow"),
            P("narrow"),
            P("wide", "narrow"),
            P("wide", "narrow"),
            P("wide", "narrow"),
            P("narrow", "wide"),
        ),
        out_specs=(P("wide", "narrow"), P("wide", "narrow", None, None)),
        check_vma=False,
    )
```

```python
import functools
import math

import jax
import jax.numpy as jnp
from jax import lax
from jax.experimental import pallas as pl
from jax.experimental.pallas import tpu as pltpu
from jax.sharding import PartitionSpec as P

D = 4608
HD = 128
WINDOW = 4096
SEGS = 8

SOFT_CAP = 50.0
QUERY_SCALE = 1.0 / 12.0
NORM_EPSILON = 1e-06
NX, NY, NZ = 4, 4, 4
MESH = pl.DeviceIdType.MESH
PRE = QUERY_SCALE / SOFT_CAP
POST = SOFT_CAP * math.log2(math.e)


QB = 256
REACH = 4
WAVES = 3


def lanes(start, size):
    return pl.ds(pl.multiple_of(start, 128), size)


def front_kernel(
    tok_ref, w_ref, meta_ref, gain_ref, ids_ref, freq_ref,
    out_ref, kv_hbm, w_out_hbm, meta_out,
    tok, w, meta_all, gain_all, cos_ref, sin_ref, floor_ref, query_all, held, total,
    w_send, w_recv, z_send, z_recv, c_send, c_recv, m_send, m_recv, g_send, g_recv, own_sem,
    out_sem, send, recv,
):
    wide = lax.axis_index("wide")
    narrow = lax.axis_index("narrow")
    x, y = lax.div(wide, NY), lax.rem(wide, NY)
    z, core = lax.div(narrow, 2), lax.rem(narrow, 2)
    shard = w_ref.shape[0]
    part_rows = shard // 2
    half = w_ref.shape[1] // WAVES
    parts, tokens, width = tok.shape
    blocks = tokens // QB

    def block_rows(b):
        return pl.ds(pl.multiple_of(b * QB, QB), QB)

    def ring(position, count, step):
        return lax.rem(position + step + count, count)

    started = []

    def remote(src, dst, send_sem, recv_sem, where):
        copy = pltpu.make_async_remote_copy(
            src_ref=src, dst_ref=dst, send_sem=send_sem, recv_sem=recv_sem,
            device_id=where, device_id_type=MESH,
        )
        copy.start()
        started.append(copy)
        return copy

    def peer(part, stage, step):
        if (part == 0) == (stage == 0):
            return {"wide": ring(x, NX, step) * NY + y}
        return {"wide": x * NY + ring(y, NY, step)}

    def rows_of(part, along, across):
        if part == 0:
            block = ring(x, NX, along) * NY + ring(y, NY, across)
        else:
            block = ring(x, NX, across) * NY + ring(y, NY, along)
        return pl.ds(pl.multiple_of(block * shard + part * part_rows, 16), part_rows)

    sent = {}

    def go(wave, part, group, kind, along, across, own=False):
        where = peer(part, 0 if group == 0 else 1, 1 if kind % 2 == 0 else -1)
        there = rows_of(part, along, across)
        if kind < 2:
            span = pl.ds(wave * half, half)
        else:
            span = pl.ds(wave * half + (kind - 2) * (half // 2), half // 2)
        src = w_ref.at[pl.ds(part * part_rows, part_rows), span] if own else w.at[there, span]
        sent[wave, part, group, kind] = remote(
            src, w.at[there, span],
            w_send.at[wave, part, group, kind], w_recv.at[wave, part, group, kind], where,
        )

    def got(wave, part, group, kind):
        sent[wave, part, group, kind].wait_recv()

    def wave_own(wave):
        for group in (0, 1):
            for part in (0, 1):
                go(wave, part, group, 0, 0, 0, True)
                go(wave, part, group, 1, 0, 0, True)

    def wave_first(wave):
        for kind, along, group in ((0, -1, 2), (1, 1, 3)):
            for part in (0, 1):
                got(wave, part, 0, kind)
                go(wave, part, 0, 2 + kind, along, 0)
                go(wave, part, group, 0, along, 0)
                go(wave, part, group, 1, along, 0)

    def wave_pass(wave, group, along):
        for part in (0, 1):
            got(wave, part, group, 0)
            go(wave, part, group, 2, along, -1)
            got(wave, part, group, 1)
            go(wave, part, group, 3, along, 1)

    def wave_far(wave):
        for part in (0, 1):
            got(wave, part, 0, 2)
            got(wave, part, 0, 3)
            go(wave, part, 4, 0, 2, 0)
            go(wave, part, 4, 1, 2, 0)

    def wave_end(wave):
        for group in range(1, 5):
            for part in (0, 1):
                got(wave, part, group, 2)
                got(wave, part, group, 3)

    toks = {}

    def zgo(kind, index, src, span):
        where = {"narrow": ring(z, NZ, 1 if kind % 2 == 0 else -1) * 2 + core}
        toks[kind] = remote(src, tok.at[index, span], z_send.at[kind], z_recv.at[kind], where)

    pair = {}

    def cgo(kind, index, src, span):
        where = {"narrow": z * 2 + (1 - core)}
        pair[kind] = remote(src, tok.at[index, span], c_send.at[kind], c_recv.at[kind], where)

    every = pl.ds(0, tokens)
    low, high = pl.ds(0, tokens // 2), pl.ds(tokens // 2, tokens // 2)

    def zblock(step):
        return ring(z, NZ, step) * 2 + core

    small = []
    for other in range(1, NX * NY):
        target = lax.rem(wide + other, NX * NY)
        small.append(remote(
            meta_ref, meta_all.at[wide], m_send.at[other], m_recv.at[other], {"wide": target}))
    for other in range(1, NZ * 2):
        target = lax.rem(narrow + other, NZ * 2)
        small.append(remote(
            gain_ref, gain_all.at[narrow], g_send.at[other], g_recv.at[other], {"narrow": target}))
    wave_own(0)
    zgo(0, narrow, tok_ref, every)
    zgo(1, narrow, tok_ref, every)
    cgo(0, narrow, tok_ref, every)
    local = [
        pltpu.make_async_copy(w_ref, w.at[pl.ds(wide * shard, shard)], own_sem.at[0]),
        pltpu.make_async_copy(tok_ref, tok.at[narrow], own_sem.at[1]),
        pltpu.make_async_copy(meta_ref, meta_all.at[wide], own_sem.at[2]),
        pltpu.make_async_copy(gain_ref, gain_all.at[narrow], own_sem.at[3]),
    ]
    for copy in local:
        copy.start()
    wave_first(0)

    for copy in small:
        copy.wait_recv()
    for copy in local:
        copy.wait()
    save_meta = pltpu.make_async_copy(meta_all, meta_out, out_sem.at[2])
    save_meta.start()
    first_token = wide * tokens
    all_ids = meta_all[:, 0:8, :]
    firsts = [
        jnp.sum((all_ids < label).astype(jnp.float32)).astype(jnp.int32)
        for label in range(1, SEGS)
    ]

    def tables(b, carry):
        rows = block_rows(b)
        ids = ids_ref[rows, :]
        start = jnp.zeros((QB, 128), jnp.int32)
        for label in range(1, SEGS):
            start = jnp.where(ids == label, firsts[label - 1], start)
        index = first_token + b * QB + lax.broadcasted_iota(jnp.int32, (QB, 128), 0)
        angle = (index - start).astype(jnp.float32) * freq_ref[0:1, :]
        cos_ref[rows, :] = jnp.cos(angle)
        sin_ref[rows, :] = jnp.sin(angle) * freq_ref[1:2, :]
        floor_ref[rows, :] = jnp.maximum(start, index - WINDOW + 1) - (first_token - WINDOW)
        return carry

    wave_pass(0, 1, 0)
    wave_far(0)
    toks[0].wait_recv()
    zgo(2, zblock(-1), tok.at[zblock(-1), low], low)
    cgo(1, zblock(-1), tok.at[zblock(-1)], every)
    toks[1].wait_recv()
    zgo(3, zblock(1), tok.at[zblock(1), high], high)
    cgo(2, zblock(1), tok.at[zblock(1)], every)
    wave_own(1)
    lax.fori_loop(0, blocks, tables, 0)
    wave_pass(0, 2, -1)
    wave_pass(0, 3, 1)
    wave_pass(0, 4, 2)
    wave_first(1)
    toks[2].wait_recv()
    cgo(3, zblock(2), tok.at[zblock(2), low], low)
    toks[3].wait_recv()
    cgo(4, zblock(2), tok.at[zblock(2), high], high)
    wave_pass(1, 1, 0)
    wave_far(1)
    wave_end(0)
    for kind in range(5):
        pair[kind].wait_recv()
    for kind in range(5):
        pair[kind].wait_send()
    for kind in range(4):
        toks[kind].wait_send()
    done = [id(copy) for copy in list(pair.values()) + list(toks.values())]
    started[:] = [copy for copy in started if id(copy) not in done]

    def rotated(value, rows):
        return value * cos_ref[rows, :] + pltpu.roll(value, HD // 2, 1) * sin_ref[rows, :]

    def key_block(b, carry):
        rows = block_rows(b)
        squares = jnp.zeros((QB, 1), jnp.float32)
        for n in range(parts):
            piece = tok[n, rows, :].astype(jnp.float32)
            squares += jnp.sum(piece * piece, axis=1, keepdims=True)
        scale = lax.rsqrt(squares / D + NORM_EPSILON)
        product = jnp.zeros((QB, half), jnp.float32)
        for n in range(parts):
            piece = tok[n, rows, :].astype(jnp.float32)
            normed = (piece * scale * gain_all[n, 0:1, :].astype(jnp.float32)).astype(jnp.bfloat16)
            tok[n, rows, :] = normed
            product += jnp.dot(
                normed, w[pl.ds(n * width, width), 0:half], preferred_element_type=jnp.float32
            )
        for g in range(2):
            key = product[:, g * 256 : g * 256 + HD]
            held[0, rows, g * 256 : g * 256 + HD] = rotated(key, rows).astype(jnp.bfloat16)
            held[0, rows, g * 256 + HD : g * 256 + 256] = product[
                :, g * 256 + HD : g * 256 + 256
            ].astype(jnp.bfloat16)
        return carry

    def query_block(b, carry):
        rows = block_rows(b)
        product = jnp.zeros((QB, half), jnp.float32)
        for n in range(parts):
            product += jnp.dot(
                tok[n, rows, :], w[pl.ds(n * width, width), half : 2 * half],
                preferred_element_type=jnp.float32,
            )
        for h in range(half // HD):
            value = product[:, h * HD : (h + 1) * HD]
            query_all[rows, h * HD : (h + 1) * HD] = rotated(value, rows).astype(jnp.bfloat16)
        return carry

    next_x = lax.rem(x + 1, NX) * NY + y
    next_y = x * NY + lax.rem(y + 1, NY)
    last_y = x * NY + lax.rem(y + NY - 1, NY)
    inner = (y == 1) | (y == 2)

    def move(kind, source, slot, where, c):
        rows = block_rows(c)
        return pltpu.make_async_remote_copy(
            src_ref=held.at[source, rows], dst_ref=held.at[slot, rows],
            send_sem=send.at[kind, c], recv_sem=recv.at[slot, c],
            device_id={"wide": where}, device_id_type=MESH,
        )

    def along_x(c):
        return move(0, 0, 4, next_x, c)

    def up(source, c):
        return move(1, source, 1, next_y, c)

    def down(source, c):
        return move(2, source, 3, last_y, c)

    def pass_up(c):
        return move(3, 1, 2, next_y, c)

    def pass_down(c):
        return move(4, 3, 2, last_y, c)

    def begin(c, carry):
        along_x(c).start()

        @pl.when(y < NY - 1)
        def _():
            up(0, c).start()

        @pl.when(y == 0)
        def _():
            down(0, c).start()

        return carry

    def chunk(d, g, qb, first, size, diagonal=False, fresh=False):
        qrows = block_rows(qb)
        krows = pl.ds(pl.multiple_of(first, 256), size)
        query = jnp.concatenate(
            [query_all[qrows, lanes(g * 256, 128)], query_all[qrows, lanes(g * 256 + 128, 128)]],
            axis=0,
        )
        keys = held[d, krows, lanes(g * 256, 128)]
        values = held[d, krows, lanes(g * 256 + 128, 128)]
        scores = lax.dot_general(
            query, keys, (((1,), (1,)), ((), ())), preferred_element_type=jnp.float32
        )
        floor = floor_ref[qrows, :] - ((REACH - d) * tokens + first)
        floor = jnp.concatenate([floor] * (size // 128), axis=1)
        column = lax.broadcasted_iota(jnp.int32, (QB, size), 1)
        allowed = column >= floor
        if diagonal:
            allowed = allowed & (column <= lax.broadcasted_iota(jnp.int32, (QB, size), 0))
        weights = jnp.exp2(jnp.tanh(scores * PRE) * POST)
        weights = jnp.concatenate(
            [
                jnp.where(allowed, weights[:QB], 0.0).astype(jnp.bfloat16),
                jnp.where(allowed, weights[QB:], 0.0).astype(jnp.bfloat16),
            ],
            axis=0,
        )
        wide_values = jnp.concatenate([values, jnp.ones_like(values)], axis=1)
        product = jnp.dot(weights, wide_values, preferred_element_type=jnp.float32)
        slot = g * blocks + qb
        if fresh:
            total[slot] = product
        else:
            total[slot] += product

    def own_pair(t, carry):
        g, qb = lax.div(t, blocks), lax.rem(t, blocks)
        chunk(0, g, qb, qb * QB, QB, diagonal=True, fresh=True)
        lax.fori_loop(0, qb, lambda k, c: (chunk(0, g, qb, k * QB, QB), c)[1], 0)
        return carry

    def segment(d, k, pairs):
        def pair(t, carry):
            chunk(d, lax.rem(t, 2), lax.div(t, 2), k * QB, QB)
            return carry

        lax.fori_loop(0, pairs, pair, 0)

    wave_own(2)
    lax.fori_loop(0, 2, key_block, 0)
    wave_pass(1, 2, -1)
    wave_pass(1, 3, 1)
    wave_pass(1, 4, 2)
    wave_first(2)
    lax.fori_loop(2, blocks, key_block, 0)
    wave_pass(2, 1, 0)
    wave_far(2)
    save = pltpu.make_async_copy(held.at[0], kv_hbm, out_sem.at[0])
    save.start()
    wave_end(1)
    lax.fori_loop(0, 2, query_block, 0)
    wave_pass(2, 2, -1)
    wave_pass(2, 3, 1)
    lax.fori_loop(2, blocks, query_block, 0)
    wave_pass(2, 4, 2)
    lax.fori_loop(0, blocks, begin, 0)
    lax.fori_loop(0, 2 * blocks, own_pair, 0)

    def step(i, carry):
        @pl.when(i < blocks)
        def _():
            along_x(i).wait_recv()

            @pl.when(y == NY - 1)
            def _():
                up(4, i).start()

            @pl.when(y > 0)
            def _():
                down(4, i).start()

            up(0, i).wait_recv()

            @pl.when(inner)
            def _():
                pass_up(i).start()

            segment(4, i, 2 * (i + 1))
            segment(1, i, 2 * blocks)

        @pl.when((i >= 1) & (i < blocks + 1))
        def _():
            down(0, i - 1).wait_recv()

            @pl.when(inner)
            def _():
                pass_down(i - 1).start()

            segment(3, i - 1, 2 * blocks)

        @pl.when(i >= 2)
        def _():
            pass_up(i - 2).wait_recv()
            segment(2, i - 2, 2 * blocks)

        return carry

    lax.fori_loop(0, blocks + 2, step, 0)

    def finish(t, carry):
        g, qb = lax.div(t, blocks), lax.rem(t, blocks)
        slot = g * blocks + qb
        result = (total[slot, :, :HD] / total[slot, :, HD:]).astype(out_ref.dtype)
        out_ref[block_rows(qb), lanes(g * 256, 128)] = result[:QB]
        out_ref[block_rows(qb), lanes(g * 256 + 128, 128)] = result[QB:]
        return carry

    lax.fori_loop(0, 2 * blocks, finish, 0)
    wave_end(2)
    save_w = pltpu.make_async_copy(w.at[:, pl.ds(2 * half, half)], w_out_hbm, out_sem.at[1])
    save_w.start()
    save.wait()
    save_meta.wait()

    def drain(c, carry):
        along_x(c).wait_send()
        up(0, c).wait_send()
        down(0, c).wait_send()

        @pl.when(inner)
        def _():
            pass_up(c).wait_send()
            pass_down(c).wait_send()

        return carry

    lax.fori_loop(0, blocks, drain, 0)
    for copy in started:
        copy.wait_send()
    save_w.wait()


def front(tokens, weights, meta, gain, ids, freq):
    rows, width = tokens.shape
    shard, columns = weights.shape
    half = columns // WAVES
    vmem_spec = pl.BlockSpec(memory_space=pltpu.VMEM)
    any_spec = pl.BlockSpec(memory_space=pl.ANY)
    dma = pltpu.SemaphoreType.DMA
    bf16 = jnp.bfloat16
    blocks = rows // QB
    return pl.pallas_call(
        front_kernel,
        out_shape=(
            jax.ShapeDtypeStruct((rows, half), bf16),
            jax.ShapeDtypeStruct((rows, half), bf16),
            jax.ShapeDtypeStruct((16 * shard, half), bf16),
            jax.ShapeDtypeStruct((16,) + meta.shape, meta.dtype),
        ),
        in_specs=[vmem_spec] * 6,
        out_specs=(vmem_spec, any_spec, any_spec, any_spec),
        scratch_shapes=[
            pltpu.VMEM((8, rows, width), bf16),
            pltpu.VMEM((16 * shard, columns), bf16),
            pltpu.VMEM((16,) + meta.shape, jnp.int32),
            pltpu.VMEM((8,) + gain.shape, bf16),
            pltpu.VMEM((rows, 128), jnp.float32),
            pltpu.VMEM((rows, 128), jnp.float32),
            pltpu.VMEM((rows, 128), jnp.int32),
            pltpu.VMEM((rows, half), bf16),
            pltpu.VMEM((REACH + 1, rows, half), bf16),
            pltpu.VMEM((8, 2 * QB, 256), jnp.float32),
            dma((3, 2, 5, 4)), dma((3, 2, 5, 4)), dma((4,)), dma((4,)), dma((5,)), dma((5,)),
            dma((16,)), dma((16,)), dma((8,)), dma((8,)), dma((4,)),
            dma((3,)), dma((5, blocks)), dma((REACH + 1, blocks)),
        ],
        cost_estimate=pl.CostEstimate(
            flops=4 * rows * 4352 * 128 * 8, bytes_accessed=32 << 20,
            transcendentals=8 * rows * 4352,
        ),
        compiler_params=pltpu.CompilerParams(
            vmem_limit_bytes=60 << 20, has_side_effects=True
        ),
        name="front",
    )(tokens, weights, meta, gain, ids, freq)


def tail_kernel(
    attn_ref, tok_ref, gain_ref, w_hbm, pages_hbm,
    mixed_ref, pages_in,
    w, w_sem, give, take, stage, far, near, kept, squares,
    p_send, p_recv, own_sem, c_send, c_recv, f_send, f_recv, n_send, n_recv, s_send, s_recv,
):
    wide = lax.axis_index("wide")
    narrow = lax.axis_index("narrow")
    z, core = lax.div(narrow, 2), lax.rem(narrow, 2)
    count = NX * NY
    tokens = attn_ref.shape[0]
    mid = tokens // 2
    low, high = pl.ds(0, mid), pl.ds(mid, mid)
    sibling = {"narrow": z * 2 + (1 - core)}

    def at_z(step):
        return lax.rem(z + step + NZ, NZ)

    def remote(src, dst, send, recv, where):
        copy = pltpu.make_async_remote_copy(
            src_ref=src, dst_ref=dst, send_sem=send, recv_sem=recv,
            device_id=where, device_id_type=MESH,
        )
        copy.start()
        return copy

    pages = [
        remote(
            pages_hbm.at[lax.rem(wide + other, count)], pages_in.at[wide],
            p_send.at[other], p_recv.at[other], {"wide": lax.rem(wide + other, count)},
        )
        for other in range(1, count)
    ]
    own = pltpu.make_async_copy(pages_hbm.at[wide], pages_in.at[wide], own_sem)
    own.start()

    steps = (2, 1, -1, 0)
    depth, width = attn_ref.shape[1], tok_ref.shape[1]
    loads = []
    for slot in range(8):
        index = at_z(steps[slot % 4]) * 2 + ((1 - core) if slot < 4 else core)
        source = pl.ds(pl.multiple_of(index * width, width), width)
        loads.append(
            pltpu.make_async_copy(
                w_hbm.at[source, pl.ds(w_hbm.shape[1] - depth, depth)], w.at[slot], w_sem.at[slot]
            )
        )
        loads[-1].start()

    def term(slot, rows):
        return lax.dot_general(
            attn_ref[rows, :], w[slot], (((1,), (1,)), ((), ())),
            preferred_element_type=jnp.float32,
        ).astype(jnp.bfloat16)

    def over_rows(body, first=0, size=tokens):
        def step(b, carry):
            body(pl.ds(pl.multiple_of(first + b * QB, QB), QB))
            return carry

        lax.fori_loop(0, size // QB, step, 0)

    passes = []
    for i in range(4):
        loads[i].wait()

        def fill(rows, i=i):
            give[i, rows, :] = term(i, rows)

        over_rows(fill)
        passes.append(remote(give.at[i], take.at[i], c_send.at[i], c_recv.at[i], sibling))

    def own_sum(i, rows):
        mine = term(4 + i, rows)
        return mine.astype(jnp.float32) + take[i, rows, :].astype(jnp.float32)

    def put(i):
        def body(rows):
            stage[i, rows, :] = own_sum(i, rows).astype(jnp.bfloat16)

        return body

    ahead, behind = {"narrow": at_z(1) * 2 + core}, {"narrow": at_z(-1) * 2 + core}
    for i in range(4, 8):
        loads[i].wait()
    passes[0].wait_recv()
    over_rows(put(0), 0, mid)
    far_up = remote(stage.at[0, low], far.at[0], f_send.at[0], f_recv.at[0], ahead)
    over_rows(put(0), mid, mid)
    far_down = remote(stage.at[0, high], far.at[1], f_send.at[1], f_recv.at[1], behind)
    passes[1].wait_recv()
    over_rows(put(1), mid, mid)
    near_a = remote(stage.at[1, high], near.at[0, high], n_send.at[0], n_recv.at[0], ahead)
    passes[2].wait_recv()
    over_rows(put(2), 0, mid)
    near_b = remote(stage.at[2, low], near.at[1, low], n_send.at[1], n_recv.at[1], behind)

    far_up.wait_recv()

    def with_far_up(rows):
        stage[1, rows, :] = (own_sum(1, rows) + far[0, rows, :].astype(jnp.float32)).astype(
            jnp.bfloat16
        )

    over_rows(with_far_up, 0, mid)
    near_c = remote(stage.at[1, low], near.at[0, low], n_send.at[2], n_recv.at[2], ahead)
    far_down.wait_recv()

    def with_far_down(b, carry):
        rows = pl.ds(pl.multiple_of(mid + b * QB, QB), QB)
        source = pl.ds(pl.multiple_of(b * QB, QB), QB)
        stage[2, rows, :] = (own_sum(2, rows) + far[1, source, :].astype(jnp.float32)).astype(
            jnp.bfloat16
        )
        return carry

    lax.fori_loop(0, mid // QB, with_far_down, 0)
    near_d = remote(stage.at[2, high], near.at[1, high], n_send.at[3], n_recv.at[3], behind)
    passes[3].wait_recv()

    def keep(rows):
        kept[rows, :] = own_sum(3, rows)

    over_rows(keep)
    for copy in (near_a, near_b, near_c, near_d):
        copy.wait_recv()

    ones = jnp.ones((8, tok_ref.shape[1]), jnp.float32)

    def finish(rows):
        value = (
            kept[rows, :]
            + near[0, rows, :].astype(jnp.float32)
            + near[1, rows, :].astype(jnp.float32)
        )
        kept[rows, :] = value
        squares[0, :, rows] = lax.dot_general(
            ones, value * value, (((1,), (1,)), ((), ())),
            precision=lax.Precision.HIGHEST, preferred_element_type=jnp.float32,
        )

    over_rows(finish)
    sums = [
        remote(
            squares.at[0], squares.at[other], s_send.at[other], s_recv.at[other],
            {"narrow": lax.rem(narrow + other, NZ * 2)},
        )
        for other in range(1, NZ * 2)
    ]
    for copy in sums:
        copy.wait_recv()
    pick = jnp.full((8, 128), 0.125, jnp.float32)

    def emit(rows):
        whole = squares[0, :, rows]
        for other in range(1, NZ * 2):
            whole += squares[other, :, rows]
        column = lax.dot_general(
            whole, pick, (((0,), (0,)), ((), ())),
            precision=lax.Precision.HIGHEST, preferred_element_type=jnp.float32,
        )
        scale = lax.rsqrt(column / D + NORM_EPSILON)[:, 0:1]
        mixed_ref[rows, :] = (
            tok_ref[rows, :].astype(jnp.float32)
            + kept[rows, :] * scale * gain_ref[0:1, :].astype(jnp.float32)
        ).astype(jnp.bfloat16)

    over_rows(emit)
    for copy in pages:
        copy.wait_recv()
    own.wait()
    for copy in pages + passes + sums:
        copy.wait_send()
    for copy in (far_up, far_down, near_a, near_b, near_c, near_d):
        copy.wait_send()


def tail(attn, w_all, tokens, post_gain, outgoing):
    rows, width = tokens.shape
    vmem_spec = pl.BlockSpec(memory_space=pltpu.VMEM)
    any_spec = pl.BlockSpec(memory_space=pl.ANY)
    dma = pltpu.SemaphoreType.DMA
    bf16 = jnp.bfloat16
    return pl.pallas_call(
        tail_kernel,
        out_shape=(
            jax.ShapeDtypeStruct(tokens.shape, bf16),
            jax.ShapeDtypeStruct(outgoing.shape, bf16),
        ),
        in_specs=[vmem_spec] * 3 + [any_spec] * 2,
        out_specs=(vmem_spec, any_spec),
        scratch_shapes=[
            pltpu.VMEM((8, width, attn.shape[1]), bf16),
            dma((8,)),
            pltpu.VMEM((4, rows, width), bf16),
            pltpu.VMEM((4, rows, width), bf16),
            pltpu.VMEM((3, rows, width), bf16),
            pltpu.VMEM((2, rows // 2, width), bf16),
            pltpu.VMEM((2, rows, width), bf16),
            pltpu.VMEM((rows, width), jnp.float32),
            pltpu.VMEM((8, 8, rows), jnp.float32),
            dma((16,)), dma((16,)), dma, dma((4,)), dma((4,)), dma((2,)), dma((2,)),
            dma((4,)), dma((4,)), dma((8,)), dma((8,)),
        ],
        cost_estimate=pl.CostEstimate(
            flops=2 * rows * 512 * D, bytes_accessed=24 << 20, transcendentals=0
        ),
        compiler_params=pltpu.CompilerParams(
            vmem_limit_bytes=56 << 20, has_side_effects=True
        ),
        name="tail",
    )(attn, tokens, post_gain, w_all, outgoing)


def local(tokens, segment_ids, page_table, pre_gain, post_gain, w_query, w_key, w_value, w_out):
    tok_w = tokens.shape[0]
    shard_count = lax.axis_size("wide")
    shard_index = lax.axis_index("wide")
    block_count = page_table.shape[0]
    pairs_here = w_key.shape[1] // HD
    seg_rows = segment_ids.reshape(8, tok_w // 8)
    table_row = jnp.pad(page_table[None, :], ((0, 7), (0, tok_w // 8 - block_count)))
    meta = jnp.concatenate([seg_rows, table_row], axis=0)
    gain_in = jnp.pad(pre_gain[None, :], ((0, 15), (0, 0)))
    columns = []
    for g in range(pairs_here):
        columns += [w_key[:, g * HD : (g + 1) * HD], w_value[:, g * HD : (g + 1) * HD]]
    weights = jnp.concatenate(columns + [w_query, jnp.transpose(w_out)], axis=1)
    half_width = HD // 2
    inverse_freq = jnp.exp(
        -math.log(10000.0) * 2.0 * jnp.arange(half_width, dtype=jnp.float32) / HD
    )
    signs = jnp.where(jnp.arange(HD) < half_width, -1.0, 1.0)
    freq = jnp.zeros((8, HD), jnp.float32)
    freq = freq.at[0].set(jnp.concatenate([inverse_freq, inverse_freq])).at[1].set(signs)
    ids = jnp.broadcast_to(segment_ids[:, None], (tok_w, 128))
    attn_out, flat, w_all, meta_all = front(tokens, weights, meta, gain_in, ids, freq)
    table_all = meta_all[:, 8, :block_count].reshape(-1)

    page_len = tok_w // block_count
    token_blocks = flat.reshape(block_count, page_len, pairs_here, 2 * HD)
    owners = page_table // block_count
    shard_ids = jnp.arange(shard_count, dtype=jnp.int32)
    send_pick = (owners[None, :] == shard_ids[:, None]).astype(jnp.bfloat16)
    outgoing = jnp.einsum(
        "sj,jpgc->sgpc", send_pick, token_blocks, preferred_element_type=jnp.float32
    ).astype(jnp.bfloat16)
    mixed, incoming = tail(
        attn_out, w_all, tokens, jnp.pad(post_gain[None, :], ((0, 15), (0, 0))), outgoing
    )
    my_pages = shard_index * block_count + jnp.arange(block_count, dtype=jnp.int32)
    found_page = table_all[None, :] == my_pages[:, None]
    anchor = jnp.sum(
        jnp.where(
            found_page, jnp.arange(table_all.shape[0], dtype=jnp.int32)[None, :] // block_count, 0
        ),
        axis=1,
    )
    take_pick = (anchor[:, None] == shard_ids[None, :]).astype(jnp.bfloat16)
    kv_pages = jnp.einsum(
        "qs,sgpc->qgpc", take_pick, incoming, preferred_element_type=jnp.float32
    ).astype(jnp.bfloat16)
    return (mixed, kv_pages)


def solution(mesh):
    return jax.shard_map(
        local,
        mesh=mesh,
        in_specs=(
            P("wide", "narrow"),
            P("wide"),
            P("wide"),
            P("narrow"),
            P("narrow"),
            P("wide", "narrow"),
            P("wide", "narrow"),
            P("wide", "narrow"),
            P("narrow", "wide"),
        ),
        out_specs=(P("wide", "narrow"), P("wide", "narrow", None, None)),
        check_vma=False,
    )
```

```python
import functools
import math

import jax
import jax.numpy as jnp
from jax import lax
from jax.experimental import pallas as pl
from jax.experimental.pallas import tpu as pltpu
from jax.sharding import PartitionSpec as P

D = 4608
HD = 128
WINDOW = 4096
SEGS = 8

SOFT_CAP = 50.0
QUERY_SCALE = 1.0 / 12.0
NORM_EPSILON = 1e-06
NX, NY, NZ = 4, 4, 4
MESH = pl.DeviceIdType.MESH
PRE = QUERY_SCALE / SOFT_CAP
POST = SOFT_CAP * math.log2(math.e)


QB = 256
REACH = 4
WAVES = 3


def lanes(start, size):
    return pl.ds(pl.multiple_of(start, 128), size)


def front_kernel(
    tok_ref, wq_ref, wk_ref, wv_ref, wo_ref, meta_ref, gain_ref, ids_ref, freq_ref,
    out_ref, kv_hbm, w_out_hbm, meta_out,
    tok, w, meta_all, gain_all, cos_ref, sin_ref, floor_ref, query_all, held, total,
    w_send, w_recv, z_send, z_recv, c_send, c_recv, m_send, m_recv, g_send, g_recv, own_sem,
    out_sem, send, recv,
):
    wide = lax.axis_index("wide")
    narrow = lax.axis_index("narrow")
    x, y = lax.div(wide, NY), lax.rem(wide, NY)
    z, core = lax.div(narrow, 2), lax.rem(narrow, 2)
    shard = wq_ref.shape[0]
    part_rows = (shard * 7 // 18, shard - shard * 7 // 18)
    part_first = (0, part_rows[0])
    half = wq_ref.shape[1]
    parts, tokens, width = tok.shape
    blocks = tokens // QB

    def block_rows(b):
        return pl.ds(pl.multiple_of(b * QB, QB), QB)

    def ring(position, count, step):
        return lax.rem(position + step + count, count)

    started = []

    def remote(src, dst, send_sem, recv_sem, where):
        copy = pltpu.make_async_remote_copy(
            src_ref=src, dst_ref=dst, send_sem=send_sem, recv_sem=recv_sem,
            device_id=where, device_id_type=MESH,
        )
        copy.start()
        started.append(copy)
        return copy

    def peer(part, stage, step):
        if (part == 0) == (stage == 0):
            return {"wide": ring(x, NX, step) * NY + y}
        return {"wide": x * NY + ring(y, NY, step)}

    def rows_of(part, along, across):
        if part == 0:
            block = ring(x, NX, along) * NY + ring(y, NY, across)
        else:
            block = ring(x, NX, across) * NY + ring(y, NY, along)
        return pl.ds(pl.multiple_of(block * shard + part_first[part], 16), part_rows[part])

    def hop(wave, part, group, kind):
        where = peer(part, 0 if group == 0 else 1, 1 if kind % 2 == 0 else -1)
        passed = (0, 0, -1, 1)[kind]
        if group == 0:
            there = rows_of(part, passed, 0)
        else:
            there = rows_of(part, (0, -1, 1, 2)[group - 1], passed)
        if kind < 2:
            span = pl.ds(wave * half, half)
        else:
            span = pl.ds(wave * half + (kind - 2) * (half // 2), half // 2)
        return pltpu.make_async_remote_copy(
            src_ref=w.at[there, span], dst_ref=w.at[there, span],
            send_sem=w_send.at[wave, part, group, kind],
            recv_sem=w_recv.at[wave, part, group, kind],
            device_id=where, device_id_type=MESH,
        )

    def go(wave, part, group, kind):
        hop(wave, part, group, kind).start()

    def got(wave, part, group, kind):
        hop(wave, part, group, kind).wait_recv()

    def wave_own(wave):
        for group in (0, 1):
            for part in (0, 1):
                go(wave, part, group, 0)
                go(wave, part, group, 1)

    def wave_first(wave):
        for kind, group in ((0, 2), (1, 3)):
            for part in (0, 1):
                got(wave, part, 0, kind)
                go(wave, part, 0, 2 + kind)
                go(wave, part, group, 0)
                go(wave, part, group, 1)

    def wave_pass(wave, group):
        for part in (0, 1):
            got(wave, part, group, 0)
            go(wave, part, group, 2)
            got(wave, part, group, 1)
            go(wave, part, group, 3)

    def wave_far(wave):
        for part in (0, 1):
            got(wave, part, 0, 2)
            got(wave, part, 0, 3)
            go(wave, part, 4, 0)
            go(wave, part, 4, 1)

    def wave_end(wave):
        for group in range(1, 5):
            for part in (0, 1):
                got(wave, part, group, 2)
                got(wave, part, group, 3)

    toks = {}

    def zgo(kind, index, src, span):
        where = {"narrow": ring(z, NZ, 1 if kind % 2 == 0 else -1) * 2 + core}
        toks[kind] = remote(src, tok.at[index, span], z_send.at[kind], z_recv.at[kind], where)

    pair = {}

    def cgo(kind, index, src, span):
        where = {"narrow": z * 2 + (1 - core)}
        pair[kind] = remote(src, tok.at[index, span], c_send.at[kind], c_recv.at[kind], where)

    every = pl.ds(0, tokens)
    low, high = pl.ds(0, tokens // 2), pl.ds(tokens // 2, tokens // 2)

    def zblock(step):
        return ring(z, NZ, step) * 2 + core

    own_rows = pl.ds(pl.multiple_of(wide * shard, 16), shard)
    pieces = [(wq_ref, half), (wo_ref, 2 * half)]
    for g in range(2):
        there = slice(g * HD, (g + 1) * HD)
        pieces.append((wk_ref.at[:, there], g * 256))
        pieces.append((wv_ref.at[:, there], g * 256 + HD))
    loads = [
        pltpu.make_async_copy(
            piece, w.at[own_rows, pl.ds(column, piece.shape[1])], own_sem.at[3 + i]
        )
        for i, (piece, column) in enumerate(pieces)
    ]
    for copy in loads[2:] + loads[:2]:
        copy.start()
    small = []
    for other in range(1, NX * NY):
        target = lax.rem(wide + other, NX * NY)
        small.append(remote(
            meta_ref, meta_all.at[wide], m_send.at[other], m_recv.at[other], {"wide": target}))
    for other in range(1, NZ * 2):
        target = lax.rem(narrow + other, NZ * 2)
        small.append(remote(
            gain_ref, gain_all.at[narrow], g_send.at[other], g_recv.at[other], {"narrow": target}))
    zgo(0, narrow, tok_ref.at[low], low)
    zgo(1, narrow, tok_ref.at[high], high)
    for copy in loads:
        copy.wait()
    wave_own(0)
    zgo(4, narrow, tok_ref.at[high], high)
    zgo(5, narrow, tok_ref.at[low], low)
    cgo(0, narrow, tok_ref, every)
    local = [
        pltpu.make_async_copy(tok_ref, tok.at[narrow], own_sem.at[0]),
        pltpu.make_async_copy(meta_ref, meta_all.at[wide], own_sem.at[1]),
        pltpu.make_async_copy(gain_ref, gain_all.at[narrow], own_sem.at[2]),
    ]
    for copy in local:
        copy.start()
    wave_own(1)
    wave_first(0)

    for copy in small:
        copy.wait_recv()
    for copy in local:
        copy.wait()
    save_meta = pltpu.make_async_copy(meta_all, meta_out, out_sem.at[2])
    save_meta.start()
    first_token = wide * tokens
    all_ids = meta_all[:, 0:8, :]
    firsts = [
        jnp.sum((all_ids < label).astype(jnp.float32)).astype(jnp.int32)
        for label in range(1, SEGS)
    ]

    def tables(b, carry):
        rows = block_rows(b)
        ids = ids_ref[rows, :]
        start = jnp.zeros((QB, 128), jnp.int32)
        for label in range(1, SEGS):
            start = jnp.where(ids == label, firsts[label - 1], start)
        index = first_token + b * QB + lax.broadcasted_iota(jnp.int32, (QB, 128), 0)
        angle = (index - start).astype(jnp.float32) * freq_ref[0:1, :]
        cos_ref[rows, :] = jnp.cos(angle)
        sin_ref[rows, :] = jnp.sin(angle) * freq_ref[1:2, :]
        floor_ref[rows, :] = jnp.maximum(start, index - WINDOW + 1) - (first_token - WINDOW)
        return carry

    wave_pass(0, 1)
    wave_far(0)
    toks[0].wait_recv()
    zgo(2, zblock(-1), tok.at[zblock(-1), low], low)
    cgo(1, zblock(-1), tok.at[zblock(-1), low], low)
    toks[1].wait_recv()
    zgo(3, zblock(1), tok.at[zblock(1), high], high)
    cgo(2, zblock(1), tok.at[zblock(1), high], high)
    wave_own(2)
    lax.fori_loop(0, blocks, tables, 0)
    wave_pass(0, 2)
    wave_pass(0, 3)
    wave_pass(0, 4)
    wave_first(1)
    wave_pass(1, 1)
    wave_far(1)
    toks[4].wait_recv()
    cgo(5, zblock(-1), tok.at[zblock(-1), high], high)
    toks[5].wait_recv()
    cgo(6, zblock(1), tok.at[zblock(1), low], low)
    wave_pass(1, 2)
    wave_pass(1, 3)
    wave_pass(1, 4)
    wave_first(2)
    toks[2].wait_recv()
    cgo(3, zblock(2), tok.at[zblock(2), low], low)
    toks[3].wait_recv()
    cgo(4, zblock(2), tok.at[zblock(2), high], high)
    wave_end(0)
    wave_pass(2, 1)
    wave_far(2)
    for kind in range(7):
        pair[kind].wait_recv()
    for kind in range(7):
        pair[kind].wait_send()
    for kind in range(6):
        toks[kind].wait_send()
    done = [id(copy) for copy in list(pair.values()) + list(toks.values())]
    started[:] = [copy for copy in started if id(copy) not in done]

    def rotated(value, rows):
        return value * cos_ref[rows, :] + pltpu.roll(value, HD // 2, 1) * sin_ref[rows, :]

    def key_block(b, carry):
        rows = block_rows(b)
        squares = jnp.zeros((QB, 1), jnp.float32)
        for n in range(parts):
            piece = tok[n, rows, :].astype(jnp.float32)
            squares += jnp.sum(piece * piece, axis=1, keepdims=True)
        scale = lax.rsqrt(squares / D + NORM_EPSILON)
        product = jnp.zeros((QB, half), jnp.float32)
        for n in range(parts):
            piece = tok[n, rows, :].astype(jnp.float32)
            normed = (piece * scale * gain_all[n, 0:1, :].astype(jnp.float32)).astype(jnp.bfloat16)
            tok[n, rows, :] = normed
            product += jnp.dot(
                normed, w[pl.ds(n * width, width), 0:half], preferred_element_type=jnp.float32
            )
        for g in range(2):
            key = product[:, g * 256 : g * 256 + HD]
            held[0, rows, g * 256 : g * 256 + HD] = rotated(key, rows).astype(jnp.bfloat16)
            held[0, rows, g * 256 + HD : g * 256 + 256] = product[
                :, g * 256 + HD : g * 256 + 256
            ].astype(jnp.bfloat16)
        return carry

    def query_block(b, carry):
        rows = block_rows(b)
        product = jnp.zeros((QB, half), jnp.float32)
        for n in range(parts):
            product += jnp.dot(
                tok[n, rows, :], w[pl.ds(n * width, width), half : 2 * half],
                preferred_element_type=jnp.float32,
            )
        for h in range(half // HD):
            value = product[:, h * HD : (h + 1) * HD]
            query_all[rows, h * HD : (h + 1) * HD] = rotated(value, rows).astype(jnp.bfloat16)
        return carry

    next_x = lax.rem(x + 1, NX) * NY + y
    next_y = x * NY + lax.rem(y + 1, NY)
    last_y = x * NY + lax.rem(y + NY - 1, NY)
    inner = (y == 1) | (y == 2)

    def move(kind, source, slot, where, c):
        rows = block_rows(c)
        return pltpu.make_async_remote_copy(
            src_ref=held.at[source, rows], dst_ref=held.at[slot, rows],
            send_sem=send.at[kind, c], recv_sem=recv.at[slot, c],
            device_id={"wide": where}, device_id_type=MESH,
        )

    def along_x(c):
        return move(0, 0, 4, next_x, c)

    def up(source, c):
        return move(1, source, 1, next_y, c)

    def down(source, c):
        return move(2, source, 3, last_y, c)

    def pass_up(c):
        return move(3, 1, 2, next_y, c)

    def pass_down(c):
        return move(4, 3, 2, last_y, c)

    def begin(c, carry):
        along_x(c).start()

        @pl.when(y < NY - 1)
        def _():
            up(0, c).start()

        @pl.when(y == 0)
        def _():
            down(0, c).start()

        return carry

    def weigh(d, g, qb, first, size, diagonal=False):
        qrows = block_rows(qb)
        krows = pl.ds(pl.multiple_of(first, 256), size)
        query = jnp.concatenate(
            [query_all[qrows, lanes(g * 256, 128)], query_all[qrows, lanes(g * 256 + 128, 128)]],
            axis=0,
        )
        keys = held[d, krows, lanes(g * 256, 128)]
        values = held[d, krows, lanes(g * 256 + 128, 128)]
        scores = lax.dot_general(
            query, keys, (((1,), (1,)), ((), ())), preferred_element_type=jnp.float32
        )
        floor = floor_ref[qrows, :] - ((REACH - d) * tokens + first)
        floor = jnp.concatenate([floor] * (size // 128), axis=1)
        column = lax.broadcasted_iota(jnp.int32, (QB, size), 1)
        allowed = column >= floor
        if diagonal:
            allowed = allowed & (column <= lax.broadcasted_iota(jnp.int32, (QB, size), 0))
        weights = jnp.exp2(jnp.tanh(scores * PRE) * POST)
        weights = jnp.concatenate(
            [
                jnp.where(allowed, weights[:QB], 0.0).astype(jnp.bfloat16),
                jnp.where(allowed, weights[QB:], 0.0).astype(jnp.bfloat16),
            ],
            axis=0,
        )
        wide_values = jnp.concatenate([values, jnp.ones_like(values)], axis=1)
        return jnp.dot(weights, wide_values, preferred_element_type=jnp.float32)

    def chunk(d, g, qb, first, size, diagonal=False, fresh=False):
        product = weigh(d, g, qb, first, size, diagonal)
        slot = g * blocks + qb
        if fresh:
            total[slot] = product
        else:
            total[slot] += product

    def own_pair(t, carry):
        g, qb = lax.div(t, blocks), lax.rem(t, blocks)
        chunk(0, g, qb, qb * QB, QB, diagonal=True, fresh=True)
        lax.fori_loop(0, qb, lambda k, c: (chunk(0, g, qb, k * QB, QB), c)[1], 0)
        return carry

    def segment(d, k, pairs):
        def pair(t, carry):
            first = weigh(d, 0, t, k * QB, QB)
            second = weigh(d, 1, t, k * QB, QB)
            total[t] += first
            total[blocks + t] += second
            return carry

        lax.fori_loop(0, pairs, pair, 0)

    for b in range(blocks):
        lax.fori_loop(b, b + 1, key_block, 0)
        lax.fori_loop(b, b + 1, begin, 0)
        if b == 1:
            wave_pass(2, 2)
        if b == 2:
            wave_pass(2, 3)
    wave_pass(2, 4)
    save = pltpu.make_async_copy(held.at[0], kv_hbm, out_sem.at[0])
    save.start()

    def pump(c):
        along_x(c).wait_recv()

        @pl.when(y == NY - 1)
        def _():
            up(4, c).start()

        @pl.when(y > 0)
        def _():
            down(4, c).start()

    wave_end(1)
    lax.fori_loop(0, 2, query_block, 0)
    pump(0)
    lax.fori_loop(2, blocks, query_block, 0)
    pump(1)
    lax.fori_loop(0, blocks, own_pair, 0)
    pump(2)
    lax.fori_loop(blocks, 2 * blocks, own_pair, 0)
    pump(3)

    def step(i, carry):
        @pl.when(i < blocks)
        def _():
            up(0, i).wait_recv()

            @pl.when(inner)
            def _():
                pass_up(i).start()

            segment(4, i, i + 1)
            down(0, i).wait_recv()

            @pl.when(inner)
            def _():
                pass_down(i).start()

            segment(1, i, blocks)

        @pl.when(i < blocks)
        def _():
            segment(3, i, blocks)

        @pl.when(i >= 1)
        def _():
            pass_up(i - 1).wait_recv()
            segment(2, i - 1, blocks)

        return carry

    lax.fori_loop(0, blocks + 1, step, 0)

    def finish(t, carry):
        g, qb = lax.div(t, blocks), lax.rem(t, blocks)
        slot = g * blocks + qb
        result = (total[slot, :, :HD] / total[slot, :, HD:]).astype(out_ref.dtype)
        out_ref[block_rows(qb), lanes(g * 256, 128)] = result[:QB]
        out_ref[block_rows(qb), lanes(g * 256 + 128, 128)] = result[QB:]
        return carry

    lax.fori_loop(0, 2 * blocks, finish, 0)
    wave_end(2)
    save_w = pltpu.make_async_copy(w.at[:, pl.ds(2 * half, half)], w_out_hbm, out_sem.at[1])
    save_w.start()
    save.wait()
    save_meta.wait()

    def drain(c, carry):
        along_x(c).wait_send()
        up(0, c).wait_send()
        down(0, c).wait_send()

        @pl.when(inner)
        def _():
            pass_up(c).wait_send()
            pass_down(c).wait_send()

        return carry

    lax.fori_loop(0, blocks, drain, 0)
    for copy in started:
        copy.wait_send()
    for wave in range(WAVES):
        for part in (0, 1):
            for group in range(5):
                for kind in range(4):
                    hop(wave, part, group, kind).wait_send()
    save_w.wait()


def front(tokens, w_query, w_key, w_value, w_out_rows, meta, gain, ids, freq):
    rows, width = tokens.shape
    shard, half = w_query.shape
    columns = WAVES * half
    vmem_spec = pl.BlockSpec(memory_space=pltpu.VMEM)
    any_spec = pl.BlockSpec(memory_space=pl.ANY)
    dma = pltpu.SemaphoreType.DMA
    bf16 = jnp.bfloat16
    blocks = rows // QB
    return pl.pallas_call(
        front_kernel,
        out_shape=(
            jax.ShapeDtypeStruct((rows, half), bf16),
            jax.ShapeDtypeStruct((rows, half), bf16),
            jax.ShapeDtypeStruct((16 * shard, half), bf16),
            jax.ShapeDtypeStruct((16,) + meta.shape, meta.dtype),
        ),
        in_specs=[any_spec] * 5 + [vmem_spec] * 4,
        out_specs=(vmem_spec, any_spec, any_spec, any_spec),
        scratch_shapes=[
            pltpu.VMEM((8, rows, width), bf16),
            pltpu.VMEM((16 * shard, columns), bf16),
            pltpu.VMEM((16,) + meta.shape, jnp.int32),
            pltpu.VMEM((8,) + gain.shape, bf16),
            pltpu.VMEM((rows, 128), jnp.float32),
            pltpu.VMEM((rows, 128), jnp.float32),
            pltpu.VMEM((rows, 128), jnp.int32),
            pltpu.VMEM((rows, half), bf16),
            pltpu.VMEM((REACH + 1, rows, half), bf16),
            pltpu.VMEM((8, 2 * QB, 256), jnp.float32),
            dma((3, 2, 5, 4)), dma((3, 2, 5, 4)), dma((6,)), dma((6,)), dma((7,)), dma((7,)),
            dma((16,)), dma((16,)), dma((8,)), dma((8,)), dma((9,)),
            dma((3,)), dma((5, blocks)), dma((REACH + 1, blocks)),
        ],
        cost_estimate=pl.CostEstimate(
            flops=4 * rows * 4352 * 128 * 8, bytes_accessed=32 << 20,
            transcendentals=8 * rows * 4352,
        ),
        compiler_params=pltpu.CompilerParams(
            vmem_limit_bytes=60 << 20, has_side_effects=True
        ),
        name="front",
    )(tokens, w_query, w_key, w_value, w_out_rows, meta, gain, ids, freq)


def tail_kernel(
    attn_ref, tok_ref, gain_ref, w_hbm, pages_hbm,
    mixed_ref, pages_in,
    w, w_sem, give, take, stage, far, near, kept, squares,
    p_send, p_recv, own_sem, c_send, c_recv, f_send, f_recv, n_send, n_recv, s_send, s_recv,
):
    wide = lax.axis_index("wide")
    narrow = lax.axis_index("narrow")
    z, core = lax.div(narrow, 2), lax.rem(narrow, 2)
    count = NX * NY
    tokens = attn_ref.shape[0]
    mid = tokens // 2
    low, high = pl.ds(0, mid), pl.ds(mid, mid)
    sibling = {"narrow": z * 2 + (1 - core)}

    def at_z(step):
        return lax.rem(z + step + NZ, NZ)

    def remote(src, dst, send, recv, where):
        copy = pltpu.make_async_remote_copy(
            src_ref=src, dst_ref=dst, send_sem=send, recv_sem=recv,
            device_id=where, device_id_type=MESH,
        )
        copy.start()
        return copy

    pages = [
        remote(
            pages_hbm.at[lax.rem(wide + other, count)], pages_in.at[wide],
            p_send.at[other], p_recv.at[other], {"wide": lax.rem(wide + other, count)},
        )
        for other in range(1, count)
    ]
    own = pltpu.make_async_copy(pages_hbm.at[wide], pages_in.at[wide], own_sem)
    own.start()

    steps = (2, 1, -1, 0)
    depth, width = attn_ref.shape[1], tok_ref.shape[1]
    loads = []
    for slot in range(8):
        index = at_z(steps[slot % 4]) * 2 + ((1 - core) if slot < 4 else core)
        source = pl.ds(pl.multiple_of(index * width, width), width)
        loads.append(
            pltpu.make_async_copy(
                w_hbm.at[source, pl.ds(w_hbm.shape[1] - depth, depth)], w.at[slot], w_sem.at[slot]
            )
        )
        loads[-1].start()

    def term(slot, rows):
        return lax.dot_general(
            attn_ref[rows, :], w[slot], (((1,), (1,)), ((), ())),
            preferred_element_type=jnp.float32,
        ).astype(jnp.bfloat16)

    def over_rows(body, first=0, size=tokens):
        def step(b, carry):
            body(pl.ds(pl.multiple_of(first + b * QB, QB), QB))
            return carry

        lax.fori_loop(0, size // QB, step, 0)

    passes = []
    for i in range(4):
        loads[i].wait()

        def fill(rows, i=i):
            give[i, rows, :] = term(i, rows)

        over_rows(fill)
        passes.append(remote(give.at[i], take.at[i], c_send.at[i], c_recv.at[i], sibling))

    def own_sum(i, rows):
        mine = term(4 + i, rows)
        return mine.astype(jnp.float32) + take[i, rows, :].astype(jnp.float32)

    def put(i):
        def body(rows):
            stage[i, rows, :] = own_sum(i, rows).astype(jnp.bfloat16)

        return body

    ahead, behind = {"narrow": at_z(1) * 2 + core}, {"narrow": at_z(-1) * 2 + core}
    for i in range(4, 8):
        loads[i].wait()
    passes[0].wait_recv()
    over_rows(put(0), 0, mid)
    far_up = remote(stage.at[0, low], far.at[0], f_send.at[0], f_recv.at[0], ahead)
    over_rows(put(0), mid, mid)
    far_down = remote(stage.at[0, high], far.at[1], f_send.at[1], f_recv.at[1], behind)
    passes[1].wait_recv()
    over_rows(put(1), mid, mid)
    near_a = remote(stage.at[1, high], near.at[0, high], n_send.at[0], n_recv.at[0], ahead)
    passes[2].wait_recv()
    over_rows(put(2), 0, mid)
    near_b = remote(stage.at[2, low], near.at[1, low], n_send.at[1], n_recv.at[1], behind)

    far_up.wait_recv()

    def with_far_up(rows):
        stage[1, rows, :] = (own_sum(1, rows) + far[0, rows, :].astype(jnp.float32)).astype(
            jnp.bfloat16
        )

    over_rows(with_far_up, 0, mid)
    near_c = remote(stage.at[1, low], near.at[0, low], n_send.at[2], n_recv.at[2], ahead)
    far_down.wait_recv()

    def with_far_down(b, carry):
        rows = pl.ds(pl.multiple_of(mid + b * QB, QB), QB)
        source = pl.ds(pl.multiple_of(b * QB, QB), QB)
        stage[2, rows, :] = (own_sum(2, rows) + far[1, source, :].astype(jnp.float32)).astype(
            jnp.bfloat16
        )
        return carry

    lax.fori_loop(0, mid // QB, with_far_down, 0)
    near_d = remote(stage.at[2, high], near.at[1, high], n_send.at[3], n_recv.at[3], behind)
    passes[3].wait_recv()

    def keep(rows):
        kept[rows, :] = own_sum(3, rows)

    over_rows(keep)
    for copy in (near_a, near_b, near_c, near_d):
        copy.wait_recv()

    ones = jnp.ones((8, tok_ref.shape[1]), jnp.float32)

    def finish(rows):
        value = (
            kept[rows, :]
            + near[0, rows, :].astype(jnp.float32)
            + near[1, rows, :].astype(jnp.float32)
        )
        kept[rows, :] = value
        squares[0, :, rows] = lax.dot_general(
            ones, value * value, (((1,), (1,)), ((), ())),
            precision=lax.Precision.HIGHEST, preferred_element_type=jnp.float32,
        )

    over_rows(finish)
    sums = [
        remote(
            squares.at[0], squares.at[other], s_send.at[other], s_recv.at[other],
            {"narrow": lax.rem(narrow + other, NZ * 2)},
        )
        for other in range(1, NZ * 2)
    ]
    for copy in sums:
        copy.wait_recv()
    pick = jnp.full((8, 128), 0.125, jnp.float32)

    def emit(rows):
        whole = squares[0, :, rows]
        for other in range(1, NZ * 2):
            whole += squares[other, :, rows]
        column = lax.dot_general(
            whole, pick, (((0,), (0,)), ((), ())),
            precision=lax.Precision.HIGHEST, preferred_element_type=jnp.float32,
        )
        scale = lax.rsqrt(column / D + NORM_EPSILON)[:, 0:1]
        mixed_ref[rows, :] = (
            tok_ref[rows, :].astype(jnp.float32)
            + kept[rows, :] * scale * gain_ref[0:1, :].astype(jnp.float32)
        ).astype(jnp.bfloat16)

    over_rows(emit)
    for copy in pages:
        copy.wait_recv()
    own.wait()
    for copy in pages + passes + sums:
        copy.wait_send()
    for copy in (far_up, far_down, near_a, near_b, near_c, near_d):
        copy.wait_send()


def tail(attn, w_all, tokens, post_gain, outgoing):
    rows, width = tokens.shape
    vmem_spec = pl.BlockSpec(memory_space=pltpu.VMEM)
    any_spec = pl.BlockSpec(memory_space=pl.ANY)
    dma = pltpu.SemaphoreType.DMA
    bf16 = jnp.bfloat16
    return pl.pallas_call(
        tail_kernel,
        out_shape=(
            jax.ShapeDtypeStruct(tokens.shape, bf16),
            jax.ShapeDtypeStruct(outgoing.shape, bf16),
        ),
        in_specs=[vmem_spec] * 3 + [any_spec] * 2,
        out_specs=(vmem_spec, any_spec),
        scratch_shapes=[
            pltpu.VMEM((8, width, attn.shape[1]), bf16),
            dma((8,)),
            pltpu.VMEM((4, rows, width), bf16),
            pltpu.VMEM((4, rows, width), bf16),
            pltpu.VMEM((3, rows, width), bf16),
            pltpu.VMEM((2, rows // 2, width), bf16),
            pltpu.VMEM((2, rows, width), bf16),
            pltpu.VMEM((rows, width), jnp.float32),
            pltpu.VMEM((8, 8, rows), jnp.float32),
            dma((16,)), dma((16,)), dma, dma((4,)), dma((4,)), dma((2,)), dma((2,)),
            dma((4,)), dma((4,)), dma((8,)), dma((8,)),
        ],
        cost_estimate=pl.CostEstimate(
            flops=2 * rows * 512 * D, bytes_accessed=24 << 20, transcendentals=0
        ),
        compiler_params=pltpu.CompilerParams(
            vmem_limit_bytes=56 << 20, has_side_effects=True
        ),
        name="tail",
    )(attn, tokens, post_gain, w_all, outgoing)


def local(tokens, segment_ids, page_table, pre_gain, post_gain, w_query, w_key, w_value, w_out):
    tok_w = tokens.shape[0]
    shard_count = lax.axis_size("wide")
    shard_index = lax.axis_index("wide")
    block_count = page_table.shape[0]
    pairs_here = w_key.shape[1] // HD
    seg_rows = segment_ids.reshape(8, tok_w // 8)
    table_row = jnp.pad(page_table[None, :], ((0, 7), (0, tok_w // 8 - block_count)))
    meta = jnp.concatenate([seg_rows, table_row], axis=0)
    gain_in = jnp.broadcast_to(pre_gain[None, :], (16, pre_gain.shape[0]))
    half_width = HD // 2
    inverse_freq = jnp.exp(
        -math.log(10000.0) * 2.0 * (jnp.arange(HD) % half_width).astype(jnp.float32) / HD
    )
    signs = jnp.where(jnp.arange(HD) < half_width, -1.0, 1.0)
    freq = jnp.where(jnp.arange(8)[:, None] == 0, inverse_freq[None, :], signs[None, :])
    ids = jnp.broadcast_to(segment_ids[:, None], (tok_w, 128))
    attn_out, flat, w_all, meta_all = front(
        tokens, w_query, w_key, w_value, jnp.transpose(w_out), meta, gain_in, ids, freq
    )
    table_all = meta_all[:, 8, :block_count].reshape(-1)

    page_len = tok_w // block_count
    token_blocks = flat.reshape(block_count, page_len, pairs_here, 2 * HD)
    owners = page_table // block_count
    shard_ids = jnp.arange(shard_count, dtype=jnp.int32)
    send_pick = (owners[None, :] == shard_ids[:, None]).astype(jnp.bfloat16)
    outgoing = jnp.einsum(
        "sj,jpgc->sgpc", send_pick, token_blocks, preferred_element_type=jnp.float32
    ).astype(jnp.bfloat16)
    mixed, incoming = tail(
        attn_out, w_all, tokens, post_gain[None, :], outgoing
    )
    my_pages = shard_index * block_count + jnp.arange(block_count, dtype=jnp.int32)
    found_page = table_all[None, :] == my_pages[:, None]
    anchor = jnp.sum(
        jnp.where(
            found_page, jnp.arange(table_all.shape[0], dtype=jnp.int32)[None, :] // block_count, 0
        ),
        axis=1,
    )
    take_pick = (anchor[:, None] == shard_ids[None, :]).astype(jnp.bfloat16)
    kv_pages = jnp.einsum(
        "qs,sgpc->qgpc", take_pick, incoming, preferred_element_type=jnp.float32
    ).astype(jnp.bfloat16)
    return (mixed, kv_pages)


def solution(mesh):
    return jax.shard_map(
        local,
        mesh=mesh,
        in_specs=(
            P("wide", "narrow"),
            P("wide"),
            P("wide"),
            P("narrow"),
            P("narrow"),
            P("wide", "narrow"),
            P("wide", "narrow"),
            P("wide", "narrow"),
            P("narrow", "wide"),
        ),
        out_specs=(P("wide", "narrow"), P("wide", "narrow", None, None)),
        check_vma=False,
    )
```

```python
import math

import jax
import jax.numpy as jnp
import numpy as np
from jax import lax
from jax.experimental import pallas as pl
from jax.experimental.pallas import tpu as pltpu
from jax.sharding import PartitionSpec as P

D = 4608
HD = 128
WINDOW = 4096
SEGS = 8

SOFT_CAP = 50.0
QUERY_SCALE = 1.0 / 12.0
NORM_EPSILON = 1e-06
NX, NY, NZ = 4, 4, 4
MESH = pl.DeviceIdType.MESH
PRE = QUERY_SCALE / SOFT_CAP
POST = SOFT_CAP * math.log2(math.e)


QB = 256
REACH = 4
WAVES = 3


def lanes(start, size):
    return pl.ds(pl.multiple_of(start, 128), size)


def front_kernel(
    tok_ref, wq_ref, wk_ref, wv_ref, wo_ref, meta_ref, gain_ref, ids_ref, freq_ref,
    out_ref, kv_hbm, w_out_hbm, meta_out,
    tok, w, meta_all, gain_all, cos_ref, sin_ref, floor_ref, query_all, held, total,
    w_send, w_recv, z_send, z_recv, c_send, c_recv, m_send, m_recv, g_send, g_recv, own_sem,
    out_sem, send, recv,
):
    wide = lax.axis_index("wide")
    narrow = lax.axis_index("narrow")
    x, y = lax.div(wide, NY), lax.rem(wide, NY)
    z, core = lax.div(narrow, 2), lax.rem(narrow, 2)
    shard = wq_ref.shape[0]
    part_rows = (shard * 7 // 18, shard - shard * 7 // 18)
    part_first = (0, part_rows[0])
    half = wq_ref.shape[1]
    parts, tokens, width = tok.shape
    blocks = tokens // QB

    def block_rows(b):
        return pl.ds(pl.multiple_of(b * QB, QB), QB)

    def ring(position, count, step):
        return lax.rem(position + step + count, count)

    started = []

    def remote(src, dst, send_sem, recv_sem, where):
        copy = pltpu.make_async_remote_copy(
            src_ref=src, dst_ref=dst, send_sem=send_sem, recv_sem=recv_sem,
            device_id=where, device_id_type=MESH,
        )
        copy.start()
        started.append(copy)
        return copy

    def peer(part, stage, step):
        if (part == 0) == (stage == 0):
            return {"wide": ring(x, NX, step) * NY + y}
        return {"wide": x * NY + ring(y, NY, step)}

    def rows_of(part, along, across):
        if part == 0:
            block = ring(x, NX, along) * NY + ring(y, NY, across)
        else:
            block = ring(x, NX, across) * NY + ring(y, NY, along)
        return pl.ds(pl.multiple_of(block * shard + part_first[part], 16), part_rows[part])

    def hop(wave, part, group, kind):
        where = peer(part, 0 if group == 0 else 1, 1 if kind % 2 == 0 else -1)
        passed = (0, 0, -1, 1)[kind]
        if group == 0:
            there = rows_of(part, passed, 0)
        else:
            there = rows_of(part, (0, -1, 1, 2)[group - 1], passed)
        if kind < 2:
            span = pl.ds(wave * half, half)
        else:
            span = pl.ds(wave * half + (kind - 2) * (half // 2), half // 2)
        return pltpu.make_async_remote_copy(
            src_ref=w.at[there, span], dst_ref=w.at[there, span],
            send_sem=w_send.at[wave, part, group, kind],
            recv_sem=w_recv.at[wave, part, group, kind],
            device_id=where, device_id_type=MESH,
        )

    def go(wave, part, group, kind):
        hop(wave, part, group, kind).start()

    def got(wave, part, group, kind):
        hop(wave, part, group, kind).wait_recv()

    def wave_own(wave):
        for group in (0, 1):
            for part in (0, 1):
                go(wave, part, group, 0)
                go(wave, part, group, 1)

    def wave_first(wave):
        for kind, group in ((0, 2), (1, 3)):
            for part in (0, 1):
                got(wave, part, 0, kind)
                go(wave, part, 0, 2 + kind)
                go(wave, part, group, 0)
                go(wave, part, group, 1)

    def wave_pass(wave, group):
        for part in (0, 1):
            got(wave, part, group, 0)
            go(wave, part, group, 2)
            got(wave, part, group, 1)
            go(wave, part, group, 3)

    def wave_far(wave):
        for part in (0, 1):
            got(wave, part, 0, 2)
            got(wave, part, 0, 3)
            go(wave, part, 4, 0)
            go(wave, part, 4, 1)

    def wave_end(wave):
        for group in range(1, 5):
            for part in (0, 1):
                got(wave, part, group, 2)
                got(wave, part, group, 3)

    toks = {}

    def zgo(kind, index, src, span):
        where = {"narrow": ring(z, NZ, 1 if kind % 2 == 0 else -1) * 2 + core}
        toks[kind] = remote(src, tok.at[index, span], z_send.at[kind], z_recv.at[kind], where)

    pair = {}

    def cgo(kind, index, src, span):
        where = {"narrow": z * 2 + (1 - core)}
        pair[kind] = remote(src, tok.at[index, span], c_send.at[kind], c_recv.at[kind], where)

    every = pl.ds(0, tokens)
    low, high = pl.ds(0, tokens // 2), pl.ds(tokens // 2, tokens // 2)

    def zblock(step):
        return ring(z, NZ, step) * 2 + core

    own_rows = pl.ds(pl.multiple_of(wide * shard, 16), shard)
    pieces = [(wq_ref, half), (wo_ref, 2 * half)]
    for g in range(2):
        there = slice(g * HD, (g + 1) * HD)
        pieces.append((wk_ref.at[:, there], g * 256))
        pieces.append((wv_ref.at[:, there], g * 256 + HD))
    loads = [
        pltpu.make_async_copy(
            piece, w.at[own_rows, pl.ds(column, piece.shape[1])], own_sem.at[3 + i]
        )
        for i, (piece, column) in enumerate(pieces)
    ]
    for copy in loads[2:] + loads[:2]:
        copy.start()
    small = []
    for other in range(1, NX * NY):
        target = lax.rem(wide + other, NX * NY)
        small.append(remote(
            meta_ref, meta_all.at[wide], m_send.at[other], m_recv.at[other], {"wide": target}))
    for other in range(1, NZ * 2):
        target = lax.rem(narrow + other, NZ * 2)
        small.append(remote(
            gain_ref, gain_all.at[narrow], g_send.at[other], g_recv.at[other], {"narrow": target}))
    zgo(0, narrow, tok_ref.at[low], low)
    zgo(1, narrow, tok_ref.at[high], high)
    for copy in loads:
        copy.wait()
    wave_own(0)
    zgo(4, narrow, tok_ref.at[high], high)
    zgo(5, narrow, tok_ref.at[low], low)
    cgo(0, narrow, tok_ref, every)
    local = [
        pltpu.make_async_copy(tok_ref, tok.at[narrow], own_sem.at[0]),
        pltpu.make_async_copy(meta_ref, meta_all.at[wide], own_sem.at[1]),
        pltpu.make_async_copy(gain_ref, gain_all.at[narrow], own_sem.at[2]),
    ]
    for copy in local:
        copy.start()
    wave_own(1)
    wave_first(0)

    for copy in small:
        copy.wait_recv()
    for copy in local:
        copy.wait()
    save_meta = pltpu.make_async_copy(meta_all, meta_out, out_sem.at[2])
    save_meta.start()
    first_token = wide * tokens
    all_ids = meta_all[:, 0:8, :]
    firsts = [
        jnp.sum((all_ids < label).astype(jnp.float32)).astype(jnp.int32)
        for label in range(1, SEGS)
    ]

    def tables(b, carry):
        rows = block_rows(b)
        ids = ids_ref[rows, :]
        start = jnp.zeros((QB, 128), jnp.int32)
        for label in range(1, SEGS):
            start = jnp.where(ids == label, firsts[label - 1], start)
        index = first_token + b * QB + lax.broadcasted_iota(jnp.int32, (QB, 128), 0)
        angle = (index - start).astype(jnp.float32) * freq_ref[0:1, :]
        cos_ref[rows, :] = jnp.cos(angle)
        sin_ref[rows, :] = jnp.sin(angle) * freq_ref[1:2, :]
        floor_ref[rows, :] = jnp.maximum(start, index - WINDOW + 1) - (first_token - WINDOW)
        return carry

    wave_pass(0, 1)
    wave_far(0)
    toks[0].wait_recv()
    zgo(2, zblock(-1), tok.at[zblock(-1), low], low)
    cgo(1, zblock(-1), tok.at[zblock(-1), low], low)
    toks[1].wait_recv()
    zgo(3, zblock(1), tok.at[zblock(1), high], high)
    cgo(2, zblock(1), tok.at[zblock(1), high], high)
    wave_own(2)
    lax.fori_loop(0, blocks, tables, 0)
    wave_pass(0, 2)
    wave_pass(0, 3)
    wave_pass(0, 4)
    wave_first(1)
    wave_pass(1, 1)
    wave_far(1)
    toks[4].wait_recv()
    cgo(5, zblock(-1), tok.at[zblock(-1), high], high)
    toks[5].wait_recv()
    cgo(6, zblock(1), tok.at[zblock(1), low], low)
    wave_pass(1, 2)
    wave_pass(1, 3)
    wave_pass(1, 4)
    wave_first(2)
    toks[2].wait_recv()
    cgo(3, zblock(2), tok.at[zblock(2), low], low)
    toks[3].wait_recv()
    cgo(4, zblock(2), tok.at[zblock(2), high], high)
    wave_end(0)
    wave_pass(2, 1)
    wave_far(2)
    for kind in range(7):
        pair[kind].wait_recv()
    for kind in range(7):
        pair[kind].wait_send()
    for kind in range(6):
        toks[kind].wait_send()
    done = [id(copy) for copy in list(pair.values()) + list(toks.values())]
    started[:] = [copy for copy in started if id(copy) not in done]

    def rotated(value, rows):
        return value * cos_ref[rows, :] + pltpu.roll(value, HD // 2, 1) * sin_ref[rows, :]

    def key_block(b, carry):
        rows = block_rows(b)
        squares = jnp.zeros((QB, 1), jnp.float32)
        for n in range(parts):
            piece = tok[n, rows, :].astype(jnp.float32)
            squares += jnp.sum(piece * piece, axis=1, keepdims=True)
        scale = lax.rsqrt(squares / D + NORM_EPSILON)
        product = jnp.zeros((QB, half), jnp.float32)
        for n in range(parts):
            piece = tok[n, rows, :].astype(jnp.float32)
            normed = (piece * scale * gain_all[n, 0:1, :].astype(jnp.float32)).astype(jnp.bfloat16)
            tok[n, rows, :] = normed
            product += jnp.dot(
                normed, w[pl.ds(n * width, width), 0:half], preferred_element_type=jnp.float32
            )
        for g in range(2):
            key = product[:, g * 256 : g * 256 + HD]
            held[0, rows, g * 256 : g * 256 + HD] = rotated(key, rows).astype(jnp.bfloat16)
            held[0, rows, g * 256 + HD : g * 256 + 256] = product[
                :, g * 256 + HD : g * 256 + 256
            ].astype(jnp.bfloat16)
        return carry

    def query_block(b, carry):
        rows = block_rows(b)
        product = jnp.zeros((QB, half), jnp.float32)
        for n in range(parts):
            product += jnp.dot(
                tok[n, rows, :], w[pl.ds(n * width, width), half : 2 * half],
                preferred_element_type=jnp.float32,
            )
        for h in range(half // HD):
            value = product[:, h * HD : (h + 1) * HD]
            query_all[rows, h * HD : (h + 1) * HD] = rotated(value, rows).astype(jnp.bfloat16)
        return carry

    next_x = lax.rem(x + 1, NX) * NY + y
    next_y = x * NY + lax.rem(y + 1, NY)
    last_y = x * NY + lax.rem(y + NY - 1, NY)
    inner = (y == 1) | (y == 2)

    def move(kind, source, slot, where, c):
        rows = block_rows(c)
        return pltpu.make_async_remote_copy(
            src_ref=held.at[source, rows], dst_ref=held.at[slot, rows],
            send_sem=send.at[kind, c], recv_sem=recv.at[slot, c],
            device_id={"wide": where}, device_id_type=MESH,
        )

    def along_x(c):
        return move(0, 0, 4, next_x, c)

    def up(source, c):
        return move(1, source, 1, next_y, c)

    def down(source, c):
        return move(2, source, 3, last_y, c)

    def pass_up(c):
        return move(3, 1, 2, next_y, c)

    def pass_down(c):
        return move(4, 3, 2, last_y, c)

    def begin(c, carry):
        along_x(c).start()

        @pl.when(y < NY - 1)
        def _():
            up(0, c).start()

        @pl.when(y == 0)
        def _():
            down(0, c).start()

        return carry

    def weigh(d, g, qb, first, size, diagonal=False):
        qrows = block_rows(qb)
        krows = pl.ds(pl.multiple_of(first, 256), size)
        query = jnp.concatenate(
            [query_all[qrows, lanes(g * 256, 128)], query_all[qrows, lanes(g * 256 + 128, 128)]],
            axis=0,
        )
        keys = held[d, krows, lanes(g * 256, 128)]
        values = held[d, krows, lanes(g * 256 + 128, 128)]
        scores = lax.dot_general(
            query, keys, (((1,), (1,)), ((), ())), preferred_element_type=jnp.float32
        )
        floor = floor_ref[qrows, :] - ((REACH - d) * tokens + first)
        floor = jnp.concatenate([floor] * (size // 128), axis=1)
        column = lax.broadcasted_iota(jnp.int32, (QB, size), 1)
        allowed = column >= floor
        if diagonal:
            allowed = allowed & (column <= lax.broadcasted_iota(jnp.int32, (QB, size), 0))
        weights = jnp.exp2(jnp.tanh(scores * PRE) * POST)
        weights = jnp.concatenate(
            [
                jnp.where(allowed, weights[:QB], 0.0).astype(jnp.bfloat16),
                jnp.where(allowed, weights[QB:], 0.0).astype(jnp.bfloat16),
            ],
            axis=0,
        )
        wide_values = jnp.concatenate([values, jnp.ones_like(values)], axis=1)
        return jnp.dot(weights, wide_values, preferred_element_type=jnp.float32)

    def chunk(d, g, qb, first, size, diagonal=False, fresh=False):
        product = weigh(d, g, qb, first, size, diagonal)
        slot = g * blocks + qb
        if fresh:
            total[slot] = product
        else:
            total[slot] += product

    def own_pair(t, carry):
        g, qb = lax.div(t, blocks), lax.rem(t, blocks)
        chunk(0, g, qb, qb * QB, QB, diagonal=True, fresh=True)
        lax.fori_loop(0, qb, lambda k, c: (chunk(0, g, qb, k * QB, QB), c)[1], 0)
        return carry

    def segment(d, k, pairs):
        def pair(t, carry):
            first = weigh(d, 0, t, k * QB, QB)
            second = weigh(d, 1, t, k * QB, QB)
            total[t] += first
            total[blocks + t] += second
            return carry

        lax.fori_loop(0, pairs, pair, 0)

    for b in range(blocks):
        lax.fori_loop(b, b + 1, key_block, 0)
        lax.fori_loop(b, b + 1, begin, 0)
        if b == 1:
            wave_pass(2, 2)
        if b == 2:
            wave_pass(2, 3)
    wave_pass(2, 4)
    save = pltpu.make_async_copy(held.at[0], kv_hbm, out_sem.at[0])
    save.start()

    def pump(c):
        along_x(c).wait_recv()

        @pl.when(y == NY - 1)
        def _():
            up(4, c).start()

        @pl.when(y > 0)
        def _():
            down(4, c).start()

    wave_end(1)
    lax.fori_loop(0, 2, query_block, 0)
    pump(0)
    lax.fori_loop(2, blocks, query_block, 0)
    pump(1)
    lax.fori_loop(0, blocks, own_pair, 0)
    pump(2)
    lax.fori_loop(blocks, 2 * blocks, own_pair, 0)
    pump(3)

    def step(i, carry):
        @pl.when(i < blocks)
        def _():
            up(0, i).wait_recv()

            @pl.when(inner)
            def _():
                pass_up(i).start()

            segment(4, i, i + 1)
            down(0, i).wait_recv()

            @pl.when(inner)
            def _():
                pass_down(i).start()

            segment(1, i, blocks)

        @pl.when(i < blocks)
        def _():
            segment(3, i, blocks)

        @pl.when(i >= 1)
        def _():
            pass_up(i - 1).wait_recv()
            segment(2, i - 1, blocks)

        return carry

    lax.fori_loop(0, blocks + 1, step, 0)

    def finish(t, carry):
        g, qb = lax.div(t, blocks), lax.rem(t, blocks)
        slot = g * blocks + qb
        result = (total[slot, :, :HD] / total[slot, :, HD:]).astype(out_ref.dtype)
        out_ref[block_rows(qb), lanes(g * 256, 128)] = result[:QB]
        out_ref[block_rows(qb), lanes(g * 256 + 128, 128)] = result[QB:]
        return carry

    lax.fori_loop(0, 2 * blocks, finish, 0)
    wave_end(2)
    save_w = pltpu.make_async_copy(w.at[:, pl.ds(2 * half, half)], w_out_hbm, out_sem.at[1])
    save_w.start()
    save.wait()
    save_meta.wait()

    def drain(c, carry):
        along_x(c).wait_send()
        up(0, c).wait_send()
        down(0, c).wait_send()

        @pl.when(inner)
        def _():
            pass_up(c).wait_send()
            pass_down(c).wait_send()

        return carry

    lax.fori_loop(0, blocks, drain, 0)
    for copy in started:
        copy.wait_send()
    for wave in range(WAVES):
        for part in (0, 1):
            for group in range(5):
                for kind in range(4):
                    hop(wave, part, group, kind).wait_send()
    save_w.wait()


def front(tokens, w_query, w_key, w_value, w_out_rows, meta, gain, ids, freq):
    rows, width = tokens.shape
    shard, half = w_query.shape
    columns = WAVES * half
    vmem_spec = pl.BlockSpec(memory_space=pltpu.VMEM)
    any_spec = pl.BlockSpec(memory_space=pl.ANY)
    dma = pltpu.SemaphoreType.DMA
    bf16 = jnp.bfloat16
    blocks = rows // QB
    return pl.pallas_call(
        front_kernel,
        out_shape=(
            jax.ShapeDtypeStruct((rows, half), bf16),
            jax.ShapeDtypeStruct((rows, half), bf16),
            jax.ShapeDtypeStruct((16 * shard, half), bf16),
            jax.ShapeDtypeStruct((16,) + meta.shape, meta.dtype),
        ),
        in_specs=[any_spec] * 5 + [vmem_spec] * 4,
        out_specs=(vmem_spec, any_spec, any_spec, any_spec),
        scratch_shapes=[
            pltpu.VMEM((8, rows, width), bf16),
            pltpu.VMEM((16 * shard, columns), bf16),
            pltpu.VMEM((16,) + meta.shape, jnp.int32),
            pltpu.VMEM((8,) + gain.shape, bf16),
            pltpu.VMEM((rows, 128), jnp.float32),
            pltpu.VMEM((rows, 128), jnp.float32),
            pltpu.VMEM((rows, 128), jnp.int32),
            pltpu.VMEM((rows, half), bf16),
            pltpu.VMEM((REACH + 1, rows, half), bf16),
            pltpu.VMEM((8, 2 * QB, 256), jnp.float32),
            dma((3, 2, 5, 4)), dma((3, 2, 5, 4)), dma((6,)), dma((6,)), dma((7,)), dma((7,)),
            dma((16,)), dma((16,)), dma((8,)), dma((8,)), dma((9,)),
            dma((3,)), dma((5, blocks)), dma((REACH + 1, blocks)),
        ],
        cost_estimate=pl.CostEstimate(
            flops=4 * rows * 4352 * 128 * 8, bytes_accessed=32 << 20,
            transcendentals=8 * rows * 4352,
        ),
        compiler_params=pltpu.CompilerParams(
            vmem_limit_bytes=60 << 20, has_side_effects=True
        ),
        name="front",
    )(tokens, w_query, w_key, w_value, w_out_rows, meta, gain, ids, freq)


def tail_kernel(
    attn_ref, tok_ref, gain_ref, w_hbm, pages_hbm,
    mixed_ref, pages_in,
    w, w_sem, give, take, stage, far, near, kept, squares,
    p_send, p_recv, own_sem, c_send, c_recv, f_send, f_recv, n_send, n_recv, s_send, s_recv,
):
    wide = lax.axis_index("wide")
    narrow = lax.axis_index("narrow")
    z, core = lax.div(narrow, 2), lax.rem(narrow, 2)
    count = NX * NY
    tokens = attn_ref.shape[0]
    mid = tokens // 2
    low, high = pl.ds(0, mid), pl.ds(mid, mid)
    sibling = {"narrow": z * 2 + (1 - core)}

    def at_z(step):
        return lax.rem(z + step + NZ, NZ)

    def remote(src, dst, send, recv, where):
        copy = pltpu.make_async_remote_copy(
            src_ref=src, dst_ref=dst, send_sem=send, recv_sem=recv,
            device_id=where, device_id_type=MESH,
        )
        copy.start()
        return copy

    pages = [
        remote(
            pages_hbm.at[lax.rem(wide + other, count)], pages_in.at[wide],
            p_send.at[other], p_recv.at[other], {"wide": lax.rem(wide + other, count)},
        )
        for other in range(1, count)
    ]
    own = pltpu.make_async_copy(pages_hbm.at[wide], pages_in.at[wide], own_sem)
    own.start()

    steps = (2, 1, -1, 0)
    depth, width = attn_ref.shape[1], tok_ref.shape[1]
    loads = []
    for slot in range(8):
        index = at_z(steps[slot % 4]) * 2 + ((1 - core) if slot < 4 else core)
        source = pl.ds(pl.multiple_of(index * width, width), width)
        loads.append(
            pltpu.make_async_copy(
                w_hbm.at[source, pl.ds(w_hbm.shape[1] - depth, depth)], w.at[slot], w_sem.at[slot]
            )
        )
        loads[-1].start()

    def term(slot, rows):
        return lax.dot_general(
            attn_ref[rows, :], w[slot], (((1,), (1,)), ((), ())),
            preferred_element_type=jnp.float32,
        ).astype(jnp.bfloat16)

    def over_rows(body, first=0, size=tokens):
        def step(b, carry):
            body(pl.ds(pl.multiple_of(first + b * QB, QB), QB))
            return carry

        lax.fori_loop(0, size // QB, step, 0)

    passes = {}

    def hand_over(i, part):
        def fill(rows):
            give[i, rows, :] = term(i, rows)

        over_rows(fill, part * mid, mid)
        span = pl.ds(part * mid, mid)
        passes[i, part] = remote(
            give.at[i, span], take.at[i, span], c_send.at[i, part], c_recv.at[i, part], sibling
        )

    def own_sum(i, rows):
        mine = term(4 + i, rows)
        return mine.astype(jnp.float32) + take[i, rows, :].astype(jnp.float32)

    def put(i):
        def body(rows):
            stage[i, rows, :] = own_sum(i, rows).astype(jnp.bfloat16)

        return body

    ahead, behind = {"narrow": at_z(1) * 2 + core}, {"narrow": at_z(-1) * 2 + core}
    loads[0].wait()
    hand_over(0, 0)
    hand_over(0, 1)
    loads[1].wait()
    hand_over(1, 1)
    loads[4].wait()
    passes[0, 0].wait_recv()
    over_rows(put(0), 0, mid)
    far_up = remote(stage.at[0, low], far.at[0], f_send.at[0], f_recv.at[0], ahead)
    passes[0, 1].wait_recv()
    over_rows(put(0), mid, mid)
    far_down = remote(stage.at[0, high], far.at[1], f_send.at[1], f_recv.at[1], behind)
    loads[2].wait()
    hand_over(2, 0)
    loads[5].wait()
    passes[1, 1].wait_recv()
    over_rows(put(1), mid, mid)
    near_a = remote(stage.at[1, high], near.at[0, high], n_send.at[0], n_recv.at[0], ahead)
    loads[6].wait()
    passes[2, 0].wait_recv()
    over_rows(put(2), 0, mid)
    near_b = remote(stage.at[2, low], near.at[1, low], n_send.at[1], n_recv.at[1], behind)
    hand_over(1, 0)
    hand_over(2, 1)
    passes[1, 0].wait_recv()
    passes[2, 1].wait_recv()

    far_up.wait_recv()

    def with_far_up(rows):
        stage[1, rows, :] = (own_sum(1, rows) + far[0, rows, :].astype(jnp.float32)).astype(
            jnp.bfloat16
        )

    over_rows(with_far_up, 0, mid)
    near_c = remote(stage.at[1, low], near.at[0, low], n_send.at[2], n_recv.at[2], ahead)
    far_down.wait_recv()

    def with_far_down(b, carry):
        rows = pl.ds(pl.multiple_of(mid + b * QB, QB), QB)
        source = pl.ds(pl.multiple_of(b * QB, QB), QB)
        stage[2, rows, :] = (own_sum(2, rows) + far[1, source, :].astype(jnp.float32)).astype(
            jnp.bfloat16
        )
        return carry

    lax.fori_loop(0, mid // QB, with_far_down, 0)
    near_d = remote(stage.at[2, high], near.at[1, high], n_send.at[3], n_recv.at[3], behind)
    loads[3].wait()
    loads[7].wait()
    hand_over(3, 0)
    hand_over(3, 1)
    passes[3, 0].wait_recv()
    passes[3, 1].wait_recv()

    def keep(rows):
        kept[rows, :] = own_sum(3, rows)

    over_rows(keep)
    for copy in (near_a, near_b, near_c, near_d):
        copy.wait_recv()

    ones = jnp.ones((8, tok_ref.shape[1]), jnp.float32)

    def finish(rows):
        value = (
            kept[rows, :]
            + near[0, rows, :].astype(jnp.float32)
            + near[1, rows, :].astype(jnp.float32)
        )
        kept[rows, :] = value
        squares[0, :, rows] = lax.dot_general(
            ones, value * value, (((1,), (1,)), ((), ())),
            precision=lax.Precision.HIGHEST, preferred_element_type=jnp.float32,
        )

    over_rows(finish)
    sums = [
        remote(
            squares.at[0], squares.at[other], s_send.at[other], s_recv.at[other],
            {"narrow": lax.rem(narrow + other, NZ * 2)},
        )
        for other in range(1, NZ * 2)
    ]
    for copy in sums:
        copy.wait_recv()
    pick = jnp.full((8, 128), 0.125, jnp.float32)

    def emit(rows):
        whole = squares[0, :, rows]
        for other in range(1, NZ * 2):
            whole += squares[other, :, rows]
        column = lax.dot_general(
            whole, pick, (((0,), (0,)), ((), ())),
            precision=lax.Precision.HIGHEST, preferred_element_type=jnp.float32,
        )
        scale = lax.rsqrt(column / D + NORM_EPSILON)[:, 0:1]
        mixed_ref[rows, :] = (
            tok_ref[rows, :].astype(jnp.float32)
            + kept[rows, :] * scale * gain_ref[0:1, :].astype(jnp.float32)
        ).astype(jnp.bfloat16)

    over_rows(emit)
    for copy in pages:
        copy.wait_recv()
    own.wait()
    for copy in pages + list(passes.values()) + sums:
        copy.wait_send()
    for copy in (far_up, far_down, near_a, near_b, near_c, near_d):
        copy.wait_send()


def tail(attn, w_all, tokens, post_gain, outgoing):
    rows, width = tokens.shape
    vmem_spec = pl.BlockSpec(memory_space=pltpu.VMEM)
    any_spec = pl.BlockSpec(memory_space=pl.ANY)
    dma = pltpu.SemaphoreType.DMA
    bf16 = jnp.bfloat16
    return pl.pallas_call(
        tail_kernel,
        out_shape=(
            jax.ShapeDtypeStruct(tokens.shape, bf16),
            jax.ShapeDtypeStruct(outgoing.shape, bf16),
        ),
        in_specs=[vmem_spec] * 3 + [any_spec] * 2,
        out_specs=(vmem_spec, any_spec),
        scratch_shapes=[
            pltpu.VMEM((8, width, attn.shape[1]), bf16),
            dma((8,)),
            pltpu.VMEM((4, rows, width), bf16),
            pltpu.VMEM((4, rows, width), bf16),
            pltpu.VMEM((3, rows, width), bf16),
            pltpu.VMEM((2, rows // 2, width), bf16),
            pltpu.VMEM((2, rows, width), bf16),
            pltpu.VMEM((rows, width), jnp.float32),
            pltpu.VMEM((8, 8, rows), jnp.float32),
            dma((16,)), dma((16,)), dma, dma((4, 2)), dma((4, 2)), dma((2,)), dma((2,)),
            dma((4,)), dma((4,)), dma((8,)), dma((8,)),
        ],
        cost_estimate=pl.CostEstimate(
            flops=2 * rows * 512 * D, bytes_accessed=24 << 20, transcendentals=0
        ),
        compiler_params=pltpu.CompilerParams(
            vmem_limit_bytes=56 << 20, has_side_effects=True
        ),
        name="tail",
    )(attn, tokens, post_gain, w_all, outgoing)


def local(tokens, segment_ids, page_table, pre_gain, post_gain, w_query, w_key, w_value, w_out):
    tok_w = tokens.shape[0]
    shard_count = lax.axis_size("wide")
    shard_index = lax.axis_index("wide")
    block_count = page_table.shape[0]
    pairs_here = w_key.shape[1] // HD
    seg_rows = segment_ids.reshape(8, tok_w // 8)
    table_row = jnp.pad(page_table[None, :], ((0, 7), (0, tok_w // 8 - block_count)))
    meta = jnp.concatenate([seg_rows, table_row], axis=0)
    gain_in = jnp.broadcast_to(pre_gain[None, :], (16, pre_gain.shape[0]))
    half_width = HD // 2
    lane = np.arange(HD)
    inverse_freq = np.exp(-math.log(10000.0) * 2.0 * (lane % half_width) / HD)
    signs = np.where(lane < half_width, -1.0, 1.0)
    freq = jnp.asarray(np.stack([inverse_freq] + [signs] * 7).astype(np.float32))
    ids = jnp.broadcast_to(segment_ids[:, None], (tok_w, 128))
    attn_out, flat, w_all, meta_all = front(
        tokens, w_query, w_key, w_value, jnp.transpose(w_out), meta, gain_in, ids, freq
    )
    table_all = meta_all[:, 8, :block_count].reshape(-1)

    page_len = tok_w // block_count
    token_blocks = flat.reshape(block_count, page_len, pairs_here, 2 * HD)
    owners = page_table // block_count
    shard_ids = jnp.arange(shard_count, dtype=jnp.int32)
    send_pick = (owners[None, :] == shard_ids[:, None]).astype(jnp.bfloat16)
    outgoing = jnp.einsum(
        "sj,jpgc->sgpc", send_pick, token_blocks, preferred_element_type=jnp.float32
    ).astype(jnp.bfloat16)
    mixed, incoming = tail(
        attn_out, w_all, tokens, post_gain[None, :], outgoing
    )
    my_pages = shard_index * block_count + jnp.arange(block_count, dtype=jnp.int32)
    found_page = table_all[None, :] == my_pages[:, None]
    anchor = jnp.sum(
        jnp.where(
            found_page, jnp.arange(table_all.shape[0], dtype=jnp.int32)[None, :] // block_count, 0
        ),
        axis=1,
    )
    take_pick = (anchor[:, None] == shard_ids[None, :]).astype(jnp.bfloat16)
    kv_pages = jnp.einsum(
        "qs,sgpc->qgpc", take_pick, incoming, preferred_element_type=jnp.float32
    ).astype(jnp.bfloat16)
    return (mixed, kv_pages)


def solution(mesh):
    return jax.shard_map(
        local,
        mesh=mesh,
        in_specs=(
            P("wide", "narrow"),
            P("wide"),
            P("wide"),
            P("narrow"),
            P("narrow"),
            P("wide", "narrow"),
            P("wide", "narrow"),
            P("wide", "narrow"),
            P("narrow", "wide"),
        ),
        out_specs=(P("wide", "narrow"), P("wide", "narrow", None, None)),
        check_vma=False,
    )
```

```python
import math

import jax
import jax.numpy as jnp
import numpy as np
from jax import lax
from jax.experimental import pallas as pl
from jax.experimental.pallas import tpu as pltpu
from jax.sharding import PartitionSpec as P

D = 4608
HD = 128
WINDOW = 4096
SEGS = 8

SOFT_CAP = 50.0
QUERY_SCALE = 1.0 / 12.0
NORM_EPSILON = 1e-06
NX, NY, NZ = 4, 4, 4
MESH = pl.DeviceIdType.MESH
PRE = QUERY_SCALE / SOFT_CAP
POST = SOFT_CAP * math.log2(math.e)


QB = 256
REACH = 4
WAVES = 3


def lanes(start, size):
    return pl.ds(pl.multiple_of(start, 128), size)


def front_kernel(
    tok_ref, wq_ref, wk_ref, wv_ref, wo_ref, meta_ref, gain_ref, ids_ref, freq_ref,
    out_ref, kv_hbm, w_out_hbm, meta_out,
    tok, w, meta_all, gain_all, cos_ref, sin_ref, floor_ref, query_all, held, total,
    w_send, w_recv, z_send, z_recv, c_send, c_recv, m_send, m_recv, g_send, g_recv, own_sem,
    out_sem, send, recv,
):
    wide = lax.axis_index("wide")
    narrow = lax.axis_index("narrow")
    x, y = lax.div(wide, NY), lax.rem(wide, NY)
    z, core = lax.div(narrow, 2), lax.rem(narrow, 2)
    shard = wq_ref.shape[0]
    part_rows = (shard * 7 // 18, shard - shard * 7 // 18)
    part_first = (0, part_rows[0])
    half = wq_ref.shape[1]
    parts, tokens, width = tok.shape
    blocks = tokens // QB

    def block_rows(b):
        return pl.ds(pl.multiple_of(b * QB, QB), QB)

    def ring(position, count, step):
        return lax.rem(position + step + count, count)

    started = []

    def remote(src, dst, send_sem, recv_sem, where):
        copy = pltpu.make_async_remote_copy(
            src_ref=src, dst_ref=dst, send_sem=send_sem, recv_sem=recv_sem,
            device_id=where, device_id_type=MESH,
        )
        copy.start()
        started.append(copy)
        return copy

    def peer(part, stage, step):
        if (part == 0) == (stage == 0):
            return {"wide": ring(x, NX, step) * NY + y}
        return {"wide": x * NY + ring(y, NY, step)}

    def rows_of(part, along, across):
        if part == 0:
            block = ring(x, NX, along) * NY + ring(y, NY, across)
        else:
            block = ring(x, NX, across) * NY + ring(y, NY, along)
        return pl.ds(pl.multiple_of(block * shard + part_first[part], 16), part_rows[part])

    def hop(wave, part, group, kind):
        where = peer(part, 0 if group == 0 else 1, 1 if kind % 2 == 0 else -1)
        passed = (0, 0, -1, 1)[kind]
        if group == 0:
            there = rows_of(part, passed, 0)
        else:
            there = rows_of(part, (0, -1, 1, 2)[group - 1], passed)
        if kind < 2:
            span = pl.ds(wave * half, half)
        else:
            span = pl.ds(wave * half + (kind - 2) * (half // 2), half // 2)
        return pltpu.make_async_remote_copy(
            src_ref=w.at[there, span], dst_ref=w.at[there, span],
            send_sem=w_send.at[wave, part, group, kind],
            recv_sem=w_recv.at[wave, part, group, kind],
            device_id=where, device_id_type=MESH,
        )

    def go(wave, part, group, kind):
        hop(wave, part, group, kind).start()

    def got(wave, part, group, kind):
        hop(wave, part, group, kind).wait_recv()

    def wave_own(wave):
        for group in (0, 1):
            for part in (0, 1):
                go(wave, part, group, 0)
                go(wave, part, group, 1)

    def wave_first(wave):
        for kind, group in ((0, 2), (1, 3)):
            for part in (0, 1):
                got(wave, part, 0, kind)
                go(wave, part, 0, 2 + kind)
                go(wave, part, group, 0)
                go(wave, part, group, 1)

    def wave_pass(wave, group):
        for part in (0, 1):
            got(wave, part, group, 0)
            go(wave, part, group, 2)
            got(wave, part, group, 1)
            go(wave, part, group, 3)

    def wave_far(wave):
        for part in (0, 1):
            got(wave, part, 0, 2)
            got(wave, part, 0, 3)
            go(wave, part, 4, 0)
            go(wave, part, 4, 1)

    def wave_end(wave):
        for group in range(1, 5):
            for part in (0, 1):
                got(wave, part, group, 2)
                got(wave, part, group, 3)

    toks = {}

    def zgo(kind, index, src, span):
        where = {"narrow": ring(z, NZ, 1 if kind % 2 == 0 else -1) * 2 + core}
        toks[kind] = remote(src, tok.at[index, span], z_send.at[kind], z_recv.at[kind], where)

    pair = {}

    def cgo(kind, index, src, span):
        where = {"narrow": z * 2 + (1 - core)}
        pair[kind] = remote(src, tok.at[index, span], c_send.at[kind], c_recv.at[kind], where)

    every = pl.ds(0, tokens)
    low, high = pl.ds(0, tokens // 2), pl.ds(tokens // 2, tokens // 2)

    def zblock(step):
        return ring(z, NZ, step) * 2 + core

    own_rows = pl.ds(pl.multiple_of(wide * shard, 16), shard)
    pieces = [(wq_ref, half), (wo_ref, 2 * half)]
    for g in range(2):
        there = slice(g * HD, (g + 1) * HD)
        pieces.append((wk_ref.at[:, there], g * 256))
        pieces.append((wv_ref.at[:, there], g * 256 + HD))
    loads = [
        pltpu.make_async_copy(
            piece, w.at[own_rows, pl.ds(column, piece.shape[1])], own_sem.at[3 + i]
        )
        for i, (piece, column) in enumerate(pieces)
    ]
    for copy in loads[2:] + loads[:2]:
        copy.start()
    small = []
    for other in range(1, NX * NY):
        target = lax.rem(wide + other, NX * NY)
        small.append(remote(
            meta_ref, meta_all.at[wide], m_send.at[other], m_recv.at[other], {"wide": target}))
    for other in range(1, NZ * 2):
        target = lax.rem(narrow + other, NZ * 2)
        small.append(remote(
            gain_ref, gain_all.at[narrow], g_send.at[other], g_recv.at[other], {"narrow": target}))
    zgo(0, narrow, tok_ref.at[low], low)
    zgo(1, narrow, tok_ref.at[high], high)
    for copy in loads:
        copy.wait()
    wave_own(0)
    zgo(4, narrow, tok_ref.at[high], high)
    zgo(5, narrow, tok_ref.at[low], low)
    cgo(0, narrow, tok_ref, every)
    local = [
        pltpu.make_async_copy(tok_ref, tok.at[narrow], own_sem.at[0]),
        pltpu.make_async_copy(meta_ref, meta_all.at[wide], own_sem.at[1]),
        pltpu.make_async_copy(gain_ref, gain_all.at[narrow], own_sem.at[2]),
    ]
    for copy in local:
        copy.start()
    wave_own(1)
    wave_first(0)

    for copy in small:
        copy.wait_recv()
    for copy in local:
        copy.wait()
    save_meta = pltpu.make_async_copy(meta_all, meta_out, out_sem.at[2])
    save_meta.start()
    first_token = wide * tokens
    all_ids = meta_all[:, 0:8, :]
    firsts = [
        jnp.sum((all_ids < label).astype(jnp.float32)).astype(jnp.int32)
        for label in range(1, SEGS)
    ]

    def tables(b, carry):
        rows = block_rows(b)
        ids = ids_ref[rows, :]
        start = jnp.zeros((QB, 128), jnp.int32)
        for label in range(1, SEGS):
            start = jnp.where(ids == label, firsts[label - 1], start)
        index = first_token + b * QB + lax.broadcasted_iota(jnp.int32, (QB, 128), 0)
        angle = (index - start).astype(jnp.float32) * freq_ref[0:1, :]
        cos_ref[rows, :] = jnp.cos(angle)
        sin_ref[rows, :] = jnp.sin(angle) * freq_ref[1:2, :]
        floor_ref[rows, :] = jnp.maximum(start, index - WINDOW + 1) - (first_token - WINDOW)
        return carry

    wave_pass(0, 1)
    wave_far(0)
    toks[0].wait_recv()
    zgo(2, zblock(-1), tok.at[zblock(-1), low], low)
    cgo(1, zblock(-1), tok.at[zblock(-1), low], low)
    toks[1].wait_recv()
    zgo(3, zblock(1), tok.at[zblock(1), high], high)
    cgo(2, zblock(1), tok.at[zblock(1), high], high)
    wave_own(2)
    lax.fori_loop(0, blocks, tables, 0)
    wave_pass(0, 2)
    wave_pass(0, 3)
    wave_pass(0, 4)
    wave_first(1)
    wave_pass(1, 1)
    wave_far(1)
    toks[4].wait_recv()
    cgo(5, zblock(-1), tok.at[zblock(-1), high], high)
    toks[5].wait_recv()
    cgo(6, zblock(1), tok.at[zblock(1), low], low)
    wave_pass(1, 2)
    wave_pass(1, 3)
    wave_pass(1, 4)
    wave_first(2)
    toks[2].wait_recv()
    cgo(3, zblock(2), tok.at[zblock(2), low], low)
    toks[3].wait_recv()
    cgo(4, zblock(2), tok.at[zblock(2), high], high)
    wave_end(0)
    wave_pass(2, 1)
    wave_far(2)
    for kind in range(7):
        pair[kind].wait_recv()
    for kind in range(7):
        pair[kind].wait_send()
    for kind in range(6):
        toks[kind].wait_send()
    done = [id(copy) for copy in list(pair.values()) + list(toks.values())]
    started[:] = [copy for copy in started if id(copy) not in done]

    def rotated(value, rows):
        return value * cos_ref[rows, :] + pltpu.roll(value, HD // 2, 1) * sin_ref[rows, :]

    def key_block(b, carry):
        rows = block_rows(b)
        squares = jnp.zeros((QB, 1), jnp.float32)
        for n in range(parts):
            piece = tok[n, rows, :].astype(jnp.float32)
            squares += jnp.sum(piece * piece, axis=1, keepdims=True)
        scale = lax.rsqrt(squares / D + NORM_EPSILON)
        product = jnp.zeros((QB, half), jnp.float32)
        for n in range(parts):
            piece = tok[n, rows, :].astype(jnp.float32)
            normed = (piece * scale * gain_all[n, 0:1, :].astype(jnp.float32)).astype(jnp.bfloat16)
            tok[n, rows, :] = normed
            product += jnp.dot(
                normed, w[pl.ds(n * width, width), 0:half], preferred_element_type=jnp.float32
            )
        for g in range(2):
            key = product[:, g * 256 : g * 256 + HD]
            held[0, rows, g * 256 : g * 256 + HD] = rotated(key, rows).astype(jnp.bfloat16)
            held[0, rows, g * 256 + HD : g * 256 + 256] = product[
                :, g * 256 + HD : g * 256 + 256
            ].astype(jnp.bfloat16)
        return carry

    def query_block(b, carry):
        rows = block_rows(b)
        product = jnp.zeros((QB, half), jnp.float32)
        for n in range(parts):
            product += jnp.dot(
                tok[n, rows, :], w[pl.ds(n * width, width), half : 2 * half],
                preferred_element_type=jnp.float32,
            )
        for h in range(half // HD):
            value = product[:, h * HD : (h + 1) * HD]
            query_all[rows, h * HD : (h + 1) * HD] = rotated(value, rows).astype(jnp.bfloat16)
        return carry

    next_x = lax.rem(x + 1, NX) * NY + y
    next_y = x * NY + lax.rem(y + 1, NY)
    last_y = x * NY + lax.rem(y + NY - 1, NY)
    inner = (y == 1) | (y == 2)

    def move(kind, source, slot, where, c):
        rows = block_rows(c)
        return pltpu.make_async_remote_copy(
            src_ref=held.at[source, rows], dst_ref=held.at[slot, rows],
            send_sem=send.at[kind, c], recv_sem=recv.at[slot, c],
            device_id={"wide": where}, device_id_type=MESH,
        )

    def along_x(c):
        return move(0, 0, 4, next_x, c)

    def up(source, c):
        return move(1, source, 1, next_y, c)

    def down(source, c):
        return move(2, source, 3, last_y, c)

    def pass_up(c):
        return move(3, 1, 2, next_y, c)

    def pass_down(c):
        return move(4, 3, 2, last_y, c)

    def begin(c, carry):
        along_x(c).start()

        @pl.when(y < NY - 1)
        def _():
            up(0, c).start()

        @pl.when(y == 0)
        def _():
            down(0, c).start()

        return carry

    def weigh(d, g, qb, first, size, diagonal=False):
        qrows = block_rows(qb)
        krows = pl.ds(pl.multiple_of(first, 256), size)
        query = jnp.concatenate(
            [query_all[qrows, lanes(g * 256, 128)], query_all[qrows, lanes(g * 256 + 128, 128)]],
            axis=0,
        )
        keys = held[d, krows, lanes(g * 256, 128)]
        values = held[d, krows, lanes(g * 256 + 128, 128)]
        scores = lax.dot_general(
            query, keys, (((1,), (1,)), ((), ())), preferred_element_type=jnp.float32
        )
        floor = floor_ref[qrows, :] - ((REACH - d) * tokens + first)
        floor = jnp.concatenate([floor] * (size // 128), axis=1)
        column = lax.broadcasted_iota(jnp.int32, (QB, size), 1)
        allowed = column >= floor
        if diagonal:
            allowed = allowed & (column <= lax.broadcasted_iota(jnp.int32, (QB, size), 0))
        weights = jnp.exp2(jnp.tanh(scores * PRE) * POST)
        weights = jnp.concatenate(
            [
                jnp.where(allowed, weights[:QB], 0.0).astype(jnp.bfloat16),
                jnp.where(allowed, weights[QB:], 0.0).astype(jnp.bfloat16),
            ],
            axis=0,
        )
        wide_values = jnp.concatenate([values, jnp.ones_like(values)], axis=1)
        return jnp.dot(weights, wide_values, preferred_element_type=jnp.float32)

    def chunk(d, g, qb, first, size, diagonal=False, fresh=False):
        product = weigh(d, g, qb, first, size, diagonal)
        slot = g * blocks + qb
        if fresh:
            total[slot] = product
        else:
            total[slot] += product

    def own_pair(t, carry):
        g, qb = lax.div(t, blocks), lax.rem(t, blocks)
        chunk(0, g, qb, qb * QB, QB, diagonal=True, fresh=True)
        lax.fori_loop(0, qb, lambda k, c: (chunk(0, g, qb, k * QB, QB), c)[1], 0)
        return carry

    def segment(d, k, pairs):
        def pair(t, carry):
            first = weigh(d, 0, t, k * QB, QB)
            second = weigh(d, 1, t, k * QB, QB)
            total[t] += first
            total[blocks + t] += second
            return carry

        lax.fori_loop(0, pairs, pair, 0)

    for b in range(blocks):
        lax.fori_loop(b, b + 1, key_block, 0)
        lax.fori_loop(b, b + 1, begin, 0)
        if b == 1:
            wave_pass(2, 2)
        if b == 2:
            wave_pass(2, 3)
    wave_pass(2, 4)
    saves = []
    for j in range(kv_hbm.shape[0]):
        for g in range(2):
            saves.append(pltpu.make_async_copy(
                held.at[0, pl.ds(j * 128, 128), pl.ds(g * 256, 256)], kv_hbm.at[j, g],
                out_sem.at[3 + 2 * j + g]))
            saves[-1].start()

    def pump(c):
        along_x(c).wait_recv()

        @pl.when(y == NY - 1)
        def _():
            up(4, c).start()

        @pl.when(y > 0)
        def _():
            down(4, c).start()

    wave_end(1)
    lax.fori_loop(0, 2, query_block, 0)
    pump(0)
    lax.fori_loop(2, blocks, query_block, 0)
    pump(1)
    lax.fori_loop(0, blocks, own_pair, 0)
    pump(2)
    lax.fori_loop(blocks, 2 * blocks, own_pair, 0)
    pump(3)

    def step(i, carry):
        @pl.when(i < blocks)
        def _():
            up(0, i).wait_recv()

            @pl.when(inner)
            def _():
                pass_up(i).start()

            segment(4, i, i + 1)
            down(0, i).wait_recv()

            @pl.when(inner)
            def _():
                pass_down(i).start()

            segment(1, i, blocks)

        @pl.when(i < blocks)
        def _():
            segment(3, i, blocks)

        @pl.when(i >= 1)
        def _():
            pass_up(i - 1).wait_recv()
            segment(2, i - 1, blocks)

        return carry

    lax.fori_loop(0, blocks + 1, step, 0)

    def finish(t, carry):
        g, qb = lax.div(t, blocks), lax.rem(t, blocks)
        slot = g * blocks + qb
        result = (total[slot, :, :HD] / total[slot, :, HD:]).astype(out_ref.dtype)
        out_ref[block_rows(qb), lanes(g * 256, 128)] = result[:QB]
        out_ref[block_rows(qb), lanes(g * 256 + 128, 128)] = result[QB:]
        return carry

    lax.fori_loop(0, 2 * blocks, finish, 0)
    wave_end(2)
    save_w = pltpu.make_async_copy(w.at[:, pl.ds(2 * half, half)], w_out_hbm, out_sem.at[1])
    save_w.start()
    for save in saves:
        save.wait()
    save_meta.wait()

    def drain(c, carry):
        along_x(c).wait_send()
        up(0, c).wait_send()
        down(0, c).wait_send()

        @pl.when(inner)
        def _():
            pass_up(c).wait_send()
            pass_down(c).wait_send()

        return carry

    lax.fori_loop(0, blocks, drain, 0)
    for copy in started:
        copy.wait_send()
    for wave in range(WAVES):
        for part in (0, 1):
            for group in range(5):
                for kind in range(4):
                    hop(wave, part, group, kind).wait_send()
    save_w.wait()


def front(tokens, w_query, w_key, w_value, w_out_rows, meta, gain, ids, freq):
    rows, width = tokens.shape
    shard, half = w_query.shape
    columns = WAVES * half
    vmem_spec = pl.BlockSpec(memory_space=pltpu.VMEM)
    any_spec = pl.BlockSpec(memory_space=pl.ANY)
    dma = pltpu.SemaphoreType.DMA
    bf16 = jnp.bfloat16
    blocks = rows // QB
    return pl.pallas_call(
        front_kernel,
        out_shape=(
            jax.ShapeDtypeStruct((rows, half), bf16),
            jax.ShapeDtypeStruct((rows // 128, 2, 128, 256), bf16),
            jax.ShapeDtypeStruct((16 * shard, half), bf16),
            jax.ShapeDtypeStruct((16,) + meta.shape, meta.dtype),
        ),
        in_specs=[any_spec] * 5 + [vmem_spec] * 4,
        out_specs=(vmem_spec, any_spec, any_spec, any_spec),
        scratch_shapes=[
            pltpu.VMEM((8, rows, width), bf16),
            pltpu.VMEM((16 * shard, columns), bf16),
            pltpu.VMEM((16,) + meta.shape, jnp.int32),
            pltpu.VMEM((8,) + gain.shape, bf16),
            pltpu.VMEM((rows, 128), jnp.float32),
            pltpu.VMEM((rows, 128), jnp.float32),
            pltpu.VMEM((rows, 128), jnp.int32),
            pltpu.VMEM((rows, half), bf16),
            pltpu.VMEM((REACH + 1, rows, half), bf16),
            pltpu.VMEM((8, 2 * QB, 256), jnp.float32),
            dma((3, 2, 5, 4)), dma((3, 2, 5, 4)), dma((6,)), dma((6,)), dma((7,)), dma((7,)),
            dma((16,)), dma((16,)), dma((8,)), dma((8,)), dma((9,)),
            dma((3 + rows // 64,)), dma((5, blocks)), dma((REACH + 1, blocks)),
        ],
        cost_estimate=pl.CostEstimate(
            flops=4 * rows * 4352 * 128 * 8, bytes_accessed=32 << 20,
            transcendentals=8 * rows * 4352,
        ),
        compiler_params=pltpu.CompilerParams(
            vmem_limit_bytes=60 << 20, has_side_effects=True
        ),
        name="front",
    )(tokens, w_query, w_key, w_value, w_out_rows, meta, gain, ids, freq)


def tail_kernel(
    attn_ref, tok_ref, gain_ref, w_hbm, pages_hbm,
    mixed_ref, pages_in,
    w, w_sem, give, take, stage, far, near, kept, squares,
    p_send, p_recv, own_sem, c_send, c_recv, f_send, f_recv, n_send, n_recv, s_send, s_recv,
):
    wide = lax.axis_index("wide")
    narrow = lax.axis_index("narrow")
    z, core = lax.div(narrow, 2), lax.rem(narrow, 2)
    count = NX * NY
    tokens = attn_ref.shape[0]
    mid = tokens // 2
    low, high = pl.ds(0, mid), pl.ds(mid, mid)
    sibling = {"narrow": z * 2 + (1 - core)}

    def at_z(step):
        return lax.rem(z + step + NZ, NZ)

    def remote(src, dst, send, recv, where):
        copy = pltpu.make_async_remote_copy(
            src_ref=src, dst_ref=dst, send_sem=send, recv_sem=recv,
            device_id=where, device_id_type=MESH,
        )
        copy.start()
        return copy

    pages = [
        remote(
            pages_hbm.at[lax.rem(wide + other, count)], pages_in.at[wide],
            p_send.at[other], p_recv.at[other], {"wide": lax.rem(wide + other, count)},
        )
        for other in range(1, count)
    ]
    own = pltpu.make_async_copy(pages_hbm.at[wide], pages_in.at[wide], own_sem)
    own.start()

    steps = (2, 1, -1, 0)
    depth, width = attn_ref.shape[1], tok_ref.shape[1]
    loads = []
    for slot in range(8):
        index = at_z(steps[slot % 4]) * 2 + ((1 - core) if slot < 4 else core)
        source = pl.ds(pl.multiple_of(index * width, width), width)
        loads.append(
            pltpu.make_async_copy(
                w_hbm.at[source, pl.ds(w_hbm.shape[1] - depth, depth)], w.at[slot], w_sem.at[slot]
            )
        )
        loads[-1].start()

    def term(slot, rows):
        return lax.dot_general(
            attn_ref[rows, :], w[slot], (((1,), (1,)), ((), ())),
            preferred_element_type=jnp.float32,
        ).astype(jnp.bfloat16)

    def over_rows(body, first=0, size=tokens):
        def step(b, carry):
            body(pl.ds(pl.multiple_of(first + b * QB, QB), QB))
            return carry

        lax.fori_loop(0, size // QB, step, 0)

    passes = {}

    def hand_over(i, part):
        def fill(rows):
            give[i, rows, :] = term(i, rows)

        over_rows(fill, part * mid, mid)
        span = pl.ds(part * mid, mid)
        passes[i, part] = remote(
            give.at[i, span], take.at[i, span], c_send.at[i, part], c_recv.at[i, part], sibling
        )

    def own_sum(i, rows):
        mine = term(4 + i, rows)
        return mine.astype(jnp.float32) + take[i, rows, :].astype(jnp.float32)

    def put(i):
        def body(rows):
            stage[i, rows, :] = own_sum(i, rows).astype(jnp.bfloat16)

        return body

    ahead, behind = {"narrow": at_z(1) * 2 + core}, {"narrow": at_z(-1) * 2 + core}
    loads[0].wait()
    hand_over(0, 0)
    hand_over(0, 1)
    loads[1].wait()
    hand_over(1, 1)
    loads[4].wait()
    passes[0, 0].wait_recv()
    over_rows(put(0), 0, mid)
    far_up = remote(stage.at[0, low], far.at[0], f_send.at[0], f_recv.at[0], ahead)
    passes[0, 1].wait_recv()
    over_rows(put(0), mid, mid)
    far_down = remote(stage.at[0, high], far.at[1], f_send.at[1], f_recv.at[1], behind)
    loads[2].wait()
    hand_over(2, 0)
    loads[5].wait()
    passes[1, 1].wait_recv()
    over_rows(put(1), mid, mid)
    near_a = remote(stage.at[1, high], near.at[0, high], n_send.at[0], n_recv.at[0], ahead)
    loads[6].wait()
    passes[2, 0].wait_recv()
    over_rows(put(2), 0, mid)
    near_b = remote(stage.at[2, low], near.at[1, low], n_send.at[1], n_recv.at[1], behind)
    hand_over(1, 0)
    hand_over(2, 1)
    passes[1, 0].wait_recv()
    passes[2, 1].wait_recv()

    far_up.wait_recv()

    def with_far_up(rows):
        stage[1, rows, :] = (own_sum(1, rows) + far[0, rows, :].astype(jnp.float32)).astype(
            jnp.bfloat16
        )

    over_rows(with_far_up, 0, mid)
    near_c = remote(stage.at[1, low], near.at[0, low], n_send.at[2], n_recv.at[2], ahead)
    far_down.wait_recv()

    def with_far_down(b, carry):
        rows = pl.ds(pl.multiple_of(mid + b * QB, QB), QB)
        source = pl.ds(pl.multiple_of(b * QB, QB), QB)
        stage[2, rows, :] = (own_sum(2, rows) + far[1, source, :].astype(jnp.float32)).astype(
            jnp.bfloat16
        )
        return carry

    lax.fori_loop(0, mid // QB, with_far_down, 0)
    near_d = remote(stage.at[2, high], near.at[1, high], n_send.at[3], n_recv.at[3], behind)
    loads[3].wait()
    loads[7].wait()
    hand_over(3, 0)
    hand_over(3, 1)
    passes[3, 0].wait_recv()
    passes[3, 1].wait_recv()

    def keep(rows):
        kept[rows, :] = own_sum(3, rows)

    over_rows(keep)
    for copy in (near_a, near_b, near_c, near_d):
        copy.wait_recv()

    ones = jnp.ones((8, tok_ref.shape[1]), jnp.float32)

    def finish(rows):
        value = (
            kept[rows, :]
            + near[0, rows, :].astype(jnp.float32)
            + near[1, rows, :].astype(jnp.float32)
        )
        kept[rows, :] = value
        squares[0, :, rows] = lax.dot_general(
            ones, value * value, (((1,), (1,)), ((), ())),
            precision=lax.Precision.HIGHEST, preferred_element_type=jnp.float32,
        )

    over_rows(finish)
    sums = [
        remote(
            squares.at[0], squares.at[other], s_send.at[other], s_recv.at[other],
            {"narrow": lax.rem(narrow + other, NZ * 2)},
        )
        for other in range(1, NZ * 2)
    ]
    for copy in sums:
        copy.wait_recv()
    pick = jnp.full((8, 128), 0.125, jnp.float32)

    def emit(rows):
        whole = squares[0, :, rows]
        for other in range(1, NZ * 2):
            whole += squares[other, :, rows]
        column = lax.dot_general(
            whole, pick, (((0,), (0,)), ((), ())),
            precision=lax.Precision.HIGHEST, preferred_element_type=jnp.float32,
        )
        scale = lax.rsqrt(column / D + NORM_EPSILON)[:, 0:1]
        mixed_ref[rows, :] = (
            tok_ref[rows, :].astype(jnp.float32)
            + kept[rows, :] * scale * gain_ref[0:1, :].astype(jnp.float32)
        ).astype(jnp.bfloat16)

    over_rows(emit)
    for copy in pages:
        copy.wait_recv()
    own.wait()
    for copy in pages + list(passes.values()) + sums:
        copy.wait_send()
    for copy in (far_up, far_down, near_a, near_b, near_c, near_d):
        copy.wait_send()


def tail(attn, w_all, tokens, post_gain, outgoing):
    rows, width = tokens.shape
    vmem_spec = pl.BlockSpec(memory_space=pltpu.VMEM)
    any_spec = pl.BlockSpec(memory_space=pl.ANY)
    dma = pltpu.SemaphoreType.DMA
    bf16 = jnp.bfloat16
    return pl.pallas_call(
        tail_kernel,
        out_shape=(
            jax.ShapeDtypeStruct(tokens.shape, bf16),
            jax.ShapeDtypeStruct(outgoing.shape, bf16),
        ),
        in_specs=[vmem_spec] * 3 + [any_spec] * 2,
        out_specs=(vmem_spec, any_spec),
        scratch_shapes=[
            pltpu.VMEM((8, width, attn.shape[1]), bf16),
            dma((8,)),
            pltpu.VMEM((4, rows, width), bf16),
            pltpu.VMEM((4, rows, width), bf16),
            pltpu.VMEM((3, rows, width), bf16),
            pltpu.VMEM((2, rows // 2, width), bf16),
            pltpu.VMEM((2, rows, width), bf16),
            pltpu.VMEM((rows, width), jnp.float32),
            pltpu.VMEM((8, 8, rows), jnp.float32),
            dma((16,)), dma((16,)), dma, dma((4, 2)), dma((4, 2)), dma((2,)), dma((2,)),
            dma((4,)), dma((4,)), dma((8,)), dma((8,)),
        ],
        cost_estimate=pl.CostEstimate(
            flops=2 * rows * 512 * D, bytes_accessed=24 << 20, transcendentals=0
        ),
        compiler_params=pltpu.CompilerParams(
            vmem_limit_bytes=56 << 20, has_side_effects=True
        ),
        name="tail",
    )(attn, tokens, post_gain, w_all, outgoing)


def local(tokens, segment_ids, page_table, pre_gain, post_gain, w_query, w_key, w_value, w_out):
    tok_w = tokens.shape[0]
    shard_count = lax.axis_size("wide")
    shard_index = lax.axis_index("wide")
    block_count = page_table.shape[0]
    seg_rows = segment_ids.reshape(8, tok_w // 8)
    table_row = jnp.pad(page_table[None, :], ((0, 7), (0, tok_w // 8 - block_count)))
    meta = jnp.concatenate([seg_rows, table_row], axis=0)
    gain_in = jnp.broadcast_to(pre_gain[None, :], (16, pre_gain.shape[0]))
    half_width = HD // 2
    lane = np.arange(HD)
    inverse_freq = np.exp(-math.log(10000.0) * 2.0 * (lane % half_width) / HD)
    signs = np.where(lane < half_width, -1.0, 1.0)
    freq = jnp.asarray(np.stack([inverse_freq] + [signs] * 7).astype(np.float32))
    ids = jnp.broadcast_to(segment_ids[:, None], (tok_w, 128))
    attn_out, flat, w_all, meta_all = front(
        tokens, w_query, w_key, w_value, jnp.transpose(w_out), meta, gain_in, ids, freq
    )
    table_all = meta_all[:, 8, :block_count].reshape(-1)

    owners = page_table // block_count
    shard_ids = jnp.arange(shard_count, dtype=jnp.int32)
    send_pick = (owners[None, :] == shard_ids[:, None]).astype(jnp.bfloat16)
    outgoing = jnp.einsum(
        "sj,jgpc->sgpc", send_pick, flat, preferred_element_type=jnp.float32
    ).astype(jnp.bfloat16)
    mixed, incoming = tail(
        attn_out, w_all, tokens, post_gain[None, :], outgoing
    )
    my_pages = shard_index * block_count + jnp.arange(block_count, dtype=jnp.int32)
    found_page = table_all[None, :] == my_pages[:, None]
    anchor = jnp.sum(
        jnp.where(
            found_page, jnp.arange(table_all.shape[0], dtype=jnp.int32)[None, :] // block_count, 0
        ),
        axis=1,
    )
    take_pick = (anchor[:, None] == shard_ids[None, :]).astype(jnp.bfloat16)
    kv_pages = jnp.einsum(
        "qs,sgpc->qgpc", take_pick, incoming, preferred_element_type=jnp.float32
    ).astype(jnp.bfloat16)
    return (mixed, kv_pages)


def solution(mesh):
    return jax.shard_map(
        local,
        mesh=mesh,
        in_specs=(
            P("wide", "narrow"),
            P("wide"),
            P("wide"),
            P("narrow"),
            P("narrow"),
            P("wide", "narrow"),
            P("wide", "narrow"),
            P("wide", "narrow"),
            P("narrow", "wide"),
        ),
        out_specs=(P("wide", "narrow"), P("wide", "narrow", None, None)),
        check_vma=False,
    )
```
